32 devices in a mesh: dp: 4 (over z), seq: 8 (over y, x, core).
Axes of the slice: x: 2, y: 2, z: 4, core: 2. Of those that a mesh axis runs over, the one named last changes fastest.
Arguments:
- layer_input: bfloat16 [4, 2048, 1152], P('dp', 'seq'), may hold values from -6 to 6
- segment_ids: int32 [4, 2048], P('dp'), may hold values from 0 to 3, as said below
- position_ids: int32 [4, 2048], P('dp', 'seq'), may hold values from 0 to 1023, as said below
- w_query: bfloat16 [1152, 1024], P('seq'), may hold values from -0.1875 to 0.1875
- w_keyval: bfloat16 [1152, 512], P('seq'), may hold values from -0.1875 to 0.1875
- w_out: bfloat16 [1024, 1152], P('seq'), may hold values from -0.1875 to 0.1875
- w_gate: bfloat16 [1152, 6912], P(None, 'seq'), may hold values from -0.1875 to 0.1875
- w_up: bfloat16 [1152, 6912], P(None, 'seq'), may hold values from -0.1875 to 0.1875
- w_down: bfloat16 [6912, 1152], P('seq'), may hold values from -0.078125 to 0.078125
- g_input: float32 [1152], replicated, may hold values from 0.25 to 1.75
- g_post_attn: float32 [1152], replicated, may hold values from 0.25 to 1.75
- g_pre_ffn: float32 [1152], replicated, may hold values from 0.25 to 1.75
- g_post_ffn: float32 [1152], replicated, may hold values from 0.25 to 1.75
- g_query: float32 [256], replicated, may hold values from 0.25 to 1.75
- g_key: float32 [256], replicated, may hold values from 0.25 to 1.75
- out_grad: float32 [4, 2048, 1152], P('dp', 'seq'), may hold values from -6 to 6
Outputs:
- layer_output: bfloat16 [4, 2048, 1152], P('dp', 'seq')
- input_grad: float32 [4, 2048, 1152], P('dp', 'seq')
- grad_w_query: float32 [1152, 1024], P('seq')
- grad_w_keyval: float32 [1152, 512], P('seq')
- grad_w_out: float32 [1024, 1152], P('seq')
- grad_w_gate: float32 [1152, 6912], P(None, 'seq')
- grad_w_up: float32 [1152, 6912], P(None, 'seq')
- grad_w_down: float32 [6912, 1152], P('seq')
- grad_g_input: float32 [1152], P('seq')
- grad_g_post_attn: float32 [1152], P('seq')
- grad_g_pre_ffn: float32 [1152], P('seq')
- grad_g_post_ffn: float32 [1152], P('seq')
- grad_g_query: float32 [256], P('seq')
- grad_g_key: float32 [256], P('seq')
The draws below stay inside these ranges and needn't reach their ends.
Inputs may be any that keep to these rules, and one draw needn't show every extreme that they name: `segment_ids`: in each row the ids never fall, start at 0 and rise by one at each document's first token; every row holds 4 documents, none longer than 1024 tokens, and in every row one of them is exactly that long. `position_ids`: A token's place within its document: 0 at the document's first token, rising by one along it; the documents are those of segment_ids.
All inputs are finite; a program needn't handle non-finite values.
Results may differ from the reference program's by a relative error of at most 0.023.
Values may be sent and summed in bfloat16 or wider, within the bound.
No kernel may reach another device: no remote copies, remote signals or barrier semaphores. Data moves between devices by JAX's collectives and lax.ppermute only.
A program may use at most 256 MiB of HBM per device.

```python
import jax
import jax.numpy as jnp
from jax import lax

D = 1152
HEADS = 4
HEAD = 256
FF = 6912
DOCS = 4
ROW_LEN = 2048
ROWS = 4


def document_cuts(key):
    row_keys = jax.random.split(jax.random.fold_in(key, 11), ROWS)
    long_len = ROW_LEN // 2
    rest_len = ROW_LEN - long_len

    def one_row(row_key):
        perm_key, slot_key = jax.random.split(row_key)
        picked = jnp.sort(jax.random.permutation(perm_key, rest_len - 1)[:DOCS - 2] + 1).astype(jnp.int32)
        bounds = jnp.concatenate([jnp.zeros((1,), jnp.int32), picked, jnp.full((1,), rest_len, jnp.int32)])
        short_lens = (bounds[1:] - bounds[:-1]).astype(jnp.int32)
        slot = jax.random.randint(slot_key, (), 0, DOCS).astype(jnp.int32)
        index = jnp.arange(DOCS, dtype=jnp.int32)
        before = short_lens[jnp.clip(index, 0, DOCS - 2)]
        after = short_lens[jnp.clip(index - 1, 0, DOCS - 2)]
        lens = jnp.where(index < slot, before, jnp.where(index == slot, jnp.int32(long_len), after)).astype(jnp.int32)
        starts = (jnp.cumsum(lens) - lens).astype(jnp.int32)
        return starts[1:]
    return jax.vmap(one_row)(row_keys)


def draw_segment_ids(key, part):
    cuts = document_cuts(key)
    index = jnp.arange(ROW_LEN, dtype=jnp.int32)
    return jnp.sum((index[None, :, None] >= cuts[:, None, :]).astype(jnp.int32), axis=2)


def draw_position_ids(key, part):
    cuts = document_cuts(key)
    index = jnp.arange(ROW_LEN, dtype=jnp.int32)
    starts = jnp.max(jnp.where(index[None, :, None] >= cuts[:, None, :], cuts[:, None, :], 0), axis=2)
    return (index[None, :] - starts).astype(jnp.int32)


def block_levels(own_key, dims, shards, least, high):
    gain, own = 1.0, jax.random.fold_in(own_key, 6)
    for axis_at, parts in shards:
        heights = jnp.exp(jax.random.uniform(jax.random.fold_in(own, axis_at), (parts,), jnp.float32, least / len(shards), high / len(shards)))
        gain = gain * jnp.repeat(heights, dims[axis_at] // parts).reshape([-1 if axis == axis_at else 1 for axis in range(len(dims))])
    return gain


def scatter_about(key, extent, spread, bound, shards=(), kind=jnp.bfloat16):
    result = jax.random.normal(key, extent, jnp.float32) * spread
    if len(shards) > 0:
        result = block_levels(key, extent, shards, -0.22, 0.18) * result
    return jnp.clip(result, min=-bound, max=bound).astype(kind)


def setup_inputs(seed: int = 0) -> dict:
    key_list = jax.random.split(jax.random.key(seed), 17)
    return {
        "layer_input": scatter_about(key_list[0], (ROWS, ROW_LEN, D), 1.0, 6.0, ((0, 4), (1, 8))),
        "segment_ids": draw_segment_ids(jax.random.fold_in(key_list[16], 71), 0),
        "position_ids": draw_position_ids(jax.random.fold_in(key_list[16], 71), 0),
        "w_query": scatter_about(key_list[3], (D, HEADS * HEAD), D ** -0.5, 0.1875, ((0, 8),)),
        "w_keyval": scatter_about(key_list[4], (D, 2 * HEAD), D ** -0.5, 0.1875, ((0, 8),)),
        "w_out": scatter_about(key_list[5], (HEADS * HEAD, D), (HEADS * HEAD) ** -0.5, 0.1875, ((0, 8),)),
        "w_gate": scatter_about(key_list[6], (D, FF), D ** -0.5, 0.1875, ((1, 8),)),
        "w_up": scatter_about(key_list[7], (D, FF), D ** -0.5, 0.1875, ((1, 8),)),
        "w_down": scatter_about(key_list[8], (FF, D), FF ** -0.5, 0.078125, ((0, 8),)),
        "g_input": jnp.clip(1.0 + 0.15 * jax.random.normal(key_list[9], (D,), jnp.float32), 0.25, 1.75),
        "g_post_attn": jnp.clip(1.0 + 0.15 * jax.random.normal(key_list[10], (D,), jnp.float32), 0.25, 1.75),
        "g_pre_ffn": jnp.clip(1.0 + 0.15 * jax.random.normal(key_list[11], (D,), jnp.float32), 0.25, 1.75),
        "g_post_ffn": jnp.clip(1.0 + 0.15 * jax.random.normal(key_list[12], (D,), jnp.float32), 0.25, 1.75),
        "g_query": jnp.clip(1.0 + 0.15 * jax.random.normal(key_list[13], (HEAD,), jnp.float32), 0.25, 1.75),
        "g_key": jnp.clip(1.0 + 0.15 * jax.random.normal(key_list[14], (HEAD,), jnp.float32), 0.25, 1.75),
        "out_grad": scatter_about(key_list[15], (ROWS, ROW_LEN, D), 1.0, 6.0, ((0, 4), (1, 8)), jnp.float32),
    }


@jax.custom_vjp
def low(v):
    return lax.optimization_barrier(v.astype(jnp.bfloat16)).astype(jnp.float32)

@jax.custom_vjp
def low_back(v):
    return v

def low_keep(v):
    return (low(v), None)

def low_pass(kept, grad):
    return (grad,)

def back_keep(v):
    return (v, None)

def back_low(kept, grad):
    return (low(grad),)
low.defvjp(low_keep, low_pass)
low_back.defvjp(back_keep, back_low)
norm_eps = 1e-06
rope_base = 1000000.0

def normalize(values):
    return values * lax.rsqrt(lax.optimization_barrier(jnp.mean(values * values, axis=-1, keepdims=True)) + norm_eps)

def rope_angles(positions, width):
    half_width = width // 2
    inverse_freq = rope_base ** (-(jnp.arange(half_width).astype(jnp.float32) * 2.0 / width))
    return positions.astype(jnp.float32)[:, None] * inverse_freq[None, :]

def rotate(values, angles):
    half_width = values.shape[-1] // 2
    first_half = values[..., :half_width]
    second_half = values[..., half_width:]
    cosine = jnp.cos(angles)
    sine_part = jnp.sin(angles)
    return jnp.concatenate([first_half * cosine - second_half * sine_part, second_half * cosine + first_half * sine_part], axis=-1)

def matmul_high(left, right):
    return jnp.dot(left, right, precision=lax.Precision.HIGHEST)

def layer_row(params, row_input, seg_row, pos_row):
    w_query, w_keyval, w_out, w_gate, w_up, w_down, g_input, g_post_attn, g_pre_ffn, g_post_ffn, g_query, g_key = params
    length = row_input.shape[0]
    angles = rope_angles(pos_row, HEAD)
    a_low = low(normalize(row_input) * g_input)
    q_pre = low_back(matmul_high(a_low, w_query)).reshape(length, HEADS, HEAD)
    kv_pre = low_back(matmul_high(a_low, w_keyval))
    queries = low(rotate(normalize(q_pre) * g_query, angles[:, None, :]))
    key_rows = low(rotate(normalize(kv_pre[:, :HEAD]) * g_key, angles))
    value_rows = low(kv_pre[:, HEAD:])
    scores = low_back(jnp.einsum('thd,sd->hts', queries, key_rows, precision=lax.Precision.HIGHEST) * HEAD ** (-0.5))
    index = jnp.arange(length)
    visible = (seg_row[None, :] == seg_row[:, None]) & (index[None, :] <= index[:, None])
    probs = low(jax.nn.softmax(jnp.where(visible[None], scores, -1e+30), axis=-1))
    attended = jnp.einsum('hts,sd->thd', probs, value_rows, precision=lax.Precision.HIGHEST).reshape(length, HEADS * HEAD)
    attended = low(low_back(attended))
    attn = low_back(matmul_high(attended, w_out))
    middle = row_input + normalize(attn) * g_post_attn
    b_low = low(normalize(middle) * g_pre_ffn)
    gate_proj = low_back(matmul_high(b_low, w_gate))
    up_proj = low_back(matmul_high(b_low, w_up))
    hidden = low(jax.nn.gelu(gate_proj, approximate=True) * up_proj)
    ffn_out = low_back(matmul_high(hidden, w_down))
    return middle + normalize(ffn_out) * g_post_ffn

def reference(layer_input, segment_ids, position_ids, w_query, w_keyval, w_out, w_gate, w_up, w_down, g_input, g_post_attn, g_pre_ffn, g_post_ffn, g_query, g_key, out_grad):
    params = (w_query.astype(jnp.float32), w_keyval.astype(jnp.float32), w_out.astype(jnp.float32), w_gate.astype(jnp.float32), w_up.astype(jnp.float32), w_down.astype(jnp.float32), g_input.astype(jnp.float32), g_post_attn.astype(jnp.float32), g_pre_ffn.astype(jnp.float32), g_post_ffn.astype(jnp.float32), g_query.astype(jnp.float32), g_key.astype(jnp.float32))
    inputs = layer_input.astype(jnp.float32)
    row_step = jax.checkpoint(layer_row)

    def forward(weights, rows_in):

        def one_row(packed):
            return row_step(weights, packed[0], packed[1], packed[2])
        return lax.map(one_row, (rows_in, segment_ids, position_ids))
    outputs, backward = jax.vjp(forward, params, inputs)
    grad_params, grad_input = backward(out_grad.astype(jnp.float32))
    return (outputs.astype(jnp.bfloat16), grad_input, grad_params[0], grad_params[1], grad_params[2], grad_params[3], grad_params[4], grad_params[5], grad_params[6], grad_params[7], grad_params[8], grad_params[9], grad_params[10], grad_params[11])
```

```python
import functools

import jax
import jax.numpy as jnp
from jax import lax
from jax.experimental import pallas as pl
from jax.experimental.pallas import tpu as pltpu
from jax.sharding import PartitionSpec as P

HEADS = 4
HEAD = 256
BLOCK = 256
LANES = 128
FEED_VMEM = 16 << 20

norm_eps = 1e-06
rope_base = 1000000.0
score_scale = HEAD**-0.5
bf16 = jnp.bfloat16
f32 = jnp.float32
BRIEF = pl.CostEstimate(flops=1, bytes_accessed=1, transcendentals=0)


def rms_forward(values):
    factor = lax.rsqrt(jnp.mean(values * values, axis=-1, keepdims=True) + norm_eps)
    return (values * factor, factor)


def rms_backward(upstream, normed, factor):
    return factor * (upstream - normed * jnp.mean(upstream * normed, axis=-1, keepdims=True))


def rope_angles(positions, width):
    half_width = width // 2
    inverse_freq = rope_base ** (-(jnp.arange(half_width).astype(f32) * 2.0 / width))
    return positions.astype(f32)[:, None] * inverse_freq[None, :]


def rotate(values, cosine, sine):
    half_width = values.shape[-1] // 2
    first = values[..., :half_width]
    second = values[..., half_width:]
    return jnp.concatenate(
        [first * cosine - second * sine, second * cosine + first * sine], axis=-1
    )


def dot(left, right):
    return jnp.dot(left, right, preferred_element_type=f32)


def dot_rows(left, right):
    return lax.dot_general(left, right, (((1,), (1,)), ((), ())), preferred_element_type=f32)


def dot_cols(left, right):
    return lax.dot_general(left, right, (((0,), (0,)), ((), ())), preferred_element_type=f32)


def visible_mask(block_id, first_row, pos_ref):
    shape = (BLOCK, BLOCK)
    query = first_row + lax.broadcasted_iota(jnp.int32, shape, 0)
    key = block_id * BLOCK + lax.broadcasted_iota(jnp.int32, shape, 1)
    return (key <= query) & (key >= query - pos_ref[...])


def attend_kernel(
    n_blocks,
    columns,
    order_ref,
    q_pre_ref,
    cos_ref,
    sin_ref,
    gain_ref,
    pos_ref,
    *refs,
):
    kv_refs, (att_ref, att_low_ref, inv_ref, q_ref, total_ref) = refs[:-5], refs[-5:]
    slot = order_ref.shape[0] - columns
    first_row = order_ref[n_blocks]
    first_key = order_ref[n_blocks + 1]
    cosine, sine = cos_ref[...], sin_ref[...]
    for h in range(HEADS):
        cols = pl.ds(h * HEAD, HEAD)
        normed, _ = rms_forward(q_pre_ref[:, cols])
        q_ref[:, cols] = rotate(normed * gain_ref[...], cosine, sine).astype(bf16)
    att_ref[...] = jnp.zeros_like(att_ref)
    total_ref[...] = jnp.zeros_like(total_ref)

    def step(kv_ref, base, k, _):
        block_id = order_ref[base + k]
        live = (block_id * BLOCK <= first_row) & ((block_id + 1) * BLOCK > first_key)

        @pl.when(live)
        def _():
            rows = pl.ds(pl.multiple_of(k * BLOCK, BLOCK), BLOCK)
            keys = kv_ref[rows, :HEAD]
            vals = kv_ref[rows, HEAD:]
            visible = visible_mask(block_id, first_row, pos_ref)
            for h in range(HEADS):
                cols = pl.ds(h * HEAD, HEAD)
                scores = dot_rows(q_ref[:, cols], keys) * score_scale
                weight = jnp.where(visible, jnp.exp(scores), 0.0)
                total_ref[:, pl.ds(h * LANES, LANES)] += weight[:, :LANES] + weight[:, LANES:]
                att_ref[:, cols] += dot(weight.astype(bf16), vals)

        return 0

    each = n_blocks // len(kv_refs)
    for i, kv_ref in enumerate(kv_refs):
        lax.fori_loop(0, each, functools.partial(step, kv_ref, i * each), 0)
    for h in range(HEADS):
        cols = pl.ds(h * HEAD, HEAD)
        lanes = pl.ds(h * LANES, LANES)
        inverse = 1.0 / jnp.sum(total_ref[:, lanes], axis=-1, keepdims=True)
        inv_ref[:, lanes] = jnp.broadcast_to(inverse, (BLOCK, LANES))
        att_ref[:, cols] = att_ref[:, cols] * inverse
    size = HEADS * HEAD // columns
    for k in range(columns):
        source = pl.ds(pl.multiple_of(order_ref[slot + k] * size, size), size)
        att_low_ref[:, pl.ds(k * size, size)] = att_ref[:, source].astype(bf16)


def attend(columns, order, q_pre, cosine, sine, gain, pos, *kv):
    rows = q_pre.shape[0]
    n_blocks = sum(v.shape[0] for v in kv) // BLOCK
    whole = pl.BlockSpec(memory_space=pltpu.VMEM)
    return pl.pallas_call(
        functools.partial(attend_kernel, n_blocks, columns),
        out_shape=(
            jax.ShapeDtypeStruct((rows, HEADS * HEAD), f32),
            jax.ShapeDtypeStruct((rows, HEADS * HEAD), bf16),
            jax.ShapeDtypeStruct((rows, HEADS * LANES), f32),
            jax.ShapeDtypeStruct((rows, HEADS * HEAD), bf16),
        ),
        in_specs=[pl.BlockSpec(memory_space=pltpu.SMEM)] + [whole] * (5 + len(kv)),
        out_specs=(whole,) * 4,
        scratch_shapes=[pltpu.VMEM((rows, HEADS * LANES), f32)],
        cost_estimate=BRIEF,
        compiler_params=pltpu.CompilerParams(vmem_limit_bytes=12 << 20),
        name="attend",
    )(order, q_pre, cosine, sine, gain, pos, *kv)


def attend_back_kernel(
    n_blocks,
    columns,
    order_ref,
    q_pre_ref,
    cos_ref,
    sin_ref,
    gain_ref,
    pos_ref,
    q_ref,
    att_ref,
    inv_ref,
    d_moved_ref,
    *refs,
):
    groups = (len(refs) - 5) // 2
    kv_refs, d_q_pre_ref, d_kv_refs = refs[:groups], refs[groups], refs[groups + 1 : -4]
    d_gain_ref, d_q_ref, row_dot_ref, d_att_ref = refs[-4:]
    slot = order_ref.shape[0] - columns
    size = HEADS * HEAD // columns
    for k in range(columns):
        target = pl.ds(pl.multiple_of(order_ref[slot + k] * size, size), size)
        d_att_ref[:, target] = d_moved_ref[:, pl.ds(k * size, size)]
    first_row = order_ref[n_blocks]
    first_key = order_ref[n_blocks + 1]
    for h in range(HEADS):
        cols = pl.ds(h * HEAD, HEAD)
        product = d_att_ref[:, cols].astype(f32) * att_ref[:, cols]
        row_dot_ref[:, pl.ds(h * LANES, LANES)] = jnp.broadcast_to(
            jnp.sum(product, axis=-1, keepdims=True), (BLOCK, LANES)
        )
    d_q_ref[...] = jnp.zeros_like(d_q_ref)

    def step(kv_ref, d_kv_ref, base, k, _):
        block_id = order_ref[base + k]
        live = (block_id * BLOCK <= first_row) & ((block_id + 1) * BLOCK > first_key)
        rows = pl.ds(pl.multiple_of(k * BLOCK, BLOCK), BLOCK)

        @pl.when(live)
        def _():
            keys = kv_ref[rows, :HEAD]
            vals = kv_ref[rows, HEAD:]
            visible = visible_mask(block_id, first_row, pos_ref)
            d_keys = jnp.zeros((BLOCK, HEAD), f32)
            d_vals = jnp.zeros((BLOCK, HEAD), f32)
            for h in range(HEADS):
                cols = pl.ds(h * HEAD, HEAD)
                query = q_ref[:, cols]
                d_att = d_att_ref[:, cols]
                inverse = inv_ref[:, pl.ds(h * LANES, 1)]
                row_dot = row_dot_ref[:, pl.ds(h * LANES, 1)]
                scores = dot_rows(query, keys) * score_scale
                prob = jnp.where(visible, jnp.exp(scores), 0.0) * inverse
                d_prob = dot_rows(d_att, vals)
                d_scores = (prob * (d_prob - row_dot)).astype(bf16)
                d_q_ref[:, cols] += dot(d_scores, keys)
                d_keys += dot_cols(d_scores, query)
                d_vals += dot_cols(prob.astype(bf16), d_att)
            d_kv_ref[rows, :HEAD] = (d_keys * score_scale).astype(bf16)
            d_kv_ref[rows, HEAD:] = d_vals.astype(bf16)

        @pl.when(jnp.logical_not(live))
        def _():
            d_kv_ref[rows, :] = jnp.zeros((BLOCK, 2 * HEAD), bf16)

        return 0

    each = n_blocks // groups
    for i in range(groups):
        walk = functools.partial(step, kv_refs[i], d_kv_refs[i], i * each)
        lax.fori_loop(0, each, walk, 0)
    cosine, sine = cos_ref[...], sin_ref[...]
    d_gain = jnp.zeros((1, HEAD), f32)
    for h in range(HEADS):
        cols = pl.ds(h * HEAD, HEAD)
        normed, factor = rms_forward(q_pre_ref[:, cols])
        d_normed = rotate(d_q_ref[:, cols] * score_scale, cosine, -sine)
        d_gain += jnp.sum(d_normed * normed, axis=0, keepdims=True)
        d_q_pre_ref[:, cols] = rms_backward(d_normed * gain_ref[...], normed, factor).astype(bf16)
    d_gain_ref[...] = d_gain


def attend_back(columns, order, q_pre, cosine, sine, gain, pos, *kv, saved, d_att):
    rows = q_pre.shape[0]
    n_blocks = sum(v.shape[0] for v in kv) // BLOCK
    whole = pl.BlockSpec(memory_space=pltpu.VMEM)
    return pl.pallas_call(
        functools.partial(attend_back_kernel, n_blocks, columns),
        out_shape=(
            jax.ShapeDtypeStruct((rows, HEADS * HEAD), bf16),
            *[jax.ShapeDtypeStruct(v.shape, bf16) for v in kv],
            jax.ShapeDtypeStruct((1, HEAD), f32),
        ),
        in_specs=[pl.BlockSpec(memory_space=pltpu.SMEM)] + [whole] * (9 + len(kv)),
        out_specs=(whole,) * (2 + len(kv)),
        scratch_shapes=[
            pltpu.VMEM((rows, HEADS * HEAD), f32),
            pltpu.VMEM((rows, HEADS * LANES), f32),
            pltpu.VMEM((rows, HEADS * HEAD), bf16),
        ],
        cost_estimate=BRIEF,
        compiler_params=pltpu.CompilerParams(vmem_limit_bytes=16 << 20),
        name="attend_back",
    )(order, q_pre, cosine, sine, gain, pos, *saved, d_att, *kv)


def gelu_parts(gate):
    c = (2.0 / jnp.pi) ** 0.5
    square = gate * gate
    t = jnp.tanh(gate * (c + (c * 0.044715) * square))
    half = 0.5 + 0.5 * t
    act = gate * half
    slope = half + act * (1.0 - t) * (c + (3 * c * 0.044715) * square)
    return act, slope


def feed_kernel(groups, b_ref, *refs):
    weights, (part_ref, hidden_ref, act_ref, slope_ref) = refs[:-4], refs[-4:]
    part = 0.0
    for i in range(groups):
        gate_ref, up_ref, down_ref = weights[3 * i : 3 * i + 3]
        gate = dot_rows(b_ref[...], gate_ref[...])
        up = dot_rows(b_ref[...], up_ref[...])
        act, slope = gelu_parts(gate)
        hidden_ref[i] = (act * up).astype(bf16)
        act_ref[i] = act.astype(bf16)
        slope_ref[i] = (up * slope).astype(bf16)
        part = part + dot(hidden_ref[i], down_ref[...])
    part_ref[...] = part.astype(part_ref.dtype)


def feed(b, weights, dtype):
    rows, width = b.shape
    groups, ff = len(weights) // 3, weights[0].shape[0]
    whole = pl.BlockSpec(memory_space=pltpu.VMEM)
    return pl.pallas_call(
        functools.partial(feed_kernel, groups),
        out_shape=(
            jax.ShapeDtypeStruct((rows, width), dtype),
            *[jax.ShapeDtypeStruct((groups, rows, ff), bf16)] * 3,
        ),
        in_specs=[whole] * (1 + len(weights)),
        out_specs=(whole,) * 4,
        cost_estimate=BRIEF,
        compiler_params=pltpu.CompilerParams(vmem_limit_bytes=FEED_VMEM),
        name="feed",
    )(b, *weights)


def feed_back_kernel(groups, d_ref, act_ref, slope_ref, *refs):
    weights, (part_ref, d_gate_ref, d_up_ref) = refs[:-3], refs[-3:]
    part = 0.0
    for i in range(groups):
        gate_ref, up_ref, down_ref = weights[3 * i : 3 * i + 3]
        d_hidden = dot_rows(d_ref[...], down_ref[...])
        d_gate_ref[i] = (d_hidden * slope_ref[i].astype(f32)).astype(bf16)
        d_up_ref[i] = (d_hidden * act_ref[i].astype(f32)).astype(bf16)
        part = part + dot(d_gate_ref[i], gate_ref[...]) + dot(d_up_ref[i], up_ref[...])
    part_ref[...] = part.astype(part_ref.dtype)


def feed_back(d, act, slope, weights, dtype):
    rows, width = d.shape
    groups, ff = len(weights) // 3, weights[0].shape[0]
    whole = pl.BlockSpec(memory_space=pltpu.VMEM)
    return pl.pallas_call(
        functools.partial(feed_back_kernel, groups),
        out_shape=(
            jax.ShapeDtypeStruct((rows, width), dtype),
            *[jax.ShapeDtypeStruct((groups, rows, ff), bf16)] * 2,
        ),
        in_specs=[whole] * (3 + len(weights)),
        out_specs=(whole,) * 3,
        cost_estimate=BRIEF,
        compiler_params=pltpu.CompilerParams(vmem_limit_bytes=FEED_VMEM),
        name="feed_back",
    )(d, act, slope, *weights)


def weight_grad_kernel(index, sizes, count, *refs):
    lefts, rights, rest = refs[:count], refs[count : 2 * count], refs[2 * count :]
    extra, outs = rest[: -len(sizes)], rest[-len(sizes) :]
    left = jnp.concatenate([v[index] for v in lefts], axis=0)
    right = jnp.concatenate([v[...] for v in rights], axis=0)
    total = dot_cols(left, right)
    if extra:
        total = total + extra[0][...].astype(f32)
    begin = 0
    for size, out in zip(sizes, outs):
        out[...] = total[begin : begin + size].astype(bf16)
        begin += size


def weight_grad(index, sizes, lefts, rights, *extra):
    rows, width = rights[0].shape
    whole = pl.BlockSpec(memory_space=pltpu.VMEM)
    return pl.pallas_call(
        functools.partial(weight_grad_kernel, index, sizes, len(lefts)),
        out_shape=tuple(jax.ShapeDtypeStruct((size, width), bf16) for size in sizes),
        in_specs=[whole] * (2 * len(lefts) + len(extra)),
        out_specs=(whole,) * len(sizes),
        cost_estimate=BRIEF,
        compiler_params=pltpu.CompilerParams(vmem_limit_bytes=FEED_VMEM),
        name="weight_grad",
    )(*lefts, *rights, *extra)


def add(*terms):
    return functools.reduce(jnp.add, [t.astype(f32) for t in terms])


fence = lax.optimization_barrier


class Plain:
    def __init__(self, n):
        self.n = n
        self.rank = lax.axis_index("seq")

    def order(self):
        return jnp.arange(self.n, dtype=jnp.int32)

    def slots(self):
        return jnp.zeros(1, jnp.int32)

    def send(self, shard):
        return [shard]

    def paired(self, shards):
        return [lax.all_gather(shards[0], "seq", axis=0, tiled=True)]

    def columns(self, value):
        return [value]

    def restored(self, parts):
        return parts[0]

    def pair(self, shard):
        return [shard]

    def tokens(self, shard):
        whole = lax.all_gather(shard, "seq", axis=0, tiled=True)
        return jnp.split(whole, self.n, axis=0)

    def part_send(self, parts, at):
        return ()

    def parts_sum(self, parts, moved):
        return self.scatter(all_of([p.astype(bf16) for p in parts]))

    def across(self, value):
        return ()

    def group_send(self, partial, moved):
        return (partial[0],)

    def group_sum(self, sent):
        return self.scatter(sent[0])

    def scatter(self, partial):
        return lax.psum_scatter(
            partial.astype(bf16), "seq", scatter_dimension=0, tiled=True
        ).astype(f32)

    def projection(self, left, right, gains):
        grad = dot_cols(left, right).reshape(self.n, -1, right.shape[1])
        gains = jnp.pad(gains, ((0, 0), (0, right.shape[1] - gains.shape[1])))
        packed = [grad, jnp.pad(gains[:, None], ((0, 0), (0, 15), (0, 0)))]
        return [jnp.concatenate(packed, axis=1).reshape(-1, right.shape[1])]

    def line(self):
        return PlainLine()


class Cube(Plain):
    chips = (0, 2, 4, 6)
    ranks = (0, 2, 4, 6, 1, 3, 5, 7)

    def hop(self, value, bit):
        return lax.ppermute(value, "seq", [(i, i ^ bit) for i in range(8)])

    def order(self):
        return self.rank ^ jnp.array(self.ranks, dtype=jnp.int32)

    def slots(self):
        return self.order()

    def send(self, shard):
        return [shard] + [self.hop(shard, bit) for bit in self.chips[1:]]

    def paired(self, shards):
        group = all_of(shards)
        return [group, self.hop(group, 1)]

    def tokens(self, shard):
        return self.send(shard)

    def part_send(self, parts, at):
        return (self.hop(parts[at].astype(bf16), self.chips[at]),)

    def parts_sum(self, parts, moved):
        return add(parts[0], *moved)

    def across(self, value):
        return (self.hop(value, 1),)

    def group_send(self, partial, moved):
        mine = add(partial[0], *moved)
        parts = jnp.split(mine, 4, axis=0)
        return (parts[0], *[self.part_send(parts, at)[0] for at in (1, 2, 3)])

    def group_sum(self, sent):
        return add(*sent)

    def select(self, size, stride):
        shape = (self.n * size, self.n * stride)
        col = lax.broadcasted_iota(jnp.int32, shape, 1)
        block, at = col // stride, col % stride
        source = self.rank ^ ((2 * block) % 8 + block // 4)
        row = lax.broadcasted_iota(jnp.int32, shape, 0)
        return ((row == source * size + at) & (at < size)).astype(bf16)

    def columns(self, value):
        moved = dot(value, self.select(value.shape[1] // self.n, value.shape[1] // self.n))
        return jnp.split(moved.astype(value.dtype), 2, axis=1)

    def restored(self, parts):
        value = jnp.concatenate(parts, axis=1)
        pick = self.select(value.shape[1] // self.n, value.shape[1] // self.n).astype(f32)
        return lax.dot_general(
            value, pick, (((1,), (1,)), ((), ())), precision=lax.Precision.HIGHEST
        )

    def pair(self, shard):
        return [shard, self.hop(shard, 1)]

    def projection(self, left, right, gains):
        size = left.shape[1] // self.n
        stride = size + 16
        moved = dot(left, self.select(size, stride)).astype(bf16)
        shape = (16, self.n * stride)
        col = lax.broadcasted_iota(jnp.int32, shape, 1)
        block, at = col // stride, col % stride
        target = self.rank ^ ((2 * block) % 8 + block // 4)
        row = lax.broadcasted_iota(jnp.int32, shape, 0)
        pick = ((row == target) & (at == size)).astype(bf16)
        left = jnp.concatenate([moved, pick], axis=0)
        gains = jnp.pad(gains, ((0, 8), (0, right.shape[1] - gains.shape[1]))).astype(bf16)
        right = jnp.concatenate([right, gains], axis=0)
        half = self.n * stride // 2
        return [dot_cols(left[:, :half], right), dot_cols(left[:, half:], right)]

    def line(self):
        return CubeLine()


class PlainLine:
    def __init__(self):
        self.chunks = []

    def send(self):
        return ()

    def settle(self, got):
        pass

    def finish(self):
        return [lax.psum(c, "dp").astype(f32) for c in self.chunks]


class CubeLine(PlainLine):
    def __init__(self):
        super().__init__()
        place = lax.axis_index("dp")
        self.inner = (place == 1) | (place == 2)
        self.halves, self.totals, self.out = {}, {}, {}
        self.at = 0

    def send(self):
        tick = self.at
        mine = self.chunks[tick] if tick < len(self.chunks) else None
        back, half = self.totals.get(tick - 2), self.halves.get(tick - 1)
        got = {}
        if mine is not None and back is not None and mine.shape == back.shape:
            both = jnp.where(self.inner, back, mine)
            got["in"] = lax.ppermute(both, "dp", [(0, 1), (1, 0), (2, 3), (3, 2)])
        else:
            if back is not None:
                got["out"] = lax.ppermute(back, "dp", [(1, 0), (2, 3)])
            if mine is not None:
                got["in"] = lax.ppermute(mine, "dp", [(0, 1), (3, 2)])
        if half is not None:
            got["middle"] = lax.ppermute(half, "dp", [(1, 2), (2, 1)])
        return got

    def settle(self, got):
        tick = self.at
        self.at += 1
        if tick < len(self.chunks):
            self.halves[tick] = add(self.chunks[tick], got["in"]).astype(bf16)
        if "middle" in got:
            self.totals[tick - 1] = add(self.halves[tick - 1], got["middle"]).astype(bf16)
        if tick >= 2:
            back = got["out"] if "out" in got else got["in"]
            self.out[tick - 2] = jnp.where(self.inner, self.totals[tick - 2], back)

    def finish(self):
        while self.at < len(self.chunks) + 2:
            self.settle(fence(self.send()))
        return [self.out[i].astype(f32) for i in range(len(self.chunks))]


def all_of(values):
    return jnp.concatenate(values, axis=0)


def on_device(
    kind,
    layer_input,
    segment_ids,
    position_ids,
    w_query,
    w_keyval,
    w_out,
    w_gate,
    w_up,
    w_down,
    g_input,
    g_post_attn,
    g_pre_ffn,
    g_post_ffn,
    g_query,
    g_key,
    out_grad,
):
    n = lax.axis_size("seq")
    comm = kind(n)
    rows = layer_input.shape[1]
    width = layer_input.shape[2]
    ff = w_gate.shape[1]
    row_offset = comm.rank * rows

    x = layer_input[0].astype(f32)
    positions = position_ids[0]
    keyval_sent = comm.send(w_keyval)
    a_normed, a_factor = rms_forward(x)
    a_low = (a_normed * g_input).astype(bf16)
    a_columns = comm.columns(a_low)
    angles = rope_angles(positions, HEAD)
    cosine, sine = jnp.cos(angles), jnp.sin(angles)
    keyval_sent, a_columns, w_query = fence((keyval_sent, a_columns, w_query))
    query_sent = comm.send(w_query)
    keyval_blocks = comm.paired(keyval_sent)
    kv_pre = add(*[dot(a, w) for a, w in zip(a_columns, keyval_blocks)])
    k_hat, k_factor = rms_forward(kv_pre[:, :HEAD])
    k_low = rotate(k_hat * g_key, cosine, sine).astype(bf16)
    kv_low = jnp.concatenate([k_low, kv_pre[:, HEAD:].astype(bf16)], axis=1)
    kv_low, query_sent, w_gate, w_up, w_down = fence((kv_low, query_sent, w_gate, w_up, w_down))
    kv_sent = comm.send(kv_low)
    query_blocks = comm.paired(query_sent)
    q_pre = add(*[dot(a, w) for a, w in zip(a_columns, query_blocks)])
    kv_sent, q_pre, w_out = fence((kv_sent, q_pre, w_out))
    out_sent = comm.send(w_out)
    kv_blocks = comm.paired(kv_sent)
    weights = [comm.pair(w) for w in (w_gate.T, w_up.T, w_down)]
    weights = [w[i] for i in range(len(weights[0])) for w in weights]
    groups = len(weights) // 3
    order = jnp.concatenate(
        [comm.order(), row_offset[None], (row_offset - positions[0])[None], comm.slots()]
    ).astype(jnp.int32)
    head_args = (
        comm.slots().shape[0],
        order,
        q_pre,
        cosine,
        sine,
        g_query[None],
        positions[:, None],
        *kv_blocks,
    )
    att, att_low, inverse, q_low = attend(*head_args)
    out_sent, att_low = fence((out_sent, att_low))
    out_blocks = comm.paired(out_sent)
    att_columns = jnp.split(att_low, len(out_blocks), axis=1)
    attn = add(*[dot(v, w) for v, w in zip(att_columns, out_blocks)])
    attn_normed, attn_factor = rms_forward(attn)
    middle = x + attn_normed * g_post_attn
    b_normed, b_factor = rms_forward(middle)
    b_low = (b_normed * g_pre_ffn).astype(bf16)
    b_low, weights = fence((b_low, weights))

    b_list = comm.tokens(b_low)
    hidden, acts, slopes, parts, moved = [], [], [], [], []
    for i, b_part in enumerate(b_list):
        sent = comm.part_send(parts, i - 1) if i > 1 else ()
        kept = feed(b_part, weights, bf16 if i else f32)
        ahead = b_list[i + 1 : i + 2]
        kept, sent, ahead = fence((kept, sent, ahead))
        b_list[i + 1 : i + 2] = ahead
        moved += sent
        for values, value in zip((parts, hidden, acts, slopes), kept):
            values.append(value)
    moved += comm.part_send(parts, len(parts) - 1)
    ffn = comm.parts_sum(parts, moved)
    ffn_normed, ffn_factor = rms_forward(ffn)
    layer_out = (middle + ffn_normed * g_post_ffn).astype(bf16)

    g = out_grad[0]
    d_ffn = rms_backward(g * g_post_ffn, ffn_normed, ffn_factor).astype(bf16)
    d_ffn, ffn_normed = fence((d_ffn, ffn_normed))
    d_list = comm.tokens(d_ffn)
    gain_post_ffn = jnp.sum(g * ffn_normed, axis=0)
    d_gate, d_up, parts, moved = [], [], [], []
    line = comm.line()
    thirds = [ff // 3] * 3

    def keep(kept):
        for values, value in zip((parts, d_gate, d_up), kept):
            values.append(value)

    for i, d_part in enumerate(d_list[:-1]):
        sent = comm.part_send(parts, i - 1) if i > 1 else ()
        kept = feed_back(d_part, acts[i], slopes[i], weights, bf16 if i else f32)
        ahead = d_list[i + 1 : i + 2]
        kept, sent, ahead = fence((kept, sent, ahead))
        d_list[i + 1 : i + 2] = ahead
        moved += sent
        keep(kept)

    def grad_pair(lefts, rights):
        if groups == 1:
            return ()
        return comm.across(weight_grad(1, [ff], lefts, rights)[0])

    sent = comm.part_send(parts, len(parts) - 1)
    other = grad_pair(hidden, d_list)
    last = len(d_list) - 1
    keep(feed_back(d_list[last], acts[last], slopes[last], weights, bf16))
    other, sent, part = fence((other, sent, parts[last]))
    parts[last] = part
    moved += sent
    line.chunks += weight_grad(0, thirds, hidden, d_list, *other)

    line.chunks, parts, d_gate, d_up = fence((line.chunks, parts, d_gate, d_up))
    got = line.send()
    sent = comm.part_send(parts, last)
    other = grad_pair(d_gate, b_list)
    other_up = grad_pair(d_up, b_list)
    grads = weight_grad(0, thirds, d_gate, b_list, *other)
    got, sent, grads, other_up, d_up = fence((got, sent, list(grads), other_up, d_up))
    line.settle(got)
    line.chunks += grads
    moved += sent

    got = line.send()
    d_b = comm.parts_sum(parts, moved)
    gain_pre_ffn = jnp.sum(d_b * b_normed, axis=0)
    d_middle = g + rms_backward(d_b * g_pre_ffn, b_normed, b_factor)
    gain_post_attn = jnp.sum(d_middle * attn_normed, axis=0)
    d_attn = rms_backward(d_middle * g_post_attn, attn_normed, attn_factor).astype(bf16)
    d_att = jnp.concatenate([dot_rows(d_attn, w).astype(bf16) for w in out_blocks], axis=1)
    d_heads = attend_back(*head_args, saved=(q_low, att, inverse), d_att=d_att)
    got, d_heads, d_attn, d_up = fence((got, d_heads, d_attn, d_up))
    d_q_pre, *d_kv_blocks, gain_query = d_heads
    line.settle(got)

    got = line.send()
    d_kv_moved = comm.across(d_kv_blocks[-1])
    grads = weight_grad(0, thirds, d_up, b_list, *other_up)
    grad_out = [dot_cols(v, d_attn) for v in att_columns]
    d_kv_sent = comm.group_send(d_kv_blocks, d_kv_moved)
    out_moved = comm.across(grad_out[-1].astype(bf16))
    got, grads, d_kv_sent, grad_out, out_moved = fence(
        (got, list(grads), d_kv_sent, grad_out, out_moved)
    )
    line.settle(got)
    line.chunks += grads

    got = line.send()
    d_kv = comm.group_sum(d_kv_sent)
    out_sent = comm.group_send(grad_out, out_moved)
    d_k_normed = rotate(d_kv[:, :HEAD], cosine, -sine)
    gain_key = jnp.sum(d_k_normed * k_hat, axis=0)
    d_k_pre = rms_backward(d_k_normed * g_key, k_hat, k_factor)
    d_kv_pre = jnp.concatenate([d_k_pre, d_kv[:, HEAD:]], axis=1).astype(bf16)
    d_a = comm.restored(
        [
            dot_rows(d_q_pre, query) + dot_rows(d_kv_pre, keyval)
            for query, keyval in zip(query_blocks, keyval_blocks)
        ]
    )
    gain_input = jnp.sum(d_a * a_normed, axis=0)
    gains = [gain_input, gain_post_attn, gain_pre_ffn, gain_post_ffn, gain_query[0], gain_key]
    got, out_sent, d_a, gains, d_kv_pre = fence((got, out_sent, d_a, gains, d_kv_pre))
    line.settle(got)

    got = line.send()
    packed = jnp.concatenate([v.reshape(n, -1) for v in gains], axis=1)
    d_qkv = jnp.concatenate([d_q_pre, d_kv_pre], axis=1)
    grad_qkv = comm.projection(a_low, d_qkv, packed)
    qkv_moved = comm.across(grad_qkv[-1].astype(bf16))
    d_input = d_middle + rms_backward(d_a * g_input, a_normed, a_factor)
    got, grad_qkv, qkv_moved, d_input = fence((got, grad_qkv, qkv_moved, d_input))
    line.settle(got)

    got = line.send()
    qkv_sent = comm.group_send(grad_qkv, qkv_moved)
    got, qkv_sent = fence((got, qkv_sent))
    line.settle(got)
    line.chunks += [comm.group_sum(out_sent).astype(bf16), comm.group_sum(qkv_sent).astype(bf16)]
    *done, total_out, tail = line.finish()
    down, gate, up = [all_of(done[i : i + 3]) for i in (0, 3, 6)]
    shard = width // n
    row = tail[shard]
    names, at = [], 0
    for v in gains:
        size = v.shape[0] // n
        names.append(row[at : at + size])
        at += size
    return (
        layer_out[None],
        d_input[None],
        tail[:shard, : HEADS * HEAD],
        tail[:shard, HEADS * HEAD :],
        total_out,
        gate.T,
        up.T,
        down,
        *names,
    )


def solution(mesh):
    cube = mesh.shape["seq"] == 8 and mesh.shape["dp"] == 4
    in_specs = (
        P("dp", "seq", None),
        P("dp", None),
        P("dp", "seq"),
        P("seq", None),
        P("seq", None),
        P("seq", None),
        P(None, "seq"),
        P(None, "seq"),
        P("seq", None),
        P(),
        P(),
        P(),
        P(),
        P(),
        P(),
        P("dp", "seq", None),
    )
    out_specs = (
        P("dp", "seq", None),
        P("dp", "seq", None),
        P("seq", None),
        P("seq", None),
        P("seq", None),
        P(None, "seq"),
        P(None, "seq"),
        P("seq", None),
        P("seq"),
        P("seq"),
        P("seq"),
        P("seq"),
        P("seq"),
        P("seq"),
    )
    return jax.shard_map(
        functools.partial(on_device, Cube if cube else Plain),
        mesh=mesh,
        in_specs=in_specs,
        out_specs=out_specs,
        check_vma=False,
    )
```

```python
import functools

import jax
import jax.numpy as jnp
from jax import lax
from jax.experimental import pallas as pl
from jax.experimental.pallas import tpu as pltpu
from jax.sharding import PartitionSpec as P

HEADS = 4
HEAD = 256
BLOCK = 256
LANES = 128
FEED_VMEM = 12 << 20

norm_eps = 1e-06
rope_base = 1000000.0
score_scale = HEAD**-0.5
bf16 = jnp.bfloat16
f32 = jnp.float32
BRIEF = pl.CostEstimate(flops=1, bytes_accessed=1, transcendentals=0)


def rms_forward(values):
    factor = lax.rsqrt(jnp.mean(values * values, axis=-1, keepdims=True) + norm_eps)
    return (values * factor, factor)


def rms_backward(upstream, normed, factor):
    return factor * (upstream - normed * jnp.mean(upstream * normed, axis=-1, keepdims=True))


def rope_angles(positions, width):
    half_width = width // 2
    inverse_freq = rope_base ** (-(jnp.arange(half_width).astype(f32) * 2.0 / width))
    return positions.astype(f32)[:, None] * inverse_freq[None, :]


def rotate(values, cosine, sine):
    half_width = values.shape[-1] // 2
    first = values[..., :half_width]
    second = values[..., half_width:]
    return jnp.concatenate(
        [first * cosine - second * sine, second * cosine + first * sine], axis=-1
    )


def dot(left, right):
    return jnp.dot(left, right, preferred_element_type=f32)


def dot_rows(left, right):
    return lax.dot_general(left, right, (((1,), (1,)), ((), ())), preferred_element_type=f32)


def dot_cols(left, right):
    return lax.dot_general(left, right, (((0,), (0,)), ((), ())), preferred_element_type=f32)


def visible_mask(block_id, first_row, pos_ref):
    shape = (BLOCK, BLOCK)
    query = first_row + lax.broadcasted_iota(jnp.int32, shape, 0)
    key = block_id * BLOCK + lax.broadcasted_iota(jnp.int32, shape, 1)
    return (key <= query) & (key >= query - pos_ref[...])


def put_queries(q_ref, q_pre_ref, gain_ref, cosine, sine):
    for h in range(HEADS):
        cols = pl.ds(h * HEAD, HEAD)
        normed, _ = rms_forward(q_pre_ref[:, cols])
        q_ref[:, cols] = rotate(normed * gain_ref[...], cosine, sine).astype(bf16)


def attend_kernel(
    n_blocks,
    columns,
    order_ref,
    q_pre_ref,
    cos_ref,
    sin_ref,
    gain_ref,
    pos_ref,
    *refs,
):
    kv_refs, (att_low_ref, inv_ref, q_ref, att_ref, total_ref) = refs[:-5], refs[-5:]
    slot = order_ref.shape[0] - columns
    first_row = order_ref[n_blocks]
    first_key = order_ref[n_blocks + 1]
    cosine, sine = cos_ref[...], sin_ref[...]
    put_queries(q_ref, q_pre_ref, gain_ref, cosine, sine)
    att_ref[...] = jnp.zeros_like(att_ref)
    total_ref[...] = jnp.zeros_like(total_ref)

    def step(kv_ref, base, k, _):
        block_id = order_ref[base + k]
        live = (block_id * BLOCK <= first_row) & ((block_id + 1) * BLOCK > first_key)

        @pl.when(live)
        def _():
            rows = pl.ds(pl.multiple_of(k * BLOCK, BLOCK), BLOCK)
            keys = kv_ref[rows, :HEAD]
            vals = kv_ref[rows, HEAD:]
            visible = visible_mask(block_id, first_row, pos_ref)
            for h in range(HEADS):
                cols = pl.ds(h * HEAD, HEAD)
                scores = dot_rows(q_ref[:, cols], keys) * score_scale
                weight = jnp.where(visible, jnp.exp(scores), 0.0)
                total_ref[:, pl.ds(h * LANES, LANES)] += weight[:, :LANES] + weight[:, LANES:]
                att_ref[:, cols] += dot(weight.astype(bf16), vals)

        return 0

    each = n_blocks // len(kv_refs)
    for i, kv_ref in enumerate(kv_refs):
        lax.fori_loop(0, each, functools.partial(step, kv_ref, i * each), 0)
    for h in range(HEADS):
        cols = pl.ds(h * HEAD, HEAD)
        lanes = pl.ds(h * LANES, LANES)
        inverse = 1.0 / jnp.sum(total_ref[:, lanes], axis=-1, keepdims=True)
        inv_ref[:, pl.ds(h, 1)] = inverse
        att_ref[:, cols] = att_ref[:, cols] * inverse
    size = HEADS * HEAD // columns
    for k in range(columns):
        source = pl.ds(pl.multiple_of(order_ref[slot + k] * size, size), size)
        att_low_ref[:, pl.ds(k * size, size)] = att_ref[:, source].astype(bf16)


def attend(columns, order, q_pre, cosine, sine, gain, pos, *kv):
    rows = q_pre.shape[0]
    n_blocks = sum(v.shape[0] for v in kv) // BLOCK
    whole = pl.BlockSpec(memory_space=pltpu.VMEM)
    return pl.pallas_call(
        functools.partial(attend_kernel, n_blocks, columns),
        out_shape=(
            jax.ShapeDtypeStruct((rows, HEADS * HEAD), bf16),
            jax.ShapeDtypeStruct((rows, LANES), f32),
        ),
        in_specs=[pl.BlockSpec(memory_space=pltpu.SMEM)] + [whole] * (5 + len(kv)),
        out_specs=(whole,) * 2,
        scratch_shapes=[
            pltpu.VMEM((rows, HEADS * HEAD), bf16),
            pltpu.VMEM((rows, HEADS * HEAD), f32),
            pltpu.VMEM((rows, HEADS * LANES), f32),
        ],
        cost_estimate=BRIEF,
        compiler_params=pltpu.CompilerParams(vmem_limit_bytes=8 << 20),
        name="attend",
    )(order, q_pre, cosine, sine, gain, pos, *kv)


def attend_back_kernel(
    n_blocks,
    columns,
    order_ref,
    q_pre_ref,
    cos_ref,
    sin_ref,
    gain_ref,
    pos_ref,
    att_ref,
    inv_ref,
    d_moved_ref,
    *refs,
):
    groups = (len(refs) - 7) // 2
    kv_refs, d_q_pre_ref, d_kv_refs = refs[:groups], refs[groups], refs[groups + 1 : -6]
    d_gain_ref, d_q_ref, row_dot_ref, d_att_ref, q_ref, dot_ref = refs[-6:]
    cosine, sine = cos_ref[...], sin_ref[...]
    put_queries(q_ref, q_pre_ref, gain_ref, cosine, sine)
    slot = order_ref.shape[0] - columns
    size = HEADS * HEAD // columns
    for k in range(columns):
        target = pl.ds(pl.multiple_of(order_ref[slot + k] * size, size), size)
        moved = d_moved_ref[:, pl.ds(k * size, size)]
        d_att_ref[:, target] = moved
        dot_ref[:, target] = moved.astype(f32) * att_ref[:, pl.ds(k * size, size)].astype(f32)
    first_row = order_ref[n_blocks]
    first_key = order_ref[n_blocks + 1]
    for h in range(HEADS):
        cols = pl.ds(h * HEAD, HEAD)
        row_dot_ref[:, pl.ds(h, 1)] = jnp.sum(dot_ref[:, cols], axis=-1, keepdims=True)
    d_q_ref[...] = jnp.zeros_like(d_q_ref)

    def step(kv_ref, d_kv_ref, base, k, _):
        block_id = order_ref[base + k]
        live = (block_id * BLOCK <= first_row) & ((block_id + 1) * BLOCK > first_key)
        rows = pl.ds(pl.multiple_of(k * BLOCK, BLOCK), BLOCK)

        @pl.when(live)
        def _():
            keys = kv_ref[rows, :HEAD]
            vals = kv_ref[rows, HEAD:]
            visible = visible_mask(block_id, first_row, pos_ref)
            d_keys = jnp.zeros((BLOCK, HEAD), f32)
            d_vals = jnp.zeros((BLOCK, HEAD), f32)
            for h in range(HEADS):
                cols = pl.ds(h * HEAD, HEAD)
                query = q_ref[:, cols]
                d_att = d_att_ref[:, cols]
                inverse = inv_ref[:, pl.ds(h, 1)]
                row_dot = row_dot_ref[:, pl.ds(h, 1)]
                scores = dot_rows(query, keys) * score_scale
                prob = jnp.where(visible, jnp.exp(scores), 0.0) * inverse
                d_prob = dot_rows(d_att, vals)
                d_scores = (prob * (d_prob - row_dot)).astype(bf16)
                d_q_ref[:, cols] += dot(d_scores, keys)
                d_keys += dot_cols(d_scores, query)
                d_vals += dot_cols(prob.astype(bf16), d_att)
            d_kv_ref[rows, :HEAD] = (d_keys * score_scale).astype(bf16)
            d_kv_ref[rows, HEAD:] = d_vals.astype(bf16)

        @pl.when(jnp.logical_not(live))
        def _():
            d_kv_ref[rows, :] = jnp.zeros((BLOCK, 2 * HEAD), bf16)

        return 0

    each = n_blocks // groups
    for i in range(groups):
        walk = functools.partial(step, kv_refs[i], d_kv_refs[i], i * each)
        lax.fori_loop(0, each, walk, 0)
    d_gain = jnp.zeros((1, HEAD), f32)
    for h in range(HEADS):
        cols = pl.ds(h * HEAD, HEAD)
        normed, factor = rms_forward(q_pre_ref[:, cols])
        d_normed = rotate(d_q_ref[:, cols] * score_scale, cosine, -sine)
        d_gain += jnp.sum(d_normed * normed, axis=0, keepdims=True)
        d_q_pre_ref[:, cols] = rms_backward(d_normed * gain_ref[...], normed, factor).astype(bf16)
    d_gain_ref[...] = d_gain


def attend_back(columns, order, q_pre, cosine, sine, gain, pos, *kv, saved, d_att):
    rows = q_pre.shape[0]
    n_blocks = sum(v.shape[0] for v in kv) // BLOCK
    whole = pl.BlockSpec(memory_space=pltpu.VMEM)
    return pl.pallas_call(
        functools.partial(attend_back_kernel, n_blocks, columns),
        out_shape=(
            jax.ShapeDtypeStruct((rows, HEADS * HEAD), bf16),
            *[jax.ShapeDtypeStruct(v.shape, bf16) for v in kv],
            jax.ShapeDtypeStruct((1, HEAD), f32),
        ),
        in_specs=[pl.BlockSpec(memory_space=pltpu.SMEM)] + [whole] * (8 + len(kv)),
        out_specs=(whole,) * (2 + len(kv)),
        scratch_shapes=[
            pltpu.VMEM((rows, HEADS * HEAD), f32),
            pltpu.VMEM((rows, LANES), f32),
            pltpu.VMEM((rows, HEADS * HEAD), bf16),
            pltpu.VMEM((rows, HEADS * HEAD), bf16),
            pltpu.VMEM((rows, HEADS * HEAD), f32),
        ],
        cost_estimate=BRIEF,
        compiler_params=pltpu.CompilerParams(vmem_limit_bytes=10 << 20),
        name="attend_back",
    )(order, q_pre, cosine, sine, gain, pos, *saved, d_att, *kv)


def gelu_parts(gate):
    c = (2.0 / jnp.pi) ** 0.5
    square = gate * gate
    t = jnp.tanh(gate * (c + (c * 0.044715) * square))
    half = 0.5 + 0.5 * t
    act = gate * half
    slope = half + act * (1.0 - t) * (c + (3 * c * 0.044715) * square)
    return act, slope


def put_halves(part, refs):
    half = part.shape[0] // 2
    refs[0][...] = part[:half].astype(refs[0].dtype)
    refs[1][...] = part[half:].astype(refs[1].dtype)


def feed_kernel(groups, pieces, *refs):
    weights, halves, (hidden_ref, act_ref, slope_ref) = refs[pieces:-5], refs[-5:-3], refs[-3:]
    b = jnp.concatenate([r[...] for r in refs[:pieces]], axis=0)
    part = 0.0
    for i in range(groups):
        gate_ref, up_ref, down_ref = weights[3 * i : 3 * i + 3]
        gate = dot_rows(b, gate_ref[...])
        up = dot_rows(b, up_ref[...])
        act, slope = gelu_parts(gate)
        hidden_ref[i] = (act * up).astype(bf16)
        act_ref[i] = act.astype(bf16)
        slope_ref[i] = (up * slope).astype(bf16)
        part = part + dot(hidden_ref[i], down_ref[...])
    put_halves(part, halves)


def feed(b, weights, dtype):
    rows, width = sum(v.shape[0] for v in b), b[0].shape[1]
    groups, ff = len(weights) // 3, weights[0].shape[0]
    whole = pl.BlockSpec(memory_space=pltpu.VMEM)
    return pl.pallas_call(
        functools.partial(feed_kernel, groups, len(b)),
        out_shape=(
            *[jax.ShapeDtypeStruct((rows // 2, width), dtype)] * 2,
            *[jax.ShapeDtypeStruct((groups, rows, ff), bf16)] * 3,
        ),
        in_specs=[whole] * (len(b) + len(weights)),
        out_specs=(whole,) * 5,
        cost_estimate=BRIEF,
        compiler_params=pltpu.CompilerParams(vmem_limit_bytes=FEED_VMEM),
        name="feed",
    )(*b, *weights)


def feed_back_kernel(groups, pieces, act_ref, slope_ref, *refs):
    weights, halves, (d_gate_ref, d_up_ref) = refs[pieces:-4], refs[-4:-2], refs[-2:]
    d = jnp.concatenate([r[...] for r in refs[:pieces]], axis=0)
    part = 0.0
    for i in range(groups):
        gate_ref, up_ref, down_ref = weights[3 * i : 3 * i + 3]
        d_hidden = dot_rows(d, down_ref[...])
        d_gate_ref[i] = (d_hidden * slope_ref[i].astype(f32)).astype(bf16)
        d_up_ref[i] = (d_hidden * act_ref[i].astype(f32)).astype(bf16)
        part = part + dot(d_gate_ref[i], gate_ref[...]) + dot(d_up_ref[i], up_ref[...])
    put_halves(part, halves)


def feed_back(d, act, slope, weights, dtype):
    rows, width = sum(v.shape[0] for v in d), d[0].shape[1]
    groups, ff = len(weights) // 3, weights[0].shape[0]
    whole = pl.BlockSpec(memory_space=pltpu.VMEM)
    return pl.pallas_call(
        functools.partial(feed_back_kernel, groups, len(d)),
        out_shape=(
            *[jax.ShapeDtypeStruct((rows // 2, width), dtype)] * 2,
            *[jax.ShapeDtypeStruct((groups, rows, ff), bf16)] * 2,
        ),
        in_specs=[whole] * (2 + len(d) + len(weights)),
        out_specs=(whole,) * 4,
        cost_estimate=BRIEF,
        compiler_params=pltpu.CompilerParams(vmem_limit_bytes=FEED_VMEM),
        name="feed_back",
    )(act, slope, *d, *weights)


def weight_grad_kernel(index, sizes, count, pieces, *refs):
    lefts, rights, rest = refs[:count], refs[count : count + pieces], refs[count + pieces :]
    extra, outs = rest[: -len(sizes)], rest[-len(sizes) :]
    left = jnp.concatenate([v[index] for v in lefts], axis=0)
    right = jnp.concatenate([v[...] for v in rights], axis=0)
    total = dot_cols(left, right)
    if extra:
        total = total + extra[0][...].astype(f32)
    begin = 0
    for size, out in zip(sizes, outs):
        out[...] = total[begin : begin + size].astype(bf16)
        begin += size


def weight_grad(index, sizes, lefts, rights, *extra):
    rights = [piece for part in rights for piece in part]
    width = rights[0].shape[1]
    whole = pl.BlockSpec(memory_space=pltpu.VMEM)
    return pl.pallas_call(
        functools.partial(weight_grad_kernel, index, sizes, len(lefts), len(rights)),
        out_shape=tuple(jax.ShapeDtypeStruct((size, width), bf16) for size in sizes),
        in_specs=[whole] * (len(lefts) + len(rights) + len(extra)),
        out_specs=(whole,) * len(sizes),
        cost_estimate=BRIEF,
        compiler_params=pltpu.CompilerParams(vmem_limit_bytes=FEED_VMEM),
        name="weight_grad",
    )(*lefts, *rights, *extra)


def add(*terms):
    return functools.reduce(jnp.add, [t.astype(f32) for t in terms])


fence = lax.optimization_barrier


class Plain:
    def __init__(self, n):
        self.n = n
        self.rank = lax.axis_index("seq")

    def order(self):
        return jnp.arange(self.n, dtype=jnp.int32)

    def slots(self):
        return jnp.zeros(1, jnp.int32)

    def send(self, shard):
        return [shard]

    def paired(self, shards):
        return [lax.all_gather(shards[0], "seq", axis=0, tiled=True)]

    def joined(self, shard, near, far):
        return self.paired([shard])

    def columns(self, value):
        return [value]

    def restored(self, parts):
        return parts[0]

    def pair(self, shard):
        return [shard]

    def near(self, shard):
        return ()

    def far(self, near):
        return ()

    def tokens(self, shard, near, far):
        whole = lax.all_gather(shard, "seq", axis=0, tiled=True)
        return [(part,) for part in jnp.split(whole, self.n, axis=0)]

    def early(self, x, y):
        return ()

    def relay(self, far):
        return ()

    def late(self, x, y, relay):
        return ()

    def parts_sum(self, parts, early, late):
        return self.scatter(all_of([half.astype(bf16) for part in parts for half in part]))

    def across(self, value):
        return ()

    def group(self, partial, moved):
        return (partial[0],)

    def group_near(self, group):
        return ()

    def group_far(self, group):
        return ()

    def group_sum(self, group, near, far):
        return self.scatter(group[0])

    def scatter(self, partial):
        return lax.psum_scatter(
            partial.astype(bf16), "seq", scatter_dimension=0, tiled=True
        ).astype(f32)

    def projection(self, left, right, gains):
        grad = dot_cols(left, right).reshape(self.n, -1, right.shape[1])
        gains = jnp.broadcast_to(gains[None], (self.n, *gains.shape))
        return [jnp.concatenate([grad, gains], axis=1).reshape(-1, right.shape[1])]

    def line(self):
        return PlainLine()


class Cube(Plain):
    chips = (0, 2, 4, 6)
    ranks = (0, 2, 4, 6, 1, 3, 5, 7)

    def hop(self, value, bit):
        return lax.ppermute(value, "seq", [(i, i ^ bit) for i in range(8)])

    def order(self):
        return self.rank ^ jnp.array(self.ranks, dtype=jnp.int32)

    def slots(self):
        return self.order()

    def send(self, shard):
        return [shard] + [self.hop(shard, bit) for bit in self.chips[1:]]

    def joined(self, shard, near, far):
        return self.paired([shard, *near, *far])

    def paired(self, shards):
        group = all_of(shards)
        return [group, self.hop(group, 1)]

    def near(self, shard):
        return (self.hop(shard, 2), self.hop(shard, 4))

    def far(self, near):
        half = near[0].shape[0] // 2
        return (self.hop(near[1][:half], 2), self.hop(near[0][half:], 4))

    def tokens(self, shard, near, far):
        return [(shard,), *[(v,) for v in near], tuple(far)]

    def early(self, x, y):
        return (self.hop(x[0], 2), self.hop(y[1], 4))

    def relay(self, far):
        return (self.hop(far[0], 2), self.hop(far[1], 4))

    def late(self, x, y, relay):
        return (
            self.hop(add(x[1], relay[1]).astype(bf16), 2),
            self.hop(add(y[0], relay[0]).astype(bf16), 4),
        )

    def parts_sum(self, parts, early, late):
        own = parts[0]
        return all_of([add(own[0], early[0], late[1]), add(own[1], early[1], late[0])])

    def across(self, value):
        return (self.hop(value, 1),)

    def group(self, partial, moved):
        parts = jnp.split(add(partial[0], *moved), 4, axis=0)
        return (parts[0], *[p.astype(bf16) for p in parts[1:]])

    def group_near(self, group):
        return (self.hop(group[1], 2), self.hop(group[2], 4))

    def group_far(self, group):
        return (self.hop(group[3], 6),)

    def group_sum(self, group, near, far):
        return add(group[0], *near, *far)

    def select(self, size, stride):
        shape = (self.n * size, self.n * stride)
        col = lax.broadcasted_iota(jnp.int32, shape, 1)
        block, at = col // stride, col % stride
        source = self.rank ^ ((2 * block) % 8 + block // 4)
        row = lax.broadcasted_iota(jnp.int32, shape, 0)
        return ((row == source * size + at) & (at < size)).astype(bf16)

    def columns(self, value):
        moved = dot(value, self.select(value.shape[1] // self.n, value.shape[1] // self.n))
        return jnp.split(moved.astype(value.dtype), 2, axis=1)

    def restored(self, parts):
        value = jnp.concatenate(parts, axis=1)
        pick = self.select(value.shape[1] // self.n, value.shape[1] // self.n).astype(f32)
        return lax.dot_general(
            value, pick, (((1,), (1,)), ((), ())), precision=lax.Precision.HIGHEST
        )

    def pair(self, shard):
        return [shard, self.hop(shard, 1)]

    def projection(self, left, right, gains):
        size, extra = left.shape[1] // self.n, gains.shape[0]
        stride = size + extra
        moved = dot(left, self.select(size, stride)).astype(bf16)
        shape = (extra, self.n * stride)
        at = lax.broadcasted_iota(jnp.int32, shape, 1) % stride
        pick = (at == size + lax.broadcasted_iota(jnp.int32, shape, 0)).astype(bf16)
        left = jnp.concatenate([moved, pick], axis=0)
        right = jnp.concatenate([right, gains.astype(bf16)], axis=0)
        half = self.n * stride // 2
        return [dot_cols(left[:, :half], right), dot_cols(left[:, half:], right)]

    def line(self):
        return CubeLine()


class PlainLine:
    def __init__(self):
        self.chunks = []

    def step(self, beside):
        return fence(beside(()))

    def finish(self):
        return [lax.psum(c, "dp").astype(f32) for c in self.chunks]


class CubeLine(PlainLine):
    def __init__(self):
        super().__init__()
        place = lax.axis_index("dp")
        self.inner = (place == 1) | (place == 2)
        self.halves, self.totals, self.out = {}, {}, {}
        self.at = 0

    def step(self, beside):
        tick = self.at
        self.at += 1
        mine = self.chunks[tick] if tick < len(self.chunks) else None
        back, half = self.totals.get(tick - 2), self.halves.get(tick - 1)
        got = {}
        if mine is not None and back is not None and mine.shape == back.shape:
            both = jnp.where(self.inner, back, mine)
            got["in"] = lax.ppermute(both, "dp", [(0, 1), (1, 0), (2, 3), (3, 2)])
        else:
            if back is not None:
                got["out"] = lax.ppermute(back, "dp", [(1, 0), (2, 3)])
            if mine is not None:
                got["in"] = lax.ppermute(mine, "dp", [(0, 1), (3, 2)])
        if half is not None:
            got["middle"] = lax.ppermute(half, "dp", [(1, 2), (2, 1)])
        values = beside(())
        got, values, self.chunks[tick + 1 :] = fence((got, values, self.chunks[tick + 1 :]))
        if mine is not None:
            self.halves[tick] = add(mine, got["in"]).astype(bf16)
        if half is not None:
            self.totals[tick - 1] = add(half, got["middle"]).astype(bf16)
        if back is not None:
            self.out[tick - 2] = jnp.where(self.inner, back, got["out"] if "out" in got else got["in"])
        return values

    def finish(self):
        while self.at < len(self.chunks) + 2:
            self.step(lambda values: values)
        return [self.out[i].astype(f32) for i in range(len(self.chunks))]


def all_of(values):
    return jnp.concatenate(values, axis=0)


def on_device(
    kind,
    layer_input,
    segment_ids,
    position_ids,
    w_query,
    w_keyval,
    w_out,
    w_gate,
    w_up,
    w_down,
    g_input,
    g_post_attn,
    g_pre_ffn,
    g_post_ffn,
    g_query,
    g_key,
    out_grad,
):
    n = lax.axis_size("seq")
    comm = kind(n)
    rows = layer_input.shape[1]
    width = layer_input.shape[2]
    ff = w_gate.shape[1]
    row_offset = comm.rank * rows

    x = layer_input[0].astype(f32)
    positions = position_ids[0]
    keyval_sent = comm.send(w_keyval)
    a_normed, a_factor = rms_forward(x)
    a_low = (a_normed * g_input).astype(bf16)
    a_columns = comm.columns(a_low)
    angles = rope_angles(positions, HEAD)
    cosine, sine = jnp.cos(angles), jnp.sin(angles)
    keyval_sent, a_columns, w_query = fence((keyval_sent, a_columns, w_query))
    query_near = comm.near(w_query)
    keyval_blocks = comm.paired(keyval_sent)
    kv_pre = add(*[dot(a, w) for a, w in zip(a_columns, keyval_blocks)])
    k_hat, k_factor = rms_forward(kv_pre[:, :HEAD])
    k_low = rotate(k_hat * g_key, cosine, sine).astype(bf16)
    kv_low = jnp.concatenate([k_low, kv_pre[:, HEAD:].astype(bf16)], axis=1)
    kv_low, query_near = fence((kv_low, query_near))
    kv_near = comm.near(kv_low)
    query_far = comm.far(query_near)
    kv_near, query_near, query_far, w_out = fence((kv_near, query_near, query_far, w_out))
    kv_far = comm.far(kv_near)
    query_blocks = comm.joined(w_query, query_near, query_far)
    q_pre = add(*[dot(a, w) for a, w in zip(a_columns, query_blocks)])
    kv_far, q_pre, w_out = fence((kv_far, q_pre, w_out))
    out_near = comm.near(w_out)
    kv_blocks = comm.joined(kv_low, kv_near, kv_far)
    kv_blocks, out_near = fence((kv_blocks, out_near))
    out_far = comm.far(out_near)
    order = jnp.concatenate(
        [comm.order(), row_offset[None], (row_offset - positions[0])[None], comm.slots()]
    ).astype(jnp.int32)
    head_args = (
        comm.slots().shape[0],
        order,
        q_pre,
        cosine,
        sine,
        g_query[None],
        positions[:, None],
        *kv_blocks,
    )
    att_low, inverse = attend(*head_args)
    out_far, att_low, w_gate, w_up, w_down = fence((out_far, att_low, w_gate, w_up, w_down))
    weights = [comm.pair(w) for w in (w_gate.T, w_up.T, w_down)]
    weights = [w[i] for i in range(len(weights[0])) for w in weights]
    groups = len(weights) // 3
    out_blocks = comm.joined(w_out, out_near, out_far)
    att_columns = jnp.split(att_low, len(out_blocks), axis=1)
    attn = add(*[dot(v, w) for v, w in zip(att_columns, out_blocks)])
    attn_normed, attn_factor = rms_forward(attn)
    middle = x + attn_normed * g_post_attn
    b_normed, b_factor = rms_forward(middle)
    b_low = (b_normed * g_pre_ffn).astype(bf16)
    b_low, weights = fence((b_low, weights))

    near = comm.near(b_low)
    kept = [feed((b_low,), weights, f32)]
    kept, near = fence((kept, near))
    far = comm.far(near)
    b_list = comm.tokens(b_low, near, far)
    kept += [feed(part, weights, bf16) for part in b_list[1:-1]]
    kept, far, tail = fence((kept, far, b_list[-1]))
    b_list[-1] = tail
    early = comm.early(kept[1][:2], kept[2][:2])
    kept.append(feed(tail, weights, bf16))
    kept, early = fence((kept, early))
    parts = [v[:2] for v in kept]
    hidden, acts, slopes = [[v[i] for v in kept] for i in (2, 3, 4)]
    relay = comm.relay(parts[-1])
    late = comm.late(parts[1], parts[2], relay)
    ffn = comm.parts_sum(parts, early, late)
    ffn_normed, ffn_factor = rms_forward(ffn)
    layer_out = (middle + ffn_normed * g_post_ffn).astype(bf16)

    g = out_grad[0]
    d_ffn = rms_backward(g * g_post_ffn, ffn_normed, ffn_factor).astype(bf16)
    d_ffn, ffn_normed = fence((d_ffn, ffn_normed))
    line = comm.line()
    thirds = [ff // 3] * 3

    def back(part, i):
        return feed_back(part, acts[i], slopes[i], weights, bf16 if i else f32)

    def other_half(lefts, rights):
        return weight_grad(1, [ff], lefts, rights) if groups > 1 else ()

    near = comm.near(d_ffn)
    gain_post_ffn = jnp.sum(g * ffn_normed, axis=0)
    kept = [back((d_ffn,), 0)]
    kept, near, gain_post_ffn = fence((kept, near, gain_post_ffn))
    far = comm.far(near)
    d_list = comm.tokens(d_ffn, near, far)
    last = len(d_list) - 1
    kept += [back(d_list[i], i) for i in range(1, last)]
    kept, far, tail = fence((kept, far, d_list[-1]))
    d_list[-1] = tail

    early = comm.early(kept[1][:2], kept[2][:2])
    other = [comm.hop(v, 1) for v in other_half(hidden, d_list)]
    kept.append(back(tail, last))
    kept, early, other = fence((kept, early, other))
    parts = [v[:2] for v in kept]
    d_gate, d_up = [[v[i] for v in kept] for i in (2, 3)]
    line.chunks += weight_grad(0, thirds, hidden, d_list, *other)

    line.chunks, parts, d_gate, d_up, a_late = fence((line.chunks, parts, d_gate, d_up, a_low))

    def beside(_):
        relay = comm.relay(parts[-1])
        late = comm.late(parts[1], parts[2], relay)
        others = other_half(d_gate, b_list), other_half(d_up, b_list)
        return late, others, d_gate, d_up, parts, early

    late, others, d_gate, d_up, parts, early = line.step(beside)

    def beside(_):
        other, other_up = [[comm.hop(v, 1) for v in values] for values in others]
        d_b = comm.parts_sum(parts, early, late)
        gain_pre_ffn = jnp.sum(d_b * b_normed, axis=0)
        d_middle = g + rms_backward(d_b * g_pre_ffn, b_normed, b_factor)
        gain_post_attn = jnp.sum(d_middle * attn_normed, axis=0)
        d_attn = rms_backward(d_middle * g_post_attn, attn_normed, attn_factor).astype(bf16)
        d_att = jnp.concatenate([dot_rows(d_attn, w).astype(bf16) for w in out_blocks], axis=1)
        grads = weight_grad(0, thirds, d_gate, b_list, *other)
        return list(grads), d_up, other_up, d_middle, d_attn, d_att, (gain_post_attn, gain_pre_ffn)

    grads, d_up, other_up, d_middle, d_attn, d_att, gains = line.step(beside)
    gain_post_attn, gain_pre_ffn = gains
    line.chunks += grads

    def beside(_):
        heads = attend_back(*head_args, saved=(att_low, inverse), d_att=d_att)
        return heads, d_up, d_attn

    (d_q_pre, *d_kv_blocks, gain_query), d_up, d_attn = line.step(beside)

    def beside(_):
        group = comm.group(d_kv_blocks, comm.across(d_kv_blocks[-1]))
        near = comm.group_near(group)
        grads = weight_grad(0, thirds, d_up, b_list, *other_up)
        return group, near, list(grads), d_attn, a_late

    group, near, grads, d_attn, a_late = line.step(beside)
    line.chunks += grads

    def beside(_):
        d_kv = comm.group_sum(group, near, comm.group_far(group))
        d_k_normed = rotate(d_kv[:, :HEAD], cosine, -sine)
        gain_key = jnp.sum(d_k_normed * k_hat, axis=0)
        d_k_pre = rms_backward(d_k_normed * g_key, k_hat, k_factor)
        d_kv_pre = jnp.concatenate([d_k_pre, d_kv[:, HEAD:]], axis=1).astype(bf16)
        d_a = comm.restored(
            [
                dot_rows(d_q_pre, query) + dot_rows(d_kv_pre, keyval)
                for query, keyval in zip(query_blocks, keyval_blocks)
            ]
        )
        gain_input = jnp.sum(d_a * a_normed, axis=0)
        grad_out = [dot_cols(v, d_attn) for v in att_columns]
        return d_kv_pre, d_a, (gain_input, gain_key), grad_out, a_late

    d_kv_pre, d_a, (gain_input, gain_key), grad_out, a_late = line.step(beside)

    def beside(_):
        out_moved = comm.across(grad_out[-1].astype(bf16))
        d_qkv = jnp.concatenate([d_q_pre, d_kv_pre], axis=1)
        gains = [gain_input, gain_post_attn, gain_pre_ffn, gain_post_ffn]
        gains.append(jnp.concatenate([gain_query[0], gain_key]))
        gains = [jnp.pad(v, (0, d_qkv.shape[1] - v.shape[0])) for v in gains]
        gains = jnp.pad(jnp.stack(gains), ((0, 16 - len(gains)), (0, 0)))
        grad_qkv = comm.projection(a_late, d_qkv, gains)
        return comm.group(grad_out, out_moved), grad_qkv, d_a

    out_group, grad_qkv, d_a = line.step(beside)

    def beside(_):
        qkv_moved = comm.across(grad_qkv[-1].astype(bf16))
        out_near = comm.group_near(out_group)
        d_input = d_middle + rms_backward(d_a * g_input, a_normed, a_factor)
        return comm.group(grad_qkv, qkv_moved), out_group, out_near, d_input

    group, out_group, out_near, d_input = line.step(beside)

    def beside(_):
        return group, comm.group_near(group), comm.group_far(out_group)

    group, near, out_far = line.step(beside)
    total_out = comm.group_sum(out_group, out_near, out_far).astype(bf16)

    def beside(_):
        return comm.group_far(group), near, total_out

    far, near, total_out = line.step(beside)
    line.chunks += [comm.group_sum(group, near, far).astype(bf16), total_out]
    *done, tail, total_out = line.finish()
    down, gate, up = all_of(done[:3]), all_of(done[3:6]), all_of(done[6:])
    shard = width // n

    def mine(row, at, size):
        return lax.dynamic_slice_in_dim(tail[shard + row], at + comm.rank * size, size)

    names = [mine(i, 0, shard) for i in range(4)]
    names += [mine(4, i * HEAD, HEAD // n) for i in range(2)]
    return (
        layer_out[None],
        d_input[None],
        tail[:shard, : HEADS * HEAD],
        tail[:shard, HEADS * HEAD :],
        total_out,
        gate.T,
        up.T,
        down,
        *names,
    )


def solution(mesh):
    cube = mesh.shape["seq"] == 8 and mesh.shape["dp"] == 4
    in_specs = (
        P("dp", "seq", None),
        P("dp", None),
        P("dp", "seq"),
        P("seq", None),
        P("seq", None),
        P("seq", None),
        P(None, "seq"),
        P(None, "seq"),
        P("seq", None),
        P(),
        P(),
        P(),
        P(),
        P(),
        P(),
        P("dp", "seq", None),
    )
    out_specs = (
        P("dp", "seq", None),
        P("dp", "seq", None),
        P("seq", None),
        P("seq", None),
        P("seq", None),
        P(None, "seq"),
        P(None, "seq"),
        P("seq", None),
        P("seq"),
        P("seq"),
        P("seq"),
        P("seq"),
        P("seq"),
        P("seq"),
    )
    return jax.shard_map(
        functools.partial(on_device, Cube if cube else Plain),
        mesh=mesh,
        in_specs=in_specs,
        out_specs=out_specs,
        check_vma=False,
    )
```

```python
import functools

import jax
import jax.numpy as jnp
from jax import lax
from jax.experimental import pallas as pl
from jax.experimental.pallas import tpu as pltpu
from jax.sharding import PartitionSpec as P

HEADS = 4
HEAD = 256
BLOCK = 256
LANES = 128
FEED_VMEM = 12 << 20

norm_eps = 1e-06
rope_base = 1000000.0
score_scale = HEAD**-0.5
bf16 = jnp.bfloat16
f32 = jnp.float32
BRIEF = pl.CostEstimate(flops=1, bytes_accessed=1, transcendentals=0)


def rms_forward(values):
    factor = lax.rsqrt(jnp.mean(values * values, axis=-1, keepdims=True) + norm_eps)
    return (values * factor, factor)


def rms_backward(upstream, normed, factor):
    return factor * (upstream - normed * jnp.mean(upstream * normed, axis=-1, keepdims=True))


def rope_angles(positions, width):
    half_width = width // 2
    inverse_freq = rope_base ** (-(jnp.arange(half_width).astype(f32) * 2.0 / width))
    return positions.astype(f32)[:, None] * inverse_freq[None, :]


def rotate(values, cosine, sine):
    half_width = values.shape[-1] // 2
    first = values[..., :half_width]
    second = values[..., half_width:]
    return jnp.concatenate(
        [first * cosine - second * sine, second * cosine + first * sine], axis=-1
    )


def dot(left, right):
    return jnp.dot(left, right, preferred_element_type=f32)


def dot_rows(left, right):
    return lax.dot_general(left, right, (((1,), (1,)), ((), ())), preferred_element_type=f32)


def dot_cols(left, right):
    return lax.dot_general(left, right, (((0,), (0,)), ((), ())), preferred_element_type=f32)


def visible_mask(block_id, first_row, pos_ref):
    shape = (BLOCK, BLOCK)
    query = first_row + lax.broadcasted_iota(jnp.int32, shape, 0)
    key = block_id * BLOCK + lax.broadcasted_iota(jnp.int32, shape, 1)
    return (key <= query) & (key >= query - pos_ref[...])


def put_queries(q_ref, q_pre_ref, gain_ref, cosine, sine):
    for h in range(HEADS):
        cols = pl.ds(h * HEAD, HEAD)
        normed, _ = rms_forward(q_pre_ref[:, cols])
        q_ref[:, cols] = rotate(normed * gain_ref[...], cosine, sine).astype(bf16)


def attend_kernel(
    n_blocks,
    columns,
    order_ref,
    q_pre_ref,
    cos_ref,
    sin_ref,
    gain_ref,
    pos_ref,
    *refs,
):
    kv_refs, (att_low_ref, inv_ref, q_ref, att_ref, total_ref) = refs[:-5], refs[-5:]
    slot = order_ref.shape[0] - columns
    first_row = order_ref[n_blocks]
    first_key = order_ref[n_blocks + 1]
    cosine, sine = cos_ref[...], sin_ref[...]
    put_queries(q_ref, q_pre_ref, gain_ref, cosine, sine)
    att_ref[...] = jnp.zeros_like(att_ref)
    total_ref[...] = jnp.zeros_like(total_ref)

    def step(kv_ref, base, k, _):
        block_id = order_ref[base + k]
        live = (block_id * BLOCK <= first_row) & ((block_id + 1) * BLOCK > first_key)

        @pl.when(live)
        def _():
            rows = pl.ds(pl.multiple_of(k * BLOCK, BLOCK), BLOCK)
            keys = kv_ref[rows, :HEAD]
            vals = kv_ref[rows, HEAD:]
            visible = visible_mask(block_id, first_row, pos_ref)
            for h in range(HEADS):
                cols = pl.ds(h * HEAD, HEAD)
                scores = dot_rows(q_ref[:, cols], keys) * score_scale
                weight = jnp.where(visible, jnp.exp(scores), 0.0)
                total_ref[:, pl.ds(h * LANES, LANES)] += weight[:, :LANES] + weight[:, LANES:]
                att_ref[:, cols] += dot(weight.astype(bf16), vals)

        return 0

    each = n_blocks // len(kv_refs)
    for i, kv_ref in enumerate(kv_refs):
        lax.fori_loop(0, each, functools.partial(step, kv_ref, i * each), 0)
    for h in range(HEADS):
        cols = pl.ds(h * HEAD, HEAD)
        lanes = pl.ds(h * LANES, LANES)
        inverse = 1.0 / jnp.sum(total_ref[:, lanes], axis=-1, keepdims=True)
        inv_ref[:, pl.ds(h, 1)] = inverse
        att_ref[:, cols] = att_ref[:, cols] * inverse
    size = HEADS * HEAD // columns
    for k in range(columns):
        source = pl.ds(pl.multiple_of(order_ref[slot + k] * size, size), size)
        att_low_ref[:, pl.ds(k * size, size)] = att_ref[:, source].astype(bf16)


def attend(columns, order, q_pre, cosine, sine, gain, pos, *kv):
    rows = q_pre.shape[0]
    n_blocks = sum(v.shape[0] for v in kv) // BLOCK
    whole = pl.BlockSpec(memory_space=pltpu.VMEM)
    return pl.pallas_call(
        functools.partial(attend_kernel, n_blocks, columns),
        out_shape=(
            jax.ShapeDtypeStruct((rows, HEADS * HEAD), bf16),
            jax.ShapeDtypeStruct((rows, LANES), f32),
        ),
        in_specs=[pl.BlockSpec(memory_space=pltpu.SMEM)] + [whole] * (5 + len(kv)),
        out_specs=(whole,) * 2,
        scratch_shapes=[
            pltpu.VMEM((rows, HEADS * HEAD), bf16),
            pltpu.VMEM((rows, HEADS * HEAD), f32),
            pltpu.VMEM((rows, HEADS * LANES), f32),
        ],
        cost_estimate=BRIEF,
        compiler_params=pltpu.CompilerParams(vmem_limit_bytes=8 << 20),
        name="attend",
    )(order, q_pre, cosine, sine, gain, pos, *kv)


def attend_back_kernel(
    n_blocks,
    columns,
    order_ref,
    q_pre_ref,
    cos_ref,
    sin_ref,
    gain_ref,
    pos_ref,
    att_ref,
    inv_ref,
    d_moved_ref,
    *refs,
):
    groups = (len(refs) - 7) // 2
    kv_refs, d_q_pre_ref, d_kv_refs = refs[:groups], refs[groups], refs[groups + 1 : -6]
    d_gain_ref, d_q_ref, row_dot_ref, d_att_ref, q_ref, dot_ref = refs[-6:]
    cosine, sine = cos_ref[...], sin_ref[...]
    put_queries(q_ref, q_pre_ref, gain_ref, cosine, sine)
    slot = order_ref.shape[0] - columns
    size = HEADS * HEAD // columns
    for k in range(columns):
        target = pl.ds(pl.multiple_of(order_ref[slot + k] * size, size), size)
        moved = d_moved_ref[:, pl.ds(k * size, size)]
        d_att_ref[:, target] = moved
        dot_ref[:, target] = moved.astype(f32) * att_ref[:, pl.ds(k * size, size)].astype(f32)
    first_row = order_ref[n_blocks]
    first_key = order_ref[n_blocks + 1]
    for h in range(HEADS):
        cols = pl.ds(h * HEAD, HEAD)
        row_dot_ref[:, pl.ds(h, 1)] = jnp.sum(dot_ref[:, cols], axis=-1, keepdims=True)
    d_q_ref[...] = jnp.zeros_like(d_q_ref)

    def step(kv_ref, d_kv_ref, base, k, _):
        block_id = order_ref[base + k]
        live = (block_id * BLOCK <= first_row) & ((block_id + 1) * BLOCK > first_key)
        rows = pl.ds(pl.multiple_of(k * BLOCK, BLOCK), BLOCK)

        @pl.when(live)
        def _():
            keys = kv_ref[rows, :HEAD]
            vals = kv_ref[rows, HEAD:]
            visible = visible_mask(block_id, first_row, pos_ref)
            d_keys = jnp.zeros((BLOCK, HEAD), f32)
            d_vals = jnp.zeros((BLOCK, HEAD), f32)
            for h in range(HEADS):
                cols = pl.ds(h * HEAD, HEAD)
                query = q_ref[:, cols]
                d_att = d_att_ref[:, cols]
                inverse = inv_ref[:, pl.ds(h, 1)]
                row_dot = row_dot_ref[:, pl.ds(h, 1)]
                scores = dot_rows(query, keys) * score_scale
                prob = jnp.where(visible, jnp.exp(scores), 0.0) * inverse
                d_prob = dot_rows(d_att, vals)
                d_scores = (prob * (d_prob - row_dot)).astype(bf16)
                d_q_ref[:, cols] += dot(d_scores, keys)
                d_keys += dot_cols(d_scores, query)
                d_vals += dot_cols(prob.astype(bf16), d_att)
            d_kv_ref[rows, :HEAD] = (d_keys * score_scale).astype(bf16)
            d_kv_ref[rows, HEAD:] = d_vals.astype(bf16)

        @pl.when(jnp.logical_not(live))
        def _():
            d_kv_ref[rows, :] = jnp.zeros((BLOCK, 2 * HEAD), bf16)

        return 0

    each = n_blocks // groups
    for i in range(groups):
        walk = functools.partial(step, kv_refs[i], d_kv_refs[i], i * each)
        lax.fori_loop(0, each, walk, 0)
    d_gain = jnp.zeros((1, HEAD), f32)
    for h in range(HEADS):
        cols = pl.ds(h * HEAD, HEAD)
        normed, factor = rms_forward(q_pre_ref[:, cols])
        d_normed = rotate(d_q_ref[:, cols] * score_scale, cosine, -sine)
        d_gain += jnp.sum(d_normed * normed, axis=0, keepdims=True)
        d_q_pre_ref[:, cols] = rms_backward(d_normed * gain_ref[...], normed, factor).astype(bf16)
    d_gain_ref[...] = d_gain


def attend_back(columns, order, q_pre, cosine, sine, gain, pos, *kv, saved, d_att):
    rows = q_pre.shape[0]
    n_blocks = sum(v.shape[0] for v in kv) // BLOCK
    whole = pl.BlockSpec(memory_space=pltpu.VMEM)
    return pl.pallas_call(
        functools.partial(attend_back_kernel, n_blocks, columns),
        out_shape=(
            jax.ShapeDtypeStruct((rows, HEADS * HEAD), bf16),
            *[jax.ShapeDtypeStruct(v.shape, bf16) for v in kv],
            jax.ShapeDtypeStruct((1, HEAD), f32),
        ),
        in_specs=[pl.BlockSpec(memory_space=pltpu.SMEM)] + [whole] * (8 + len(kv)),
        out_specs=(whole,) * (2 + len(kv)),
        scratch_shapes=[
            pltpu.VMEM((rows, HEADS * HEAD), f32),
            pltpu.VMEM((rows, LANES), f32),
            pltpu.VMEM((rows, HEADS * HEAD), bf16),
            pltpu.VMEM((rows, HEADS * HEAD), bf16),
            pltpu.VMEM((rows, HEADS * HEAD), f32),
        ],
        cost_estimate=BRIEF,
        compiler_params=pltpu.CompilerParams(vmem_limit_bytes=10 << 20),
        name="attend_back",
    )(order, q_pre, cosine, sine, gain, pos, *saved, d_att, *kv)


def gelu_parts(gate):
    c = (2.0 / jnp.pi) ** 0.5
    square = gate * gate
    t = jnp.tanh(gate * (c + (c * 0.044715) * square))
    half = 0.5 + 0.5 * t
    act = gate * half
    slope = half + act * (1.0 - t) * (c + (3 * c * 0.044715) * square)
    return act, slope


def put_halves(part, refs):
    half = part.shape[0] // 2
    refs[0][...] = part[:half].astype(refs[0].dtype)
    refs[1][...] = part[half:].astype(refs[1].dtype)


def feed_kernel(groups, pieces, *refs):
    weights, halves, (hidden_ref, act_ref, slope_ref) = refs[pieces:-5], refs[-5:-3], refs[-3:]
    b = jnp.concatenate([r[...] for r in refs[:pieces]], axis=0)
    part = 0.0
    for i in range(groups):
        gate_ref, up_ref, down_ref = weights[3 * i : 3 * i + 3]
        gate = dot_rows(b, gate_ref[...])
        up = dot_rows(b, up_ref[...])
        act, slope = gelu_parts(gate)
        hidden_ref[i] = (act * up).astype(bf16)
        act_ref[i] = act.astype(bf16)
        slope_ref[i] = (up * slope).astype(bf16)
        part = part + dot(hidden_ref[i], down_ref[...])
    put_halves(part, halves)


def feed(b, weights, dtype):
    rows, width = sum(v.shape[0] for v in b), b[0].shape[1]
    groups, ff = len(weights) // 3, weights[0].shape[0]
    whole = pl.BlockSpec(memory_space=pltpu.VMEM)
    return pl.pallas_call(
        functools.partial(feed_kernel, groups, len(b)),
        out_shape=(
            *[jax.ShapeDtypeStruct((rows // 2, width), dtype)] * 2,
            *[jax.ShapeDtypeStruct((groups, rows, ff), bf16)] * 3,
        ),
        in_specs=[whole] * (len(b) + len(weights)),
        out_specs=(whole,) * 5,
        cost_estimate=BRIEF,
        compiler_params=pltpu.CompilerParams(vmem_limit_bytes=FEED_VMEM),
        name="feed",
    )(*b, *weights)


def feed_back_kernel(groups, pieces, act_ref, slope_ref, *refs):
    weights, halves, (d_gate_ref, d_up_ref) = refs[pieces:-4], refs[-4:-2], refs[-2:]
    d = jnp.concatenate([r[...] for r in refs[:pieces]], axis=0)
    part = 0.0
    for i in range(groups):
        gate_ref, up_ref, down_ref = weights[3 * i : 3 * i + 3]
        d_hidden = dot_rows(d, down_ref[...])
        d_gate_ref[i] = (d_hidden * slope_ref[i].astype(f32)).astype(bf16)
        d_up_ref[i] = (d_hidden * act_ref[i].astype(f32)).astype(bf16)
        part = part + dot(d_gate_ref[i], gate_ref[...]) + dot(d_up_ref[i], up_ref[...])
    put_halves(part, halves)


def feed_back(d, act, slope, weights, dtype):
    rows, width = sum(v.shape[0] for v in d), d[0].shape[1]
    groups, ff = len(weights) // 3, weights[0].shape[0]
    whole = pl.BlockSpec(memory_space=pltpu.VMEM)
    return pl.pallas_call(
        functools.partial(feed_back_kernel, groups, len(d)),
        out_shape=(
            *[jax.ShapeDtypeStruct((rows // 2, width), dtype)] * 2,
            *[jax.ShapeDtypeStruct((groups, rows, ff), bf16)] * 2,
        ),
        in_specs=[whole] * (2 + len(d) + len(weights)),
        out_specs=(whole,) * 4,
        cost_estimate=BRIEF,
        compiler_params=pltpu.CompilerParams(vmem_limit_bytes=FEED_VMEM),
        name="feed_back",
    )(act, slope, *d, *weights)


def weight_grad_kernel(index, sizes, count, pieces, *refs):
    lefts, rights, rest = refs[:count], refs[count : count + pieces], refs[count + pieces :]
    extra, outs = rest[: -len(sizes)], rest[-len(sizes) :]
    left = jnp.concatenate([v[index] for v in lefts], axis=0)
    right = jnp.concatenate([v[...] for v in rights], axis=0)
    total = dot_cols(left, right)
    if extra:
        total = total + extra[0][...].astype(f32)
    begin = 0
    for size, out in zip(sizes, outs):
        out[...] = total[begin : begin + size].astype(bf16)
        begin += size


def weight_grad(index, sizes, lefts, rights, *extra):
    rights = [piece for part in rights for piece in part]
    width = rights[0].shape[1]
    whole = pl.BlockSpec(memory_space=pltpu.VMEM)
    return pl.pallas_call(
        functools.partial(weight_grad_kernel, index, sizes, len(lefts), len(rights)),
        out_shape=tuple(jax.ShapeDtypeStruct((size, width), bf16) for size in sizes),
        in_specs=[whole] * (len(lefts) + len(rights) + len(extra)),
        out_specs=(whole,) * len(sizes),
        cost_estimate=BRIEF,
        compiler_params=pltpu.CompilerParams(vmem_limit_bytes=FEED_VMEM),
        name="weight_grad",
    )(*lefts, *rights, *extra)


def middle_back_kernel(counts, out_count, *refs):
    terms, refs = refs[: sum(counts)], refs[sum(counts) :]
    g_ref, middle_ref, attn_ref, pre_ref, post_ref = refs[:5]
    outs, (d_middle_ref, d_attn_ref, d_att_ref, gain_ref) = refs[5 : 5 + out_count], refs[-4:]
    pre, post = 0.0, 0.0
    half = g_ref.shape[0] // 2
    for i in range(2):
        own = terms[: counts[0]] if i == 0 else terms[counts[0] :]
        rows = pl.ds(i * half, half)
        d_b = functools.reduce(jnp.add, [t[...].astype(f32) for t in own])
        normed, factor = rms_forward(middle_ref[rows, :])
        pre = pre + jnp.sum(d_b * normed, axis=0, keepdims=True)
        d_middle = g_ref[rows, :] + rms_backward(d_b * pre_ref[...], normed, factor)
        d_middle_ref[rows, :] = d_middle
        normed, factor = rms_forward(attn_ref[rows, :])
        post = post + jnp.sum(d_middle * normed, axis=0, keepdims=True)
        d_attn = rms_backward(d_middle * post_ref[...], normed, factor).astype(bf16)
        d_attn_ref[rows, :] = d_attn
    at = 0
    for out in outs:
        d_att_ref[:, at : at + out.shape[0]] = dot_rows(d_attn_ref[...], out[...]).astype(bf16)
        at += out.shape[0]
    gain_ref[0:1, :] = pre
    gain_ref[1:2, :] = post


def middle_back(halves, g, middle, attn, g_pre, g_post, outs):
    rows, width = g.shape
    whole = pl.BlockSpec(memory_space=pltpu.VMEM)
    return pl.pallas_call(
        functools.partial(middle_back_kernel, [len(h) for h in halves], len(outs)),
        out_shape=(
            jax.ShapeDtypeStruct((rows, width), f32),
            jax.ShapeDtypeStruct((rows, width), bf16),
            jax.ShapeDtypeStruct((rows, HEADS * HEAD), bf16),
            jax.ShapeDtypeStruct((2, width), f32),
        ),
        in_specs=[whole] * (sum(len(h) for h in halves) + 5 + len(outs)),
        out_specs=(whole,) * 4,
        cost_estimate=BRIEF,
        compiler_params=pltpu.CompilerParams(vmem_limit_bytes=FEED_VMEM),
        name="middle_back",
    )(*halves[0], *halves[1], g, middle, attn, g_pre[None], g_post[None], *outs)


def add(*terms):
    return functools.reduce(jnp.add, [t.astype(f32) for t in terms])


fence = lax.optimization_barrier


class Plain:
    def __init__(self, n, rank, place):
        self.n, self.rank, self.place = n, rank, place

    def order(self):
        return jnp.arange(self.n, dtype=jnp.int32)

    def slots(self):
        return jnp.zeros(1, jnp.int32)

    def send(self, shard):
        return [shard]

    def paired(self, shards):
        return [lax.all_gather(shards[0], "seq", axis=0, tiled=True)]

    def joined(self, shard, near, far):
        return self.paired([shard])

    def columns(self, value):
        return [value]

    def ordered(self, blocks):
        return blocks[0]

    def pair(self, shard):
        return [shard]

    def near(self, shard):
        return ()

    def far(self, near):
        return ()

    def tokens(self, shard, near, far):
        whole = lax.all_gather(shard, "seq", axis=0, tiled=True)
        return [(part,) for part in jnp.split(whole, self.n, axis=0)]

    def early(self, x, y):
        return ()

    def relay(self, far):
        return ()

    def late(self, x, y, relay):
        return ()

    def halves(self, parts, early, late):
        whole = self.scatter(all_of([half.astype(bf16) for part in parts for half in part]))
        return [[half] for half in jnp.split(whole, 2, axis=0)]

    def across(self, value):
        return ()

    def group(self, partial, moved):
        return (partial[0],)

    def group_near(self, group):
        return ()

    def group_far(self, group):
        return ()

    def group_sum(self, group, near, far):
        return self.scatter(group[0])

    def scatter(self, partial):
        return lax.psum_scatter(
            partial.astype(bf16), "seq", scatter_dimension=0, tiled=True
        ).astype(f32)

    def projection(self, left, right, gains):
        grad = dot_cols(left, right).reshape(self.n, -1, right.shape[1])
        gains = jnp.broadcast_to(gains[None], (self.n, *gains.shape))
        return [jnp.concatenate([grad, gains], axis=1).reshape(-1, right.shape[1])]

    def line(self):
        return PlainLine(None)


class Cube(Plain):
    chips = (0, 2, 4, 6)
    ranks = (0, 2, 4, 6, 1, 3, 5, 7)

    def hop(self, value, bit):
        return lax.ppermute(value, "seq", [(i, i ^ bit) for i in range(8)])

    def order(self):
        return self.rank ^ jnp.array(self.ranks, dtype=jnp.int32)

    def slots(self):
        return self.order()

    def send(self, shard):
        return [shard] + [self.hop(shard, bit) for bit in self.chips[1:]]

    def joined(self, shard, near, far):
        return self.paired([shard, *near, *far])

    def paired(self, shards):
        group = all_of(shards)
        return [group, self.hop(group, 1)]

    def near(self, shard):
        return (self.hop(shard, 2), self.hop(shard, 4))

    def far(self, near):
        half = near[0].shape[0] // 2
        return (self.hop(near[1][:half], 2), self.hop(near[0][half:], 4))

    def tokens(self, shard, near, far):
        return [(shard,), *[(v,) for v in near], tuple(far)]

    def early(self, x, y):
        return (self.hop(x[0], 2), self.hop(y[1], 4))

    def relay(self, far):
        return (self.hop(far[0], 2), self.hop(far[1], 4))

    def late(self, x, y, relay):
        return (
            self.hop(add(x[1], relay[1]).astype(bf16), 2),
            self.hop(add(y[0], relay[0]).astype(bf16), 4),
        )

    def halves(self, parts, early, late):
        own = parts[0]
        return [[own[0], early[0], late[1]], [own[1], early[1], late[0]]]

    def across(self, value):
        return (self.hop(value, 1),)

    def group(self, partial, moved):
        parts = jnp.split(add(partial[0], *moved), 4, axis=0)
        return (parts[0], *[p.astype(bf16) for p in parts[1:]])

    def group_near(self, group):
        return (self.hop(group[1], 2), self.hop(group[2], 4))

    def group_far(self, group):
        return (self.hop(group[3], 6),)

    def group_sum(self, group, near, far):
        return add(group[0], *near, *far)

    def select(self, size, stride):
        shape = (self.n * size, self.n * stride)
        col = lax.broadcasted_iota(jnp.int32, shape, 1)
        block, at = col // stride, col % stride
        source = self.rank ^ ((2 * block) % 8 + block // 4)
        row = lax.broadcasted_iota(jnp.int32, shape, 0)
        return ((row == source * size + at) & (at < size)).astype(bf16)

    def columns(self, value):
        moved = dot(value, self.select(value.shape[1] // self.n, value.shape[1] // self.n))
        return jnp.split(moved.astype(value.dtype), 2, axis=1)

    def ordered(self, blocks):
        whole = all_of(blocks)
        size = whole.shape[0] // self.n
        return dot(self.select(size, size), whole).astype(whole.dtype)

    def pair(self, shard):
        return [shard, self.hop(shard, 1)]

    def projection(self, left, right, gains):
        size, extra = left.shape[1] // self.n, gains.shape[0]
        stride = size + extra
        moved = dot(left, self.select(size, stride)).astype(bf16)
        shape = (extra, self.n * stride)
        at = lax.broadcasted_iota(jnp.int32, shape, 1) % stride
        pick = (at == size + lax.broadcasted_iota(jnp.int32, shape, 0)).astype(bf16)
        left = jnp.concatenate([moved, pick], axis=0)
        right = jnp.concatenate([right, gains.astype(bf16)], axis=0)
        half = self.n * stride // 2
        return [dot_cols(left[:, :half], right), dot_cols(left[:, half:], right)]

    def line(self):
        return CubeLine((self.place == 1) | (self.place == 2))


class PlainLine:
    def __init__(self, inner):
        self.inner = inner
        self.chunks, self.wholes = [], []

    def add_rows(self, whole, parts):
        size = whole.shape[0] // parts
        self.wholes.append(whole)
        self.chunks += [(len(self.wholes) - 1, i * size, size) for i in range(parts)]

    def chunk(self, at):
        if len(self.chunks[at]) == 1:
            return self.chunks[at][0]
        source, start, size = self.chunks[at]
        return self.wholes[source][start : start + size]

    def step(self, beside):
        return fence(beside(()))

    def finish(self, early):
        chunks = [self.chunk(i) for i in range(len(self.chunks))]
        done = [lax.psum(c, "dp").astype(f32) for c in chunks]
        return done, early(done[-2])


class CubeLine(PlainLine):
    def __init__(self, inner):
        super().__init__(inner)
        self.halves, self.totals, self.out = {}, {}, {}
        self.at = 0

    def step(self, beside):
        tick = self.at
        self.at += 1
        mine = self.chunk(tick) if tick < len(self.chunks) else None
        back, half = self.totals.get(tick - 2), self.halves.get(tick - 1)
        got = {}
        if mine is not None and back is not None and mine.shape == back.shape:
            both = jnp.where(self.inner, back, mine)
            got["in"] = lax.ppermute(both, "dp", [(0, 1), (1, 0), (2, 3), (3, 2)])
        else:
            if back is not None:
                got["out"] = lax.ppermute(back, "dp", [(1, 0), (2, 3)])
            if mine is not None:
                got["in"] = lax.ppermute(mine, "dp", [(0, 1), (3, 2)])
        if half is not None:
            got["middle"] = lax.ppermute(half, "dp", [(1, 2), (2, 1)])
        values = beside(())
        later = [c for c in self.chunks[tick + 1 :] if len(c) == 1]
        got, values, later, self.wholes = fence((got, values, later, self.wholes))
        for at in range(tick + 1, len(self.chunks)):
            if len(self.chunks[at]) == 1:
                self.chunks[at] = later.pop(0)
        if mine is not None:
            self.halves[tick] = add(mine, got["in"]).astype(bf16)
        if half is not None:
            self.totals[tick - 1] = add(half, got["middle"]).astype(bf16)
        if back is not None:
            self.out[tick - 2] = jnp.where(self.inner, back, got["out"] if "out" in got else got["in"])
        return values

    def finish(self, early):
        count = len(self.chunks)
        while self.at < count + 1:
            self.step(lambda values: values)
        made = self.step(lambda _: early(self.out[count - 2].astype(f32)))
        return [self.out[i].astype(f32) for i in range(count)], made


def all_of(values):
    return jnp.concatenate(values, axis=0)


def on_device(
    kind,
    layer_input,
    segment_ids,
    position_ids,
    w_query,
    w_keyval,
    w_out,
    w_gate,
    w_up,
    w_down,
    g_input,
    g_post_attn,
    g_pre_ffn,
    g_post_ffn,
    g_query,
    g_key,
    out_grad,
):
    n = lax.axis_size("seq")
    comm = kind(n, lax.axis_index("seq"), lax.axis_index("dp"))
    rows = layer_input.shape[1]
    width = layer_input.shape[2]
    ff = w_gate.shape[1]
    positions = position_ids[0]
    row_offset = comm.rank * rows
    order = jnp.concatenate(
        [comm.order(), row_offset[None], (row_offset - positions[0])[None], comm.slots()]
    ).astype(jnp.int32)
    shard = width // n
    starts = (comm.rank * shard, comm.rank * (HEAD // n), HEAD + comm.rank * (HEAD // n))
    line = comm.line()
    position_column = positions[:, None]

    x = layer_input[0].astype(f32)
    keyval_sent = comm.send(w_keyval)
    a_normed, a_factor = rms_forward(x)
    a_low = (a_normed * g_input).astype(bf16)
    a_columns = comm.columns(a_low)
    angles = rope_angles(positions, HEAD)
    cosine, sine = jnp.cos(angles), jnp.sin(angles)
    keyval_sent, a_columns, w_query, order, starts, position_column, line.inner, comm.rank = fence(
        (keyval_sent, a_columns, w_query, order, starts, position_column, line.inner, comm.rank)
    )
    query_near = comm.near(w_query)
    keyval_blocks = comm.paired(keyval_sent)
    kv_pre = add(*[dot(a, w) for a, w in zip(a_columns, keyval_blocks)])
    k_hat, k_factor = rms_forward(kv_pre[:, :HEAD])
    k_low = rotate(k_hat * g_key, cosine, sine).astype(bf16)
    kv_low = jnp.concatenate([k_low, kv_pre[:, HEAD:].astype(bf16)], axis=1)
    kv_low, query_near = fence((kv_low, query_near))
    kv_near = comm.near(kv_low)
    query_far = comm.far(query_near)
    kv_near, query_near, query_far, w_out = fence((kv_near, query_near, query_far, w_out))
    kv_far = comm.far(kv_near)
    query_blocks = comm.joined(w_query, query_near, query_far)
    q_pre = add(*[dot(a, w) for a, w in zip(a_columns, query_blocks)])
    kv_far, q_pre, w_out, query_blocks, keyval_blocks = fence(
        (kv_far, q_pre, w_out, query_blocks, keyval_blocks)
    )
    out_near = comm.near(w_out)
    kv_blocks = comm.joined(kv_low, kv_near, kv_far)
    kv_blocks, out_near, w_gate, w_up, w_down = fence((kv_blocks, out_near, w_gate, w_up, w_down))
    out_far = comm.far(out_near)
    head_args = (
        comm.slots().shape[0],
        order,
        q_pre,
        cosine,
        sine,
        g_query[None],
        position_column,
        *kv_blocks,
    )
    att_low, inverse = attend(*head_args)
    out_far, att_low, w_gate, w_up, w_down = fence((out_far, att_low, w_gate, w_up, w_down))
    out_blocks = comm.joined(w_out, out_near, out_far)
    gate_w, up_w, down_w = [comm.pair(w) for w in (w_gate.T, w_up.T, w_down)]
    groups = len(gate_w)
    att_columns = jnp.split(att_low, len(out_blocks), axis=1)
    attn = add(*[dot(v, w) for v, w in zip(att_columns, out_blocks)])
    attn_normed, attn_factor = rms_forward(attn)
    middle = x + attn_normed * g_post_attn
    b_normed, b_factor = rms_forward(middle)
    b_low = (b_normed * g_pre_ffn).astype(bf16)
    b_low, query_blocks, keyval_blocks = fence((b_low, query_blocks, keyval_blocks))
    weights = [w[i] for i in range(groups) for w in (gate_w, up_w, down_w)]

    near = comm.near(b_low)
    kept = [feed((b_low,), weights, f32)]
    query_whole = comm.ordered(query_blocks)
    kept, near, query_whole, keyval_blocks = fence((kept, near, query_whole, keyval_blocks))
    far = comm.far(near)
    b_list = comm.tokens(b_low, near, far)
    kept += [feed(part, weights, bf16) for part in b_list[1:-1]]
    kept, far, tail = fence((kept, far, b_list[-1]))
    b_list[-1] = tail
    early = comm.early(kept[1][:2], kept[2][:2])
    kept.append(feed(tail, weights, bf16))
    kept, early = fence((kept, early))
    parts = [v[:2] for v in kept]
    hidden, acts, slopes = [[v[i] for v in kept] for i in (2, 3, 4)]
    relay = comm.relay(parts[-1])
    late = comm.late(parts[1], parts[2], relay)
    ffn = all_of([add(*terms) for terms in comm.halves(parts, early, late)])
    ffn_normed, ffn_factor = rms_forward(ffn)
    layer_out = (middle + ffn_normed * g_post_ffn).astype(bf16)

    g = out_grad[0]
    d_ffn = rms_backward(g * g_post_ffn, ffn_normed, ffn_factor).astype(bf16)
    d_ffn, ffn_normed, keyval_blocks = fence((d_ffn, ffn_normed, keyval_blocks))

    def back(part, i):
        return feed_back(part, acts[i], slopes[i], weights, bf16 if i else f32)

    def other_half(lefts, rights):
        return weight_grad(1, [ff], lefts, rights) if groups > 1 else ()

    near = comm.near(d_ffn)
    gain_post_ffn = jnp.sum(g * ffn_normed, axis=0)
    kept = [back((d_ffn,), 0)]
    keyval_whole = comm.ordered(keyval_blocks)
    kept, near, gain_post_ffn, keyval_whole = fence((kept, near, gain_post_ffn, keyval_whole))
    far = comm.far(near)
    d_list = comm.tokens(d_ffn, near, far)
    last = len(d_list) - 1
    kept += [back(d_list[i], i) for i in range(1, last)]
    kept, far, tail = fence((kept, far, d_list[-1]))
    d_list[-1] = tail

    other = [comm.hop(v, 1) for v in other_half(hidden, d_list)]
    kept.append(back(tail, last))
    kept, other = fence((kept, other))
    parts = [v[:2] for v in kept]
    d_gate, d_up = [[v[i] for v in kept] for i in (2, 3)]
    thirds = [ff // 3] * 3
    line.chunks += [(v,) for v in weight_grad(0, thirds, hidden, d_list, *other)]

    line.chunks, parts, d_gate, d_up, a_late = fence((line.chunks, parts, d_gate, d_up, a_low))

    def beside(_):
        early = comm.early(parts[1], parts[2])
        relay = comm.relay(parts[-1])
        others = other_half(d_gate, b_list), other_half(d_up, b_list)
        return early, relay, others, d_gate, d_up, parts

    early, relay, others, d_gate, d_up, parts = line.step(beside)

    def beside(_):
        late = comm.late(parts[1], parts[2], relay)
        (grads,) = weight_grad(0, [ff], d_gate, b_list, *[comm.hop(v, 1) for v in others[0]])
        late, grads = fence((late, grads))
        middles = middle_back(
            comm.halves(parts, early, late), g, middle, attn, g_pre_ffn, g_post_attn, out_blocks
        )
        return grads, d_up, others[1], middles

    grads, d_up, other_up, (d_middle, d_attn, d_att, gain_pair) = line.step(beside)
    line.add_rows(grads, 3)

    def beside(_):
        heads = attend_back(*head_args, saved=(att_low, inverse), d_att=d_att)
        grad_out = [dot_cols(v, d_attn) for v in att_columns]
        return heads, d_up, grad_out, [comm.hop(v, 1) for v in other_up]

    heads, d_up, grad_out, other_up = line.step(beside)
    d_q_pre, *d_kv_blocks, gain_query = heads

    def beside(_):
        group = comm.group(d_kv_blocks, comm.across(d_kv_blocks[-1]))
        near = comm.group_near(group)
        (grads,) = weight_grad(0, [ff], d_up, b_list, *other_up)
        return group, near, grads, grad_out, a_late, (gain_post_ffn, gain_pair, gain_query)

    group, near, grads, grad_out, a_late, early_gains = line.step(beside)
    line.add_rows(grads, 3)

    def beside(_):
        d_kv = comm.group_sum(group, near, comm.group_far(group))
        d_k_normed = rotate(d_kv[:, :HEAD], cosine, -sine)
        gain_key = jnp.sum(d_k_normed * k_hat, axis=0)
        d_k_pre = rms_backward(d_k_normed * g_key, k_hat, k_factor)
        d_kv_pre = jnp.concatenate([d_k_pre, d_kv[:, HEAD:]], axis=1).astype(bf16)
        d_a = dot_rows(d_q_pre, query_whole) + dot_rows(d_kv_pre, keyval_whole)
        gain_input = jnp.sum(d_a * a_normed, axis=0)
        out_group = comm.group(grad_out, comm.across(grad_out[-1].astype(bf16)))
        return d_kv_pre, d_a, (gain_input, gain_key), out_group, a_late, early_gains

    d_kv_pre, d_a, (gain_input, gain_key), out_group, a_late, early_gains = line.step(beside)
    gain_post_ffn, gain_pair, gain_query = early_gains

    def beside(_):
        out_near = comm.group_near(out_group)
        d_qkv = jnp.concatenate([d_q_pre, d_kv_pre], axis=1)
        gains = [gain_input, gain_pair[1], gain_pair[0], gain_post_ffn]
        gains.append(jnp.concatenate([gain_query[0], gain_key]))
        gains = [jnp.pad(v, (0, d_qkv.shape[1] - v.shape[0])) for v in gains]
        row = lax.broadcasted_iota(jnp.int32, (16, d_qkv.shape[1]), 0)
        gains = add(*[jnp.where(row == i, v[None], 0.0) for i, v in enumerate(gains)])
        grad_qkv = comm.projection(a_late, d_qkv, gains)
        return out_group, out_near, grad_qkv, d_a

    out_group, out_near, grad_qkv, d_a = line.step(beside)

    def beside(_):
        qkv_moved = comm.across(grad_qkv[-1].astype(bf16))
        out_far = comm.group_far(out_group)
        d_input = d_middle + rms_backward(d_a * g_input, a_normed, a_factor)
        total_out = comm.group_sum(out_group, out_near, out_far).astype(bf16)
        return comm.group(grad_qkv, qkv_moved), total_out, d_input

    group, total_out, d_input = line.step(beside)

    def beside(_):
        return group, comm.group_near(group), total_out

    group, near, total_out = line.step(beside)

    def beside(_):
        return comm.group_far(group), near, total_out

    far, near, total_out = line.step(beside)
    line.chunks += [(comm.group_sum(group, near, far).astype(bf16),), (total_out,)]
    def owned(tail):
        def mine(row, start, size):
            return lax.dynamic_slice(
                tail[shard + row], (start,), (size,), allow_negative_indices=False
            )

        grads = [tail[:shard, : HEADS * HEAD], tail[:shard, HEADS * HEAD :]]
        names = [mine(i, starts[0], shard) for i in range(4)]
        return grads, names + [mine(4, start, HEAD // n) for start in starts[1:]]

    (*done, _, total_out), ((grad_query, grad_keyval), names) = line.finish(owned)
    down, gate, up = all_of(done[:3]), all_of(done[3:6]), all_of(done[6:])
    return (
        layer_out[None],
        d_input[None],
        grad_query,
        grad_keyval,
        total_out,
        gate.T,
        up.T,
        down,
        *names,
    )


def solution(mesh):
    cube = mesh.shape["seq"] == 8 and mesh.shape["dp"] == 4
    in_specs = (
        P("dp", "seq", None),
        P("dp", None),
        P("dp", "seq"),
        P("seq", None),
        P("seq", None),
        P("seq", None),
        P(None, "seq"),
        P(None, "seq"),
        P("seq", None),
        P(),
        P(),
        P(),
        P(),
        P(),
        P(),
        P("dp", "seq", None),
    )
    out_specs = (
        P("dp", "seq", None),
        P("dp", "seq", None),
        P("seq", None),
        P("seq", None),
        P("seq", None),
        P(None, "seq"),
        P(None, "seq"),
        P("seq", None),
        P("seq"),
        P("seq"),
        P("seq"),
        P("seq"),
        P("seq"),
        P("seq"),
    )
    return jax.shard_map(
        functools.partial(on_device, Cube if cube else Plain),
        mesh=mesh,
        in_specs=in_specs,
        out_specs=out_specs,
        check_vma=False,
    )
```

```python
import functools

import jax
import jax.numpy as jnp
from jax import lax
from jax.experimental import pallas as pl
from jax.experimental.pallas import tpu as pltpu
from jax.sharding import PartitionSpec as P

HEADS = 4
HEAD = 256
BLOCK = 256
LANES = 128
FEED_VMEM = 12 << 20

norm_eps = 1e-06
rope_base = 1000000.0
score_scale = HEAD**-0.5
bf16 = jnp.bfloat16
f32 = jnp.float32
BRIEF = pl.CostEstimate(flops=1, bytes_accessed=1, transcendentals=0)


def rms_forward(values):
    factor = lax.rsqrt(jnp.mean(values * values, axis=-1, keepdims=True) + norm_eps)
    return (values * factor, factor)


def rms_backward(upstream, normed, factor):
    return factor * (upstream - normed * jnp.mean(upstream * normed, axis=-1, keepdims=True))


def rope_angles(positions, width):
    half_width = width // 2
    inverse_freq = rope_base ** (-(jnp.arange(half_width).astype(f32) * 2.0 / width))
    return positions.astype(f32)[:, None] * inverse_freq[None, :]


def rotate(values, cosine, sine):
    half_width = values.shape[-1] // 2
    first = values[..., :half_width]
    second = values[..., half_width:]
    return jnp.concatenate(
        [first * cosine - second * sine, second * cosine + first * sine], axis=-1
    )


def dot(left, right):
    return jnp.dot(left, right, preferred_element_type=f32)


def dot_rows(left, right):
    return lax.dot_general(left, right, (((1,), (1,)), ((), ())), preferred_element_type=f32)


def dot_cols(left, right):
    return lax.dot_general(left, right, (((0,), (0,)), ((), ())), preferred_element_type=f32)


def visible_mask(block_id, first_row, pos_ref):
    shape = (BLOCK, BLOCK)
    query = first_row + lax.broadcasted_iota(jnp.int32, shape, 0)
    key = block_id * BLOCK + lax.broadcasted_iota(jnp.int32, shape, 1)
    return (key <= query) & (key >= query - pos_ref[:, :1])


def head_rows(h):
    return pl.ds(h * BLOCK, BLOCK)


def put_queries(q_ref, q_pre_ref, gain_ref, cosine, sine):
    for h in range(HEADS):
        normed, _ = rms_forward(q_pre_ref[:, pl.ds(h * HEAD, HEAD)])
        q_ref[head_rows(h), :] = rotate(normed * gain_ref[...], cosine, sine).astype(bf16)


def column_blocks(columns, order_ref):
    if columns == 1:
        for h in range(HEADS):
            yield pl.ds(h * HEAD, HEAD), head_rows(h), pl.ds(0, HEAD)
        return
    slot, size = order_ref.shape[0] - columns, HEADS * HEAD // columns
    for k in range(columns):
        at = order_ref[slot + k] * size
        rows = pl.ds(pl.multiple_of(at // HEAD * BLOCK, BLOCK), BLOCK)
        yield pl.ds(k * size, size), rows, pl.ds(pl.multiple_of(at % HEAD, size), size)


def attend_kernel(
    n_blocks,
    columns,
    order_ref,
    q_pre_ref,
    cos_ref,
    sin_ref,
    gain_ref,
    pos_ref,
    *refs,
):
    kv_refs = refs[:-7]
    att_low_ref, inv_ref, q_ref, att_ref, total_ref, score_ref, weight_ref = refs[-7:]
    first_row = order_ref[n_blocks]
    first_key = order_ref[n_blocks + 1]
    put_queries(q_ref, q_pre_ref, gain_ref, cos_ref[...], sin_ref[...])
    att_ref[...] = jnp.zeros_like(att_ref)
    total_ref[...] = jnp.zeros_like(total_ref)

    def step(kv_ref, base, k, _):
        block_id = order_ref[base + k]
        live = (block_id * BLOCK <= first_row) & ((block_id + 1) * BLOCK > first_key)

        @pl.when(live)
        def _():
            rows = pl.ds(pl.multiple_of(k * BLOCK, BLOCK), BLOCK)
            visible = visible_mask(block_id, first_row, pos_ref)
            score_ref[...] = dot_rows(q_ref[...], kv_ref[rows, :HEAD])
            for h in range(HEADS):
                at = head_rows(h)
                weight = jnp.where(visible, jnp.exp(score_ref[at, :] * score_scale), 0.0)
                total_ref[at, :] += weight[:, :LANES] + weight[:, LANES:]
                weight_ref[at, :] = weight.astype(bf16)
            att_ref[...] += dot(weight_ref[...], kv_ref[rows, HEAD:])

        return 0

    each = n_blocks // len(kv_refs)
    for i, kv_ref in enumerate(kv_refs):
        lax.fori_loop(0, each, functools.partial(step, kv_ref, i * each), 0)
    for h in range(HEADS):
        at = head_rows(h)
        inverse = 1.0 / jnp.sum(total_ref[at, :], axis=-1, keepdims=True)
        inv_ref[:, pl.ds(h, 1)] = inverse
        att_ref[at, :] = att_ref[at, :] * inverse
    for stored, rows, lanes in column_blocks(columns, order_ref):
        att_low_ref[:, stored] = att_ref[rows, lanes].astype(bf16)


def attend(columns, order, q_pre, cosine, sine, gain, pos, *kv):
    rows = q_pre.shape[0]
    n_blocks = sum(v.shape[0] for v in kv) // BLOCK
    whole = pl.BlockSpec(memory_space=pltpu.VMEM)
    return pl.pallas_call(
        functools.partial(attend_kernel, n_blocks, columns),
        out_shape=(
            jax.ShapeDtypeStruct((rows, HEADS * HEAD), bf16),
            jax.ShapeDtypeStruct((rows, LANES), f32),
        ),
        in_specs=[pl.BlockSpec(memory_space=pltpu.SMEM)] + [whole] * (5 + len(kv)),
        out_specs=(whole,) * 2,
        scratch_shapes=[
            pltpu.VMEM((HEADS * rows, HEAD), bf16),
            pltpu.VMEM((HEADS * rows, HEAD), f32),
            pltpu.VMEM((HEADS * rows, LANES), f32),
            pltpu.VMEM((HEADS * rows, HEAD), f32),
            pltpu.VMEM((HEADS * rows, HEAD), bf16),
        ],
        cost_estimate=BRIEF,
        compiler_params=pltpu.CompilerParams(vmem_limit_bytes=10 << 20),
        name="attend",
    )(order, q_pre, cosine, sine, gain, pos, *kv)


def attend_back_kernel(
    n_blocks,
    columns,
    order_ref,
    q_pre_ref,
    cos_ref,
    sin_ref,
    gain_ref,
    pos_ref,
    att_ref,
    inv_ref,
    d_moved_ref,
    *refs,
):
    groups = (len(refs) - 10) // 2
    kv_refs, d_q_pre_ref, d_kv_refs = refs[:groups], refs[groups], refs[groups + 1 : -9]
    d_gain_ref, d_q_ref, row_dot_ref, d_att_ref, q_ref = refs[-9:-4]
    score_ref, d_prob_ref, prob_ref, d_score_ref = refs[-4:]
    cosine, sine = cos_ref[...], sin_ref[...]
    put_queries(q_ref, q_pre_ref, gain_ref, cosine, sine)
    row_dot_ref[...] = jnp.zeros_like(row_dot_ref)
    for stored, rows, lanes in column_blocks(columns, order_ref):
        moved = d_moved_ref[:, stored]
        d_att_ref[rows, lanes] = moved
        product = moved.astype(f32) * att_ref[:, stored].astype(f32)
        for i in range(product.shape[1] // LANES):
            row_dot_ref[rows, :] += product[:, i * LANES : (i + 1) * LANES]
    for h in range(HEADS):
        at = head_rows(h)
        total = jnp.sum(row_dot_ref[at, :], axis=-1, keepdims=True)
        row_dot_ref[at, pl.ds(0, 1)] = total
    first_row = order_ref[n_blocks]
    first_key = order_ref[n_blocks + 1]
    d_q_ref[...] = jnp.zeros_like(d_q_ref)

    def step(kv_ref, d_kv_ref, base, k, _):
        block_id = order_ref[base + k]
        live = (block_id * BLOCK <= first_row) & ((block_id + 1) * BLOCK > first_key)
        rows = pl.ds(pl.multiple_of(k * BLOCK, BLOCK), BLOCK)

        @pl.when(live)
        def _():
            keys = kv_ref[rows, :HEAD]
            visible = visible_mask(block_id, first_row, pos_ref)
            score_ref[...] = dot_rows(q_ref[...], keys)
            d_prob_ref[...] = dot_rows(d_att_ref[...], kv_ref[rows, HEAD:])
            for h in range(HEADS):
                at = head_rows(h)
                weight = jnp.where(visible, jnp.exp(score_ref[at, :] * score_scale), 0.0)
                prob = weight * inv_ref[:, pl.ds(h, 1)]
                prob_ref[at, :] = prob.astype(bf16)
                d_score = prob * (d_prob_ref[at, :] - row_dot_ref[at, pl.ds(0, 1)])
                d_score_ref[at, :] = d_score.astype(bf16)
            d_q_ref[...] += dot(d_score_ref[...], keys)
            d_keys = dot_cols(d_score_ref[...], q_ref[...])
            d_kv_ref[rows, :HEAD] = (d_keys * score_scale).astype(bf16)
            d_kv_ref[rows, HEAD:] = dot_cols(prob_ref[...], d_att_ref[...]).astype(bf16)

        @pl.when(jnp.logical_not(live))
        def _():
            d_kv_ref[rows, :] = jnp.zeros((BLOCK, 2 * HEAD), bf16)

        return 0

    each = n_blocks // groups
    for i in range(groups):
        walk = functools.partial(step, kv_refs[i], d_kv_refs[i], i * each)
        lax.fori_loop(0, each, walk, 0)
    d_gain = jnp.zeros((1, HEAD), f32)
    for h in range(HEADS):
        cols = pl.ds(h * HEAD, HEAD)
        normed, factor = rms_forward(q_pre_ref[:, cols])
        d_normed = rotate(d_q_ref[head_rows(h), :] * score_scale, cosine, -sine)
        d_gain += jnp.sum(d_normed * normed, axis=0, keepdims=True)
        d_q_pre_ref[:, cols] = rms_backward(d_normed * gain_ref[...], normed, factor).astype(bf16)
    d_gain_ref[...] = d_gain


def attend_back(columns, order, q_pre, cosine, sine, gain, pos, *kv, saved, d_att):
    rows = q_pre.shape[0]
    n_blocks = sum(v.shape[0] for v in kv) // BLOCK
    whole = pl.BlockSpec(memory_space=pltpu.VMEM)
    return pl.pallas_call(
        functools.partial(attend_back_kernel, n_blocks, columns),
        out_shape=(
            jax.ShapeDtypeStruct((rows, HEADS * HEAD), bf16),
            *[jax.ShapeDtypeStruct(v.shape, bf16) for v in kv],
            jax.ShapeDtypeStruct((1, HEAD), f32),
        ),
        in_specs=[pl.BlockSpec(memory_space=pltpu.SMEM)] + [whole] * (8 + len(kv)),
        out_specs=(whole,) * (2 + len(kv)),
        scratch_shapes=[
            pltpu.VMEM((HEADS * rows, HEAD), f32),
            pltpu.VMEM((HEADS * rows, LANES), f32),
            pltpu.VMEM((HEADS * rows, HEAD), bf16),
            pltpu.VMEM((HEADS * rows, HEAD), bf16),
            pltpu.VMEM((HEADS * rows, HEAD), f32),
            pltpu.VMEM((HEADS * rows, HEAD), f32),
            pltpu.VMEM((HEADS * rows, HEAD), bf16),
            pltpu.VMEM((HEADS * rows, HEAD), bf16),
        ],
        cost_estimate=BRIEF,
        compiler_params=pltpu.CompilerParams(vmem_limit_bytes=16 << 20),
        name="attend_back",
    )(order, q_pre, cosine, sine, gain, pos, *saved, d_att, *kv)


def gelu_parts(gate):
    c = (2.0 / jnp.pi) ** 0.5
    square = gate * gate
    t = jnp.tanh(gate * (c + (c * 0.044715) * square))
    half = 0.5 + 0.5 * t
    act = gate * half
    slope = half + act * (1.0 - t) * (c + (3 * c * 0.044715) * square)
    return act, slope


def put_halves(part, refs):
    half = part.shape[0] // 2
    refs[0][...] = part[:half].astype(refs[0].dtype)
    refs[1][...] = part[half:].astype(refs[1].dtype)


def feed_kernel(groups, pieces, *refs):
    weights, halves, (hidden_ref, act_ref, slope_ref) = refs[pieces:-5], refs[-5:-3], refs[-3:]
    b = jnp.concatenate([r[...] for r in refs[:pieces]], axis=0)
    part = 0.0
    for i in range(groups):
        gate_ref, up_ref, down_ref = weights[3 * i : 3 * i + 3]
        gate = dot_rows(b, gate_ref[...])
        up = dot_rows(b, up_ref[...])
        act, slope = gelu_parts(gate)
        hidden_ref[i] = (act * up).astype(bf16)
        act_ref[i] = act.astype(bf16)
        slope_ref[i] = (up * slope).astype(bf16)
        part = part + dot(hidden_ref[i], down_ref[...])
    put_halves(part, halves)


def feed(b, weights, dtype):
    rows, width = sum(v.shape[0] for v in b), b[0].shape[1]
    groups, ff = len(weights) // 3, weights[0].shape[0]
    whole = pl.BlockSpec(memory_space=pltpu.VMEM)
    return pl.pallas_call(
        functools.partial(feed_kernel, groups, len(b)),
        out_shape=(
            *[jax.ShapeDtypeStruct((rows // 2, width), dtype)] * 2,
            *[jax.ShapeDtypeStruct((groups, rows, ff), bf16)] * 3,
        ),
        in_specs=[whole] * (len(b) + len(weights)),
        out_specs=(whole,) * 5,
        cost_estimate=BRIEF,
        compiler_params=pltpu.CompilerParams(vmem_limit_bytes=FEED_VMEM),
        name="feed",
    )(*b, *weights)


def feed_back_kernel(groups, pieces, act_ref, slope_ref, *refs):
    weights, halves, (d_gate_ref, d_up_ref) = refs[pieces:-4], refs[-4:-2], refs[-2:]
    d = jnp.concatenate([r[...] for r in refs[:pieces]], axis=0)
    part = 0.0
    for i in range(groups):
        gate_ref, up_ref, down_ref = weights[3 * i : 3 * i + 3]
        d_hidden = dot_rows(d, down_ref[...])
        d_gate_ref[i] = (d_hidden * slope_ref[i].astype(f32)).astype(bf16)
        d_up_ref[i] = (d_hidden * act_ref[i].astype(f32)).astype(bf16)
        part = part + dot(d_gate_ref[i], gate_ref[...]) + dot(d_up_ref[i], up_ref[...])
    put_halves(part, halves)


def feed_back(d, act, slope, weights, dtype):
    rows, width = sum(v.shape[0] for v in d), d[0].shape[1]
    groups, ff = len(weights) // 3, weights[0].shape[0]
    whole = pl.BlockSpec(memory_space=pltpu.VMEM)
    return pl.pallas_call(
        functools.partial(feed_back_kernel, groups, len(d)),
        out_shape=(
            *[jax.ShapeDtypeStruct((rows // 2, width), dtype)] * 2,
            *[jax.ShapeDtypeStruct((groups, rows, ff), bf16)] * 2,
        ),
        in_specs=[whole] * (2 + len(d) + len(weights)),
        out_specs=(whole,) * 4,
        cost_estimate=BRIEF,
        compiler_params=pltpu.CompilerParams(vmem_limit_bytes=FEED_VMEM),
        name="feed_back",
    )(act, slope, *d, *weights)


def weight_grad_kernel(index, sizes, count, pieces, *refs):
    lefts, rights, rest = refs[:count], refs[count : count + pieces], refs[count + pieces :]
    extra, outs = rest[: -len(sizes)], rest[-len(sizes) :]
    left = jnp.concatenate([v[index] for v in lefts], axis=0)
    right = jnp.concatenate([v[...] for v in rights], axis=0)
    total = dot_cols(left, right)
    if extra:
        total = total + extra[0][...].astype(f32)
    begin = 0
    for size, out in zip(sizes, outs):
        out[...] = total[begin : begin + size].astype(bf16)
        begin += size


def weight_grad(index, sizes, lefts, rights, *extra):
    rights = [piece for part in rights for piece in part]
    width = rights[0].shape[1]
    whole = pl.BlockSpec(memory_space=pltpu.VMEM)
    return pl.pallas_call(
        functools.partial(weight_grad_kernel, index, sizes, len(lefts), len(rights)),
        out_shape=tuple(jax.ShapeDtypeStruct((size, width), bf16) for size in sizes),
        in_specs=[whole] * (len(lefts) + len(rights) + len(extra)),
        out_specs=(whole,) * len(sizes),
        cost_estimate=BRIEF,
        compiler_params=pltpu.CompilerParams(vmem_limit_bytes=FEED_VMEM),
        name="weight_grad",
    )(*lefts, *rights, *extra)


def middle_back_kernel(counts, out_count, *refs):
    terms, refs = refs[: sum(counts)], refs[sum(counts) :]
    g_ref, middle_ref, attn_ref, pre_ref, post_ref = refs[:5]
    outs, (d_middle_ref, d_attn_ref, d_att_ref, gain_ref) = refs[5 : 5 + out_count], refs[-4:]
    pre, post = 0.0, 0.0
    half = g_ref.shape[0] // 2
    for i in range(2):
        own = terms[: counts[0]] if i == 0 else terms[counts[0] :]
        rows = pl.ds(i * half, half)
        d_b = functools.reduce(jnp.add, [t[...].astype(f32) for t in own])
        normed, factor = rms_forward(middle_ref[rows, :])
        pre = pre + jnp.sum(d_b * normed, axis=0, keepdims=True)
        d_middle = g_ref[rows, :] + rms_backward(d_b * pre_ref[...], normed, factor)
        d_middle_ref[rows, :] = d_middle
        normed, factor = rms_forward(attn_ref[rows, :])
        post = post + jnp.sum(d_middle * normed, axis=0, keepdims=True)
        d_attn = rms_backward(d_middle * post_ref[...], normed, factor).astype(bf16)
        d_attn_ref[rows, :] = d_attn
    at = 0
    for out in outs:
        d_att_ref[:, at : at + out.shape[0]] = dot_rows(d_attn_ref[...], out[...]).astype(bf16)
        at += out.shape[0]
    gain_ref[0:1, :] = pre
    gain_ref[1:2, :] = post


def middle_back(halves, g, middle, attn, g_pre, g_post, outs):
    rows, width = g.shape
    whole = pl.BlockSpec(memory_space=pltpu.VMEM)
    return pl.pallas_call(
        functools.partial(middle_back_kernel, [len(h) for h in halves], len(outs)),
        out_shape=(
            jax.ShapeDtypeStruct((rows, width), f32),
            jax.ShapeDtypeStruct((rows, width), bf16),
            jax.ShapeDtypeStruct((rows, HEADS * HEAD), bf16),
            jax.ShapeDtypeStruct((2, width), f32),
        ),
        in_specs=[whole] * (sum(len(h) for h in halves) + 5 + len(outs)),
        out_specs=(whole,) * 4,
        cost_estimate=BRIEF,
        compiler_params=pltpu.CompilerParams(vmem_limit_bytes=FEED_VMEM),
        name="middle_back",
    )(*halves[0], *halves[1], g, middle, attn, g_pre[None], g_post[None], *outs)


def add(*terms):
    return functools.reduce(jnp.add, [t.astype(f32) for t in terms])


fence = lax.optimization_barrier


class Plain:
    def __init__(self, n, rank, place):
        self.n, self.rank, self.place = n, rank, place

    def order(self):
        return jnp.arange(self.n, dtype=jnp.int32)

    def slots(self):
        return jnp.zeros(1, jnp.int32)

    def send(self, shard):
        return [shard]

    def paired(self, shards):
        return [lax.all_gather(shards[0], "seq", axis=0, tiled=True)]

    def joined(self, shard, near, far):
        return self.paired([shard])

    def columns(self, value):
        return [value]

    def ordered(self, blocks):
        return blocks[0]

    def pair(self, shard):
        return [shard]

    def near(self, shard):
        return ()

    def far(self, near):
        return ()

    def tokens(self, shard, near, far):
        whole = lax.all_gather(shard, "seq", axis=0, tiled=True)
        return [(part,) for part in jnp.split(whole, self.n, axis=0)]

    def early(self, x, y):
        return ()

    def relay(self, far):
        return ()

    def late(self, x, y, relay):
        return ()

    def halves(self, parts, early, late):
        whole = self.scatter(all_of([half.astype(bf16) for part in parts for half in part]))
        return [[half] for half in jnp.split(whole, 2, axis=0)]

    def across(self, value):
        return ()

    def group(self, partial, moved):
        return (partial[0],)

    def group_near(self, group):
        return ()

    def group_far(self, group):
        return ()

    def group_sum(self, group, near, far):
        return self.scatter(group[0])

    def scatter(self, partial):
        return lax.psum_scatter(
            partial.astype(bf16), "seq", scatter_dimension=0, tiled=True
        ).astype(f32)

    def projection(self, left, right, gains):
        grad = dot_cols(left, right).reshape(self.n, -1, right.shape[1])
        gains = jnp.broadcast_to(gains[None], (self.n, *gains.shape))
        return [jnp.concatenate([grad, gains], axis=1).reshape(-1, right.shape[1])]

    def line(self):
        return PlainLine(None)


class Cube(Plain):
    chips = (0, 2, 4, 6)
    ranks = (0, 2, 4, 6, 1, 3, 5, 7)

    def hop(self, value, bit):
        return lax.ppermute(value, "seq", [(i, i ^ bit) for i in range(8)])

    def order(self):
        return self.rank ^ jnp.array(self.ranks, dtype=jnp.int32)

    def slots(self):
        return self.order()

    def send(self, shard):
        return [shard] + [self.hop(shard, bit) for bit in self.chips[1:]]

    def joined(self, shard, near, far):
        return self.paired([shard, *near, *far])

    def paired(self, shards):
        group = all_of(shards)
        return [group, self.hop(group, 1)]

    def near(self, shard):
        return (self.hop(shard, 2), self.hop(shard, 4))

    def far(self, near):
        half = near[0].shape[0] // 2
        return (self.hop(near[1][:half], 2), self.hop(near[0][half:], 4))

    def tokens(self, shard, near, far):
        return [(shard,), *[(v,) for v in near], tuple(far)]

    def early(self, x, y):
        return (self.hop(x[0], 2), self.hop(y[1], 4))

    def relay(self, far):
        return (self.hop(far[0], 2), self.hop(far[1], 4))

    def late(self, x, y, relay):
        return (
            self.hop(add(x[1], relay[1]).astype(bf16), 2),
            self.hop(add(y[0], relay[0]).astype(bf16), 4),
        )

    def halves(self, parts, early, late):
        own = parts[0]
        return [[own[0], early[0], late[1]], [own[1], early[1], late[0]]]

    def across(self, value):
        return (self.hop(value, 1),)

    def group(self, partial, moved):
        parts = jnp.split(add(partial[0], *moved), 4, axis=0)
        return (parts[0], *[p.astype(bf16) for p in parts[1:]])

    def group_near(self, group):
        return (self.hop(group[1], 2), self.hop(group[2], 4))

    def group_far(self, group):
        return (self.hop(group[3], 6),)

    def group_sum(self, group, near, far):
        return add(group[0], *near, *far)

    def select(self, size, stride):
        shape = (self.n * size, self.n * stride)
        col = lax.broadcasted_iota(jnp.int32, shape, 1)
        block, at = col // stride, col % stride
        source = self.rank ^ ((2 * block) % 8 + block // 4)
        row = lax.broadcasted_iota(jnp.int32, shape, 0)
        return ((row == source * size + at) & (at < size)).astype(bf16)

    def columns(self, value):
        moved = dot(value, self.select(value.shape[1] // self.n, value.shape[1] // self.n))
        return jnp.split(moved.astype(value.dtype), 2, axis=1)

    def ordered(self, blocks):
        whole = all_of(blocks)
        size = whole.shape[0] // self.n
        return dot(self.select(size, size), whole).astype(whole.dtype)

    def pair(self, shard):
        return [shard, self.hop(shard, 1)]

    def projection(self, left, right, gains):
        size, extra = left.shape[1] // self.n, gains.shape[0]
        stride = size + extra
        moved = dot(left, self.select(size, stride)).astype(bf16)
        shape = (extra, self.n * stride)
        at = lax.broadcasted_iota(jnp.int32, shape, 1) % stride
        pick = (at == size + lax.broadcasted_iota(jnp.int32, shape, 0)).astype(bf16)
        left = jnp.concatenate([moved, pick], axis=0)
        right = jnp.concatenate([right, gains.astype(bf16)], axis=0)
        half = self.n * stride // 2
        return [dot_cols(left[:, :half], right), dot_cols(left[:, half:], right)]

    def line(self):
        return CubeLine((self.place == 1) | (self.place == 2))


class PlainLine:
    def __init__(self, inner):
        self.inner = inner
        self.chunks, self.wholes = [], []

    def add_rows(self, whole, parts):
        size = whole.shape[0] // parts
        self.wholes.append(whole)
        self.chunks += [(len(self.wholes) - 1, i * size, size) for i in range(parts)]

    def chunk(self, at):
        if len(self.chunks[at]) == 1:
            return self.chunks[at][0]
        source, start, size = self.chunks[at]
        return self.wholes[source][start : start + size]

    def step(self, beside):
        return fence(beside(()))

    def finish(self, early):
        chunks = [self.chunk(i) for i in range(len(self.chunks))]
        done = [lax.psum(c, "dp").astype(f32) for c in chunks]
        return done, early(done[-2])


class CubeLine(PlainLine):
    def __init__(self, inner):
        super().__init__(inner)
        self.halves, self.totals, self.out = {}, {}, {}
        self.at = 0

    def step(self, beside):
        tick = self.at
        self.at += 1
        mine = self.chunk(tick) if tick < len(self.chunks) else None
        back, half = self.totals.get(tick - 2), self.halves.get(tick - 1)
        got = {}
        if mine is not None and back is not None and mine.shape == back.shape:
            both = jnp.where(self.inner, back, mine)
            got["in"] = lax.ppermute(both, "dp", [(0, 1), (1, 0), (2, 3), (3, 2)])
        else:
            if back is not None:
                got["out"] = lax.ppermute(back, "dp", [(1, 0), (2, 3)])
            if mine is not None:
                got["in"] = lax.ppermute(mine, "dp", [(0, 1), (3, 2)])
        if half is not None:
            got["middle"] = lax.ppermute(half, "dp", [(1, 2), (2, 1)])
        values = beside(())
        later = [c for c in self.chunks[tick + 1 :] if len(c) == 1]
        got, values, later, self.wholes = fence((got, values, later, self.wholes))
        for at in range(tick + 1, len(self.chunks)):
            if len(self.chunks[at]) == 1:
                self.chunks[at] = later.pop(0)
        if mine is not None:
            self.halves[tick] = add(mine, got["in"]).astype(bf16)
        if half is not None:
            self.totals[tick - 1] = add(half, got["middle"]).astype(bf16)
        if back is not None:
            self.out[tick - 2] = jnp.where(self.inner, back, got["out"] if "out" in got else got["in"])
        return values

    def finish(self, early):
        count = len(self.chunks)
        while self.at < count + 1:
            self.step(lambda values: values)
        made = self.step(lambda _: early(self.out[count - 2].astype(f32)))
        return [self.out[i].astype(f32) for i in range(count)], made


def all_of(values):
    return jnp.concatenate(values, axis=0)


def on_device(
    kind,
    layer_input,
    segment_ids,
    position_ids,
    w_query,
    w_keyval,
    w_out,
    w_gate,
    w_up,
    w_down,
    g_input,
    g_post_attn,
    g_pre_ffn,
    g_post_ffn,
    g_query,
    g_key,
    out_grad,
):
    n = lax.axis_size("seq")
    comm = kind(n, lax.axis_index("seq"), lax.axis_index("dp"))
    rows = layer_input.shape[1]
    width = layer_input.shape[2]
    ff = w_gate.shape[1]
    positions = position_ids[0]
    row_offset = comm.rank * rows
    order = jnp.concatenate(
        [comm.order(), row_offset[None], (row_offset - positions[0])[None], comm.slots()]
    ).astype(jnp.int32)
    shard = width // n
    starts = (comm.rank * shard, comm.rank * (HEAD // n), HEAD + comm.rank * (HEAD // n))
    line = comm.line()
    position_column = positions[:, None] + jnp.zeros((1, LANES), jnp.int32)

    x = layer_input[0].astype(f32)
    near = comm.near(w_keyval), comm.near(w_query)
    a_normed, a_factor = rms_forward(x)
    a_low = (a_normed * g_input).astype(bf16)
    a_columns = comm.columns(a_low)
    angles = rope_angles(positions, HEAD)
    cosine, sine = jnp.cos(angles), jnp.sin(angles)
    near, a_columns, order, starts, position_column, line.inner, comm.rank = fence(
        (near, a_columns, order, starts, position_column, line.inner, comm.rank)
    )
    far = [comm.far(v) for v in near]
    far, w_out = fence((far, w_out))
    out_near = comm.near(w_out)
    keyval_blocks = comm.joined(w_keyval, near[0], far[0])
    query_blocks = comm.joined(w_query, near[1], far[1])
    kv_pre = add(*[dot(a, w) for a, w in zip(a_columns, keyval_blocks)])
    k_hat, k_factor = rms_forward(kv_pre[:, :HEAD])
    k_low = rotate(k_hat * g_key, cosine, sine).astype(bf16)
    kv_low = jnp.concatenate([k_low, kv_pre[:, HEAD:].astype(bf16)], axis=1)
    kv_low, keyval_blocks, query_blocks = fence((kv_low, keyval_blocks, query_blocks))
    kv_near = comm.near(kv_low)
    q_pre = add(*[dot(a, w) for a, w in zip(a_columns, query_blocks)])
    kv_near, out_near, q_pre = fence((kv_near, out_near, q_pre))
    kv_far = comm.far(kv_near)
    kv_far, out_near = fence((kv_far, out_near))
    kv_blocks = comm.joined(kv_low, kv_near, kv_far)
    out_far = comm.far(out_near)
    kv_blocks, out_far, w_gate, w_up, w_down, query_blocks, keyval_blocks = fence(
        (kv_blocks, out_far, w_gate, w_up, w_down, query_blocks, keyval_blocks)
    )
    out_blocks = comm.joined(w_out, out_near, out_far)
    head_args = (
        comm.slots().shape[0],
        order,
        q_pre,
        cosine,
        sine,
        g_query[None],
        position_column,
        *kv_blocks,
    )
    att_low, inverse = attend(*head_args)
    out_blocks, att_low, w_gate, w_up, w_down = fence((out_blocks, att_low, w_gate, w_up, w_down))
    gate_w, up_w, down_w = [comm.pair(w) for w in (w_gate.T, w_up.T, w_down)]
    groups = len(gate_w)
    att_columns = jnp.split(att_low, len(out_blocks), axis=1)
    attn = add(*[dot(v, w) for v, w in zip(att_columns, out_blocks)])
    attn_normed, attn_factor = rms_forward(attn)
    middle = x + attn_normed * g_post_attn
    b_normed, b_factor = rms_forward(middle)
    b_low = (b_normed * g_pre_ffn).astype(bf16)
    b_low, query_blocks, keyval_blocks = fence((b_low, query_blocks, keyval_blocks))
    weights = [w[i] for i in range(groups) for w in (gate_w, up_w, down_w)]

    near = comm.near(b_low)
    kept = [feed((b_low,), weights, f32)]
    query_whole = comm.ordered(query_blocks)
    kept, near, query_whole, keyval_blocks = fence((kept, near, query_whole, keyval_blocks))
    far = comm.far(near)
    b_list = comm.tokens(b_low, near, far)
    kept += [feed(part, weights, bf16) for part in b_list[1:-1]]
    kept, far, tail = fence((kept, far, b_list[-1]))
    b_list[-1] = tail
    early = comm.early(kept[1][:2], kept[2][:2])
    kept.append(feed(tail, weights, bf16))
    kept, early = fence((kept, early))
    parts = [v[:2] for v in kept]
    hidden, acts, slopes = [[v[i] for v in kept] for i in (2, 3, 4)]
    relay = comm.relay(parts[-1])
    late = comm.late(parts[1], parts[2], relay)
    ffn = all_of([add(*terms) for terms in comm.halves(parts, early, late)])
    ffn_normed, ffn_factor = rms_forward(ffn)
    layer_out = (middle + ffn_normed * g_post_ffn).astype(bf16)

    g = out_grad[0]
    d_ffn = rms_backward(g * g_post_ffn, ffn_normed, ffn_factor).astype(bf16)
    d_ffn, ffn_normed, keyval_blocks = fence((d_ffn, ffn_normed, keyval_blocks))

    def back(part, i):
        return feed_back(part, acts[i], slopes[i], weights, bf16 if i else f32)

    def other_half(lefts, rights):
        return weight_grad(1, [ff], lefts, rights) if groups > 1 else ()

    near = comm.near(d_ffn)
    gain_post_ffn = jnp.sum(g * ffn_normed, axis=0)
    kept = [back((d_ffn,), 0)]
    keyval_whole = comm.ordered(keyval_blocks)
    kept, near, gain_post_ffn, keyval_whole = fence((kept, near, gain_post_ffn, keyval_whole))
    far = comm.far(near)
    d_list = comm.tokens(d_ffn, near, far)
    last = len(d_list) - 1
    kept += [back(d_list[i], i) for i in range(1, last)]
    kept, far, tail = fence((kept, far, d_list[-1]))
    d_list[-1] = tail

    other = [comm.hop(v, 1) for v in other_half(hidden, d_list)]
    kept.append(back(tail, last))
    kept, other = fence((kept, other))
    parts = [v[:2] for v in kept]
    d_gate, d_up = [[v[i] for v in kept] for i in (2, 3)]
    thirds = [ff // 3] * 3
    line.chunks += [(v,) for v in weight_grad(0, thirds, hidden, d_list, *other)]

    line.chunks, parts, d_gate, d_up, a_late = fence((line.chunks, parts, d_gate, d_up, a_low))

    def beside(_):
        early = comm.early(parts[1], parts[2])
        relay = comm.relay(parts[-1])
        others = other_half(d_gate, b_list), other_half(d_up, b_list)
        return early, relay, others, d_gate, d_up, parts

    early, relay, others, d_gate, d_up, parts = line.step(beside)

    def beside(_):
        late = comm.late(parts[1], parts[2], relay)
        (grads,) = weight_grad(0, [ff], d_gate, b_list, *[comm.hop(v, 1) for v in others[0]])
        late, grads = fence((late, grads))
        middles = middle_back(
            comm.halves(parts, early, late), g, middle, attn, g_pre_ffn, g_post_attn, out_blocks
        )
        return grads, d_up, others[1], middles

    grads, d_up, other_up, (d_middle, d_attn, d_att, gain_pair) = line.step(beside)
    line.add_rows(grads, 3)

    def beside(_):
        heads = attend_back(*head_args, saved=(att_low, inverse), d_att=d_att)
        grad_out = [dot_cols(v, d_attn) for v in att_columns]
        return heads, d_up, grad_out, [comm.hop(v, 1) for v in other_up]

    heads, d_up, grad_out, other_up = line.step(beside)
    d_q_pre, *d_kv_blocks, gain_query = heads

    def beside(_):
        group = comm.group(d_kv_blocks, comm.across(d_kv_blocks[-1]))
        near = comm.group_near(group)
        (grads,) = weight_grad(0, [ff], d_up, b_list, *other_up)
        return group, near, grads, grad_out, a_late, (gain_post_ffn, gain_pair, gain_query)

    group, near, grads, grad_out, a_late, early_gains = line.step(beside)
    line.add_rows(grads, 3)

    def beside(_):
        d_kv = comm.group_sum(group, near, comm.group_far(group))
        d_k_normed = rotate(d_kv[:, :HEAD], cosine, -sine)
        gain_key = jnp.sum(d_k_normed * k_hat, axis=0)
        d_k_pre = rms_backward(d_k_normed * g_key, k_hat, k_factor)
        d_kv_pre = jnp.concatenate([d_k_pre, d_kv[:, HEAD:]], axis=1).astype(bf16)
        d_a = dot_rows(d_q_pre, query_whole) + dot_rows(d_kv_pre, keyval_whole)
        gain_input = jnp.sum(d_a * a_normed, axis=0)
        out_group = comm.group(grad_out, comm.across(grad_out[-1].astype(bf16)))
        return d_kv_pre, d_a, (gain_input, gain_key), out_group, a_late, early_gains

    d_kv_pre, d_a, (gain_input, gain_key), out_group, a_late, early_gains = line.step(beside)
    gain_post_ffn, gain_pair, gain_query = early_gains

    def beside(_):
        out_near = comm.group_near(out_group)
        d_qkv = jnp.concatenate([d_q_pre, d_kv_pre], axis=1)
        gains = [gain_input, gain_pair[1], gain_pair[0], gain_post_ffn]
        gains.append(jnp.concatenate([gain_query[0], gain_key]))
        gains = [jnp.pad(v, (0, d_qkv.shape[1] - v.shape[0])) for v in gains]
        row = lax.broadcasted_iota(jnp.int32, (16, d_qkv.shape[1]), 0)
        gains = add(*[jnp.where(row == i, v[None], 0.0) for i, v in enumerate(gains)])
        grad_qkv = comm.projection(a_late, d_qkv, gains)
        return out_group, out_near, grad_qkv, d_a

    out_group, out_near, grad_qkv, d_a = line.step(beside)

    def beside(_):
        qkv_moved = comm.across(grad_qkv[-1].astype(bf16))
        out_far = comm.group_far(out_group)
        d_input = d_middle + rms_backward(d_a * g_input, a_normed, a_factor)
        total_out = comm.group_sum(out_group, out_near, out_far).astype(bf16)
        return comm.group(grad_qkv, qkv_moved), total_out, d_input

    group, total_out, d_input = line.step(beside)

    def beside(_):
        return group, comm.group_near(group), total_out

    group, near, total_out = line.step(beside)

    def beside(_):
        return comm.group_far(group), near, total_out

    far, near, total_out = line.step(beside)
    line.chunks += [(comm.group_sum(group, near, far).astype(bf16),), (total_out,)]
    def owned(tail):
        def mine(row, start, size):
            return lax.dynamic_slice(
                tail[shard + row], (start,), (size,), allow_negative_indices=False
            )

        grads = [tail[:shard, : HEADS * HEAD], tail[:shard, HEADS * HEAD :]]
        names = [mine(i, starts[0], shard) for i in range(4)]
        return grads, names + [mine(4, start, HEAD // n) for start in starts[1:]]

    (*done, _, total_out), ((grad_query, grad_keyval), names) = line.finish(owned)
    down, gate, up = all_of(done[:3]), all_of(done[3:6]), all_of(done[6:])
    return (
        layer_out[None],
        d_input[None],
        grad_query,
        grad_keyval,
        total_out,
        gate.T,
        up.T,
        down,
        *names,
    )


def solution(mesh):
    cube = mesh.shape["seq"] == 8 and mesh.shape["dp"] == 4
    in_specs = (
        P("dp", "seq", None),
        P("dp", None),
        P("dp", "seq"),
        P("seq", None),
        P("seq", None),
        P("seq", None),
        P(None, "seq"),
        P(None, "seq"),
        P("seq", None),
        P(),
        P(),
        P(),
        P(),
        P(),
        P(),
        P("dp", "seq", None),
    )
    out_specs = (
        P("dp", "seq", None),
        P("dp", "seq", None),
        P("seq", None),
        P("seq", None),
        P("seq", None),
        P(None, "seq"),
        P(None, "seq"),
        P("seq", None),
        P("seq"),
        P("seq"),
        P("seq"),
        P("seq"),
        P("seq"),
        P("seq"),
    )
    return jax.shard_map(
        functools.partial(on_device, Cube if cube else Plain),
        mesh=mesh,
        in_specs=in_specs,
        out_specs=out_specs,
        check_vma=False,
    )
```

```python
import functools

import jax
import jax.numpy as jnp
from jax import lax
from jax.experimental import pallas as pl
from jax.experimental.pallas import tpu as pltpu
from jax.sharding import PartitionSpec as P

HEADS = 4
HEAD = 256
BLOCK = 256
LANES = 128
FEED_VMEM = 12 << 20

norm_eps = 1e-06
rope_base = 1000000.0
score_scale = HEAD**-0.5
bf16 = jnp.bfloat16
f32 = jnp.float32
BRIEF = pl.CostEstimate(flops=1, bytes_accessed=1, transcendentals=0)


def rms_forward(values):
    factor = lax.rsqrt(jnp.mean(values * values, axis=-1, keepdims=True) + norm_eps)
    return (values * factor, factor)


def rms_backward(upstream, normed, factor):
    return factor * (upstream - normed * jnp.mean(upstream * normed, axis=-1, keepdims=True))


def rope_angles(positions, width):
    half_width = width // 2
    inverse_freq = rope_base ** (-(jnp.arange(half_width).astype(f32) * 2.0 / width))
    return positions.astype(f32)[:, None] * inverse_freq[None, :]


def rotate(values, cosine, sine):
    half_width = values.shape[-1] // 2
    first = values[..., :half_width]
    second = values[..., half_width:]
    return jnp.concatenate(
        [first * cosine - second * sine, second * cosine + first * sine], axis=-1
    )


def dot(left, right):
    return jnp.dot(left, right, preferred_element_type=f32)


def dot_rows(left, right):
    return lax.dot_general(left, right, (((1,), (1,)), ((), ())), preferred_element_type=f32)


def dot_cols(left, right):
    return lax.dot_general(left, right, (((0,), (0,)), ((), ())), preferred_element_type=f32)


def visible_mask(block_id, first_row, pos_ref):
    shape = (BLOCK, BLOCK)
    query = first_row + lax.broadcasted_iota(jnp.int32, shape, 0)
    key = block_id * BLOCK + lax.broadcasted_iota(jnp.int32, shape, 1)
    return (key <= query) & (key >= query - pos_ref[:, :1])


def head_rows(h):
    return pl.ds(h * BLOCK, BLOCK)


def put_queries(q_ref, q_pre_ref, gain_ref, cosine, sine):
    for h in range(HEADS):
        normed, _ = rms_forward(q_pre_ref[:, pl.ds(h * HEAD, HEAD)])
        q_ref[head_rows(h), :] = rotate(normed * gain_ref[...], cosine, sine).astype(bf16)


def column_blocks(columns, order_ref):
    if columns == 1:
        for h in range(HEADS):
            yield pl.ds(h * HEAD, HEAD), head_rows(h), pl.ds(0, HEAD)
        return
    slot, size = order_ref.shape[0] - columns, HEADS * HEAD // columns
    for k in range(columns):
        at = order_ref[slot + k] * size
        rows = pl.ds(pl.multiple_of(at // HEAD * BLOCK, BLOCK), BLOCK)
        yield pl.ds(k * size, size), rows, pl.ds(pl.multiple_of(at % HEAD, size), size)


def attend_kernel(
    n_blocks,
    columns,
    order_ref,
    q_pre_ref,
    cos_ref,
    sin_ref,
    gain_ref,
    pos_ref,
    *refs,
):
    kv_refs = refs[:-7]
    att_low_ref, inv_ref, q_ref, att_ref, total_ref, score_ref, weight_ref = refs[-7:]
    first_row = order_ref[n_blocks]
    first_key = order_ref[n_blocks + 1]
    put_queries(q_ref, q_pre_ref, gain_ref, cos_ref[...], sin_ref[...])
    att_ref[...] = jnp.zeros_like(att_ref)
    total_ref[...] = jnp.zeros_like(total_ref)

    def step(kv_ref, base, k, _):
        block_id = order_ref[base + k]
        live = (block_id * BLOCK <= first_row) & ((block_id + 1) * BLOCK > first_key)

        @pl.when(live)
        def _():
            rows = pl.ds(pl.multiple_of(k * BLOCK, BLOCK), BLOCK)
            visible = visible_mask(block_id, first_row, pos_ref)
            score_ref[...] = dot_rows(q_ref[...], kv_ref[rows, :HEAD])
            for h in range(HEADS):
                at = head_rows(h)
                weight = jnp.where(visible, jnp.exp(score_ref[at, :] * score_scale), 0.0)
                total_ref[at, :] += weight[:, :LANES] + weight[:, LANES:]
                weight_ref[at, :] = weight.astype(bf16)
            att_ref[...] += dot(weight_ref[...], kv_ref[rows, HEAD:])

        return 0

    each = n_blocks // len(kv_refs)
    for i, kv_ref in enumerate(kv_refs):
        lax.fori_loop(0, each, functools.partial(step, kv_ref, i * each), 0)
    for h in range(HEADS):
        at = head_rows(h)
        inverse = 1.0 / jnp.sum(total_ref[at, :], axis=-1, keepdims=True)
        inv_ref[:, pl.ds(h, 1)] = inverse
        att_ref[at, :] = att_ref[at, :] * inverse
    for stored, rows, lanes in column_blocks(columns, order_ref):
        att_low_ref[:, stored] = att_ref[rows, lanes].astype(bf16)


def attend(columns, order, q_pre, cosine, sine, gain, pos, *kv):
    rows = q_pre.shape[0]
    n_blocks = sum(v.shape[0] for v in kv) // BLOCK
    whole = pl.BlockSpec(memory_space=pltpu.VMEM)
    return pl.pallas_call(
        functools.partial(attend_kernel, n_blocks, columns),
        out_shape=(
            jax.ShapeDtypeStruct((rows, HEADS * HEAD), bf16),
            jax.ShapeDtypeStruct((rows, LANES), f32),
        ),
        in_specs=[pl.BlockSpec(memory_space=pltpu.SMEM)] + [whole] * (5 + len(kv)),
        out_specs=(whole,) * 2,
        scratch_shapes=[
            pltpu.VMEM((HEADS * rows, HEAD), bf16),
            pltpu.VMEM((HEADS * rows, HEAD), f32),
            pltpu.VMEM((HEADS * rows, LANES), f32),
            pltpu.VMEM((HEADS * rows, HEAD), f32),
            pltpu.VMEM((HEADS * rows, HEAD), bf16),
        ],
        cost_estimate=BRIEF,
        compiler_params=pltpu.CompilerParams(vmem_limit_bytes=10 << 20),
        name="attend",
    )(order, q_pre, cosine, sine, gain, pos, *kv)


def attend_back_kernel(
    n_blocks,
    columns,
    order_ref,
    q_pre_ref,
    cos_ref,
    sin_ref,
    gain_ref,
    pos_ref,
    att_ref,
    inv_ref,
    d_moved_ref,
    *refs,
):
    groups = (len(refs) - 10) // 2
    kv_refs, d_q_pre_ref, d_kv_refs = refs[:groups], refs[groups], refs[groups + 1 : -9]
    d_gain_ref, d_q_ref, row_dot_ref, d_att_ref, q_ref = refs[-9:-4]
    score_ref, d_prob_ref, prob_ref, d_score_ref = refs[-4:]
    cosine, sine = cos_ref[...], sin_ref[...]
    put_queries(q_ref, q_pre_ref, gain_ref, cosine, sine)
    row_dot_ref[...] = jnp.zeros_like(row_dot_ref)
    for stored, rows, lanes in column_blocks(columns, order_ref):
        moved = d_moved_ref[:, stored]
        d_att_ref[rows, lanes] = moved
        product = moved.astype(f32) * att_ref[:, stored].astype(f32)
        for i in range(product.shape[1] // LANES):
            row_dot_ref[rows, :] += product[:, i * LANES : (i + 1) * LANES]
    for h in range(HEADS):
        at = head_rows(h)
        total = jnp.sum(row_dot_ref[at, :], axis=-1, keepdims=True)
        row_dot_ref[at, pl.ds(0, 1)] = total
    first_row = order_ref[n_blocks]
    first_key = order_ref[n_blocks + 1]
    d_q_ref[...] = jnp.zeros_like(d_q_ref)

    def step(kv_ref, d_kv_ref, base, k, _):
        block_id = order_ref[base + k]
        live = (block_id * BLOCK <= first_row) & ((block_id + 1) * BLOCK > first_key)
        rows = pl.ds(pl.multiple_of(k * BLOCK, BLOCK), BLOCK)

        @pl.when(live)
        def _():
            keys = kv_ref[rows, :HEAD]
            visible = visible_mask(block_id, first_row, pos_ref)
            score_ref[...] = dot_rows(q_ref[...], keys)
            d_prob_ref[...] = dot_rows(d_att_ref[...], kv_ref[rows, HEAD:])
            for h in range(HEADS):
                at = head_rows(h)
                weight = jnp.where(visible, jnp.exp(score_ref[at, :] * score_scale), 0.0)
                prob = weight * inv_ref[:, pl.ds(h, 1)]
                prob_ref[at, :] = prob.astype(bf16)
                d_score = prob * (d_prob_ref[at, :] - row_dot_ref[at, pl.ds(0, 1)])
                d_score_ref[at, :] = d_score.astype(bf16)
            d_q_ref[...] += dot(d_score_ref[...], keys)
            d_keys = dot_cols(d_score_ref[...], q_ref[...])
            d_kv_ref[rows, :HEAD] = (d_keys * score_scale).astype(bf16)
            d_kv_ref[rows, HEAD:] = dot_cols(prob_ref[...], d_att_ref[...]).astype(bf16)

        @pl.when(jnp.logical_not(live))
        def _():
            d_kv_ref[rows, :] = jnp.zeros((BLOCK, 2 * HEAD), bf16)

        return 0

    each = n_blocks // groups
    for i in range(groups):
        walk = functools.partial(step, kv_refs[i], d_kv_refs[i], i * each)
        lax.fori_loop(0, each, walk, 0)
    d_gain = jnp.zeros((1, HEAD), f32)
    for h in range(HEADS):
        cols = pl.ds(h * HEAD, HEAD)
        normed, factor = rms_forward(q_pre_ref[:, cols])
        d_normed = rotate(d_q_ref[head_rows(h), :] * score_scale, cosine, -sine)
        d_gain += jnp.sum(d_normed * normed, axis=0, keepdims=True)
        d_q_pre_ref[:, cols] = rms_backward(d_normed * gain_ref[...], normed, factor).astype(bf16)
    d_gain_ref[...] = d_gain


def attend_back(columns, order, q_pre, cosine, sine, gain, pos, *kv, saved, d_att):
    rows = q_pre.shape[0]
    n_blocks = sum(v.shape[0] for v in kv) // BLOCK
    whole = pl.BlockSpec(memory_space=pltpu.VMEM)
    return pl.pallas_call(
        functools.partial(attend_back_kernel, n_blocks, columns),
        out_shape=(
            jax.ShapeDtypeStruct((rows, HEADS * HEAD), bf16),
            *[jax.ShapeDtypeStruct(v.shape, bf16) for v in kv],
            jax.ShapeDtypeStruct((1, HEAD), f32),
        ),
        in_specs=[pl.BlockSpec(memory_space=pltpu.SMEM)] + [whole] * (8 + len(kv)),
        out_specs=(whole,) * (2 + len(kv)),
        scratch_shapes=[
            pltpu.VMEM((HEADS * rows, HEAD), f32),
            pltpu.VMEM((HEADS * rows, LANES), f32),
            pltpu.VMEM((HEADS * rows, HEAD), bf16),
            pltpu.VMEM((HEADS * rows, HEAD), bf16),
            pltpu.VMEM((HEADS * rows, HEAD), f32),
            pltpu.VMEM((HEADS * rows, HEAD), f32),
            pltpu.VMEM((HEADS * rows, HEAD), bf16),
            pltpu.VMEM((HEADS * rows, HEAD), bf16),
        ],
        cost_estimate=BRIEF,
        compiler_params=pltpu.CompilerParams(vmem_limit_bytes=16 << 20),
        name="attend_back",
    )(order, q_pre, cosine, sine, gain, pos, *saved, d_att, *kv)


def gelu_parts(gate):
    c = (2.0 / jnp.pi) ** 0.5
    square = gate * gate
    t = jnp.tanh(gate * (c + (c * 0.044715) * square))
    half = 0.5 + 0.5 * t
    act = gate * half
    slope = half + act * (1.0 - t) * (c + (3 * c * 0.044715) * square)
    return act, slope


def put_halves(part, refs):
    half = part.shape[0] // 2
    refs[0][...] = part[:half].astype(refs[0].dtype)
    refs[1][...] = part[half:].astype(refs[1].dtype)


def feed_kernel(groups, pieces, *refs):
    weights, halves, (hidden_ref, act_ref, slope_ref) = refs[pieces:-5], refs[-5:-3], refs[-3:]
    b = jnp.concatenate([r[...] for r in refs[:pieces]], axis=0)
    part = 0.0
    for i in range(groups):
        gate_ref, up_ref, down_ref = weights[3 * i : 3 * i + 3]
        gate = dot_rows(b, gate_ref[...])
        up = dot_rows(b, up_ref[...])
        act, slope = gelu_parts(gate)
        hidden_ref[i] = (act * up).astype(bf16)
        act_ref[i] = act.astype(bf16)
        slope_ref[i] = (up * slope).astype(bf16)
        part = part + dot(hidden_ref[i], down_ref[...])
    put_halves(part, halves)


def feed(b, weights, dtype):
    rows, width = sum(v.shape[0] for v in b), b[0].shape[1]
    groups, ff = len(weights) // 3, weights[0].shape[0]
    whole = pl.BlockSpec(memory_space=pltpu.VMEM)
    return pl.pallas_call(
        functools.partial(feed_kernel, groups, len(b)),
        out_shape=(
            *[jax.ShapeDtypeStruct((rows // 2, width), dtype)] * 2,
            *[jax.ShapeDtypeStruct((groups, rows, ff), bf16)] * 3,
        ),
        in_specs=[whole] * (len(b) + len(weights)),
        out_specs=(whole,) * 5,
        cost_estimate=BRIEF,
        compiler_params=pltpu.CompilerParams(vmem_limit_bytes=FEED_VMEM),
        name="feed",
    )(*b, *weights)


def feed_back_kernel(groups, pieces, act_ref, slope_ref, *refs):
    weights, halves, (d_gate_ref, d_up_ref) = refs[pieces:-4], refs[-4:-2], refs[-2:]
    d = jnp.concatenate([r[...] for r in refs[:pieces]], axis=0)
    part = 0.0
    for i in range(groups):
        gate_ref, up_ref, down_ref = weights[3 * i : 3 * i + 3]
        d_hidden = dot_rows(d, down_ref[...])
        d_gate_ref[i] = (d_hidden * slope_ref[i].astype(f32)).astype(bf16)
        d_up_ref[i] = (d_hidden * act_ref[i].astype(f32)).astype(bf16)
        part = part + dot(d_gate_ref[i], gate_ref[...]) + dot(d_up_ref[i], up_ref[...])
    put_halves(part, halves)


def feed_back(d, act, slope, weights, dtype):
    rows, width = sum(v.shape[0] for v in d), d[0].shape[1]
    groups, ff = len(weights) // 3, weights[0].shape[0]
    whole = pl.BlockSpec(memory_space=pltpu.VMEM)
    return pl.pallas_call(
        functools.partial(feed_back_kernel, groups, len(d)),
        out_shape=(
            *[jax.ShapeDtypeStruct((rows // 2, width), dtype)] * 2,
            *[jax.ShapeDtypeStruct((groups, rows, ff), bf16)] * 2,
        ),
        in_specs=[whole] * (2 + len(d) + len(weights)),
        out_specs=(whole,) * 4,
        cost_estimate=BRIEF,
        compiler_params=pltpu.CompilerParams(vmem_limit_bytes=FEED_VMEM),
        name="feed_back",
    )(act, slope, *d, *weights)


def weight_grad_kernel(index, sizes, count, pieces, *refs):
    lefts, rights, rest = refs[:count], refs[count : count + pieces], refs[count + pieces :]
    extra, outs = rest[: -len(sizes)], rest[-len(sizes) :]
    left = jnp.concatenate([v[index] for v in lefts], axis=0)
    right = jnp.concatenate([v[...] for v in rights], axis=0)
    total = dot_cols(left, right)
    if extra:
        total = total + extra[0][...].astype(f32)
    begin = 0
    for size, out in zip(sizes, outs):
        out[...] = total[begin : begin + size].astype(bf16)
        begin += size


def weight_grad(index, sizes, lefts, rights, *extra):
    rights = [piece for part in rights for piece in part]
    width = rights[0].shape[1]
    whole = pl.BlockSpec(memory_space=pltpu.VMEM)
    return pl.pallas_call(
        functools.partial(weight_grad_kernel, index, sizes, len(lefts), len(rights)),
        out_shape=tuple(jax.ShapeDtypeStruct((size, width), bf16) for size in sizes),
        in_specs=[whole] * (len(lefts) + len(rights) + len(extra)),
        out_specs=(whole,) * len(sizes),
        cost_estimate=BRIEF,
        compiler_params=pltpu.CompilerParams(vmem_limit_bytes=FEED_VMEM),
        name="weight_grad",
    )(*lefts, *rights, *extra)


def middle_back_kernel(counts, out_count, *refs):
    terms, refs = refs[: sum(counts)], refs[sum(counts) :]
    g_ref, middle_ref, attn_ref, pre_ref, post_ref = refs[:5]
    outs, (d_middle_ref, d_attn_ref, d_att_ref, gain_ref) = refs[5 : 5 + out_count], refs[-4:]
    pre, post = 0.0, 0.0
    half = g_ref.shape[0] // 2
    for i in range(2):
        own = terms[: counts[0]] if i == 0 else terms[counts[0] :]
        rows = pl.ds(i * half, half)
        d_b = functools.reduce(jnp.add, [t[...].astype(f32) for t in own])
        normed, factor = rms_forward(middle_ref[rows, :])
        pre = pre + jnp.sum(d_b * normed, axis=0, keepdims=True)
        d_middle = g_ref[rows, :] + rms_backward(d_b * pre_ref[...], normed, factor)
        d_middle_ref[rows, :] = d_middle
        normed, factor = rms_forward(attn_ref[rows, :])
        post = post + jnp.sum(d_middle * normed, axis=0, keepdims=True)
        d_attn = rms_backward(d_middle * post_ref[...], normed, factor).astype(bf16)
        d_attn_ref[rows, :] = d_attn
    at = 0
    for out in outs:
        d_att_ref[:, at : at + out.shape[0]] = dot_rows(d_attn_ref[...], out[...]).astype(bf16)
        at += out.shape[0]
    gain_ref[0:1, :] = pre
    gain_ref[1:2, :] = post


def middle_back(halves, g, middle, attn, g_pre, g_post, outs):
    rows, width = g.shape
    whole = pl.BlockSpec(memory_space=pltpu.VMEM)
    return pl.pallas_call(
        functools.partial(middle_back_kernel, [len(h) for h in halves], len(outs)),
        out_shape=(
            jax.ShapeDtypeStruct((rows, width), f32),
            jax.ShapeDtypeStruct((rows, width), bf16),
            jax.ShapeDtypeStruct((rows, HEADS * HEAD), bf16),
            jax.ShapeDtypeStruct((2, width), f32),
        ),
        in_specs=[whole] * (sum(len(h) for h in halves) + 5 + len(outs)),
        out_specs=(whole,) * 4,
        cost_estimate=BRIEF,
        compiler_params=pltpu.CompilerParams(vmem_limit_bytes=FEED_VMEM),
        name="middle_back",
    )(*halves[0], *halves[1], g, middle, attn, g_pre[None], g_post[None], *outs)


def add(*terms):
    return functools.reduce(jnp.add, [t.astype(f32) for t in terms])


fence = lax.optimization_barrier


class Plain:
    def __init__(self, n, rank, place):
        self.n, self.rank, self.place = n, rank, place

    def order(self):
        return jnp.arange(self.n, dtype=jnp.int32)

    def slots(self):
        return jnp.zeros(1, jnp.int32)

    def send(self, shard):
        return [shard]

    def paired(self, shards):
        return [lax.all_gather(shards[0], "seq", axis=0, tiled=True)]

    def joined(self, shard, near, far):
        return self.paired([shard])

    def columns(self, value):
        return [value]

    def ordered(self, blocks):
        return blocks[0]

    def pair(self, shard):
        return [shard]

    def near(self, shard):
        return ()

    def far(self, near):
        return ()

    def spread(self, shard):
        return tuple(jnp.split(self.joined(shard, (), ())[0], self.n, axis=0))

    def first(self, shard, near):
        return (near[0],)

    def tokens(self, shard, near, far):
        return [(part,) for part in near]

    def early(self, x, y):
        return ()

    def relay(self, far):
        return ()

    def late(self, x, y, relay):
        return ()

    def halves(self, parts, early, late):
        whole = self.scatter(all_of([half.astype(bf16) for part in parts for half in part]))
        return [[half] for half in jnp.split(whole, 2, axis=0)]

    def across(self, value):
        return ()

    def group(self, partial, moved):
        return (partial[0],)

    def group_near(self, group):
        return ()

    def group_far(self, group):
        return ()

    def group_sum(self, group, near, far):
        return self.scatter(group[0])

    def scatter(self, partial):
        return lax.psum_scatter(
            partial.astype(bf16), "seq", scatter_dimension=0, tiled=True
        ).astype(f32)

    def projection(self, left, right, gains):
        grad = dot_cols(left, right).reshape(self.n, -1, right.shape[1])
        gains = jnp.broadcast_to(gains[None], (self.n, *gains.shape))
        return [jnp.concatenate([grad, gains], axis=1).reshape(-1, right.shape[1])]

    def line(self):
        return PlainLine(None)


class Cube(Plain):
    chips = (0, 2, 4, 6)
    ranks = (0, 2, 4, 6, 1, 3, 5, 7)

    def hop(self, value, bit):
        return lax.ppermute(value, "seq", [(i, i ^ bit) for i in range(8)])

    def order(self):
        return self.rank ^ jnp.array(self.ranks, dtype=jnp.int32)

    def slots(self):
        return self.order()

    def send(self, shard):
        return [shard] + [self.hop(shard, bit) for bit in self.chips[1:]]

    def joined(self, shard, near, far):
        return self.paired([shard, *near, *far])

    def paired(self, shards):
        group = all_of(shards)
        return [group, self.hop(group, 1)]

    def near(self, shard):
        return (self.hop(shard, 2), self.hop(shard, 4))

    def far(self, near):
        half = near[0].shape[0] // 2
        return (self.hop(near[1][:half], 2), self.hop(near[0][half:], 4))

    def spread(self, shard):
        return self.near(shard)

    def first(self, shard, near):
        return (shard,)

    def tokens(self, shard, near, far):
        return [(shard,), *[(v,) for v in near], tuple(far)]

    def early(self, x, y):
        return (self.hop(x[0], 2), self.hop(y[1], 4))

    def relay(self, far):
        return (self.hop(far[0], 2), self.hop(far[1], 4))

    def late(self, x, y, relay):
        return (
            self.hop(add(x[1], relay[1]).astype(bf16), 2),
            self.hop(add(y[0], relay[0]).astype(bf16), 4),
        )

    def halves(self, parts, early, late):
        own = parts[0]
        return [[own[0], early[0], late[1]], [own[1], early[1], late[0]]]

    def across(self, value):
        return (self.hop(value, 1),)

    def group(self, partial, moved):
        parts = jnp.split(add(partial[0], *moved), 4, axis=0)
        return (parts[0], *[p.astype(bf16) for p in parts[1:]])

    def group_near(self, group):
        return (self.hop(group[1], 2), self.hop(group[2], 4))

    def group_far(self, group):
        return (self.hop(group[3], 6),)

    def group_sum(self, group, near, far):
        return add(group[0], *near, *far)

    def select(self, size, stride):
        shape = (self.n * size, self.n * stride)
        col = lax.broadcasted_iota(jnp.int32, shape, 1)
        block, at = col // stride, col % stride
        source = self.rank ^ ((2 * block) % 8 + block // 4)
        row = lax.broadcasted_iota(jnp.int32, shape, 0)
        return ((row == source * size + at) & (at < size)).astype(bf16)

    def columns(self, value):
        moved = dot(value, self.select(value.shape[1] // self.n, value.shape[1] // self.n))
        return jnp.split(moved.astype(value.dtype), 2, axis=1)

    def ordered(self, blocks):
        whole = all_of(blocks)
        size = whole.shape[0] // self.n
        return dot(self.select(size, size), whole).astype(whole.dtype)

    def pair(self, shard):
        return [shard, self.hop(shard, 1)]

    def projection(self, left, right, gains):
        size, extra = left.shape[1] // self.n, gains.shape[0]
        stride = size + extra
        moved = dot(left, self.select(size, stride)).astype(bf16)
        shape = (extra, self.n * stride)
        at = lax.broadcasted_iota(jnp.int32, shape, 1) % stride
        pick = (at == size + lax.broadcasted_iota(jnp.int32, shape, 0)).astype(bf16)
        left = jnp.concatenate([moved, pick], axis=0)
        right = jnp.concatenate([right, gains.astype(bf16)], axis=0)
        half = self.n * stride // 2
        return [dot_cols(left[:, :half], right), dot_cols(left[:, half:], right)]

    def line(self):
        return CubeLine((self.place == 1) | (self.place == 2))


class PlainLine:
    def __init__(self, inner):
        self.inner = inner
        self.chunks, self.wholes = [], []

    def add_rows(self, whole, parts):
        size = whole.shape[0] // parts
        self.wholes.append(whole)
        self.chunks += [(len(self.wholes) - 1, i * size, size) for i in range(parts)]

    def chunk(self, at):
        if len(self.chunks[at]) == 1:
            return self.chunks[at][0]
        source, start, size = self.chunks[at]
        return self.wholes[source][start : start + size]

    def step(self, beside):
        return fence(beside(()))

    def finish(self, early):
        chunks = [self.chunk(i) for i in range(len(self.chunks))]
        done = [lax.psum(c, "dp").astype(f32) for c in chunks]
        return done, early(done[-2])


class CubeLine(PlainLine):
    def __init__(self, inner):
        super().__init__(inner)
        self.halves, self.totals, self.out = {}, {}, {}
        self.at = 0

    def step(self, beside):
        tick = self.at
        self.at += 1
        mine = self.chunk(tick) if tick < len(self.chunks) else None
        back, half = self.totals.get(tick - 2), self.halves.get(tick - 1)
        got = {}
        if mine is not None and back is not None and mine.shape == back.shape:
            both = jnp.where(self.inner, back, mine)
            got["in"] = lax.ppermute(both, "dp", [(0, 1), (1, 0), (2, 3), (3, 2)])
        else:
            if back is not None:
                got["out"] = self.outwards(back)
            if mine is not None:
                got["in"] = lax.ppermute(mine, "dp", [(0, 1), (3, 2)])
        if half is not None:
            got["middle"] = lax.ppermute(half, "dp", [(1, 2), (2, 1)])
        values = beside(())
        later = [c for c in self.chunks[tick + 1 :] if len(c) == 1]
        got, values, later, self.wholes = fence((got, values, later, self.wholes))
        for at in range(tick + 1, len(self.chunks)):
            if len(self.chunks[at]) == 1:
                self.chunks[at] = later.pop(0)
        if mine is not None:
            self.halves[tick] = add(mine, got["in"]).astype(bf16)
        if half is not None:
            self.totals[tick - 1] = add(half, got["middle"]).astype(bf16)
        if back is not None:
            self.out[tick - 2] = jnp.where(self.inner, back, got["out"] if "out" in got else got["in"])
        return values

    def finish(self, early):
        count = len(self.chunks)
        while self.at < count:
            self.step(lambda values: values)
        back, half = self.totals[count - 2], self.halves[count - 1]
        back_moved = self.outwards(back)
        total = add(half, lax.ppermute(half, "dp", [(1, 2), (2, 1)])).astype(bf16)
        self.out[count - 2] = jnp.where(self.inner, back, back_moved)
        self.out[count - 1] = jnp.where(self.inner, total, self.outwards(total))
        made = early(self.out[count - 2].astype(f32))
        return [self.out[i].astype(f32) for i in range(count)], made

    def outwards(self, value):
        return lax.ppermute(value, "dp", [(1, 0), (2, 3)])


def all_of(values):
    return jnp.concatenate(values, axis=0)


def on_device(
    kind,
    layer_input,
    segment_ids,
    position_ids,
    w_query,
    w_keyval,
    w_out,
    w_gate,
    w_up,
    w_down,
    g_input,
    g_post_attn,
    g_pre_ffn,
    g_post_ffn,
    g_query,
    g_key,
    out_grad,
):
    n = lax.axis_size("seq")
    comm = kind(n, lax.axis_index("seq"), lax.axis_index("dp"))
    rows = layer_input.shape[1]
    width = layer_input.shape[2]
    ff = w_gate.shape[1]
    positions = position_ids[0]
    row_offset = comm.rank * rows
    order = jnp.concatenate(
        [comm.order(), row_offset[None], (row_offset - positions[0])[None], comm.slots()]
    ).astype(jnp.int32)
    shard = width // n
    starts = (comm.rank * shard, comm.rank * (HEAD // n), HEAD + comm.rank * (HEAD // n))
    line = comm.line()
    position_column = positions[:, None] + jnp.zeros((1, LANES), jnp.int32)

    x = layer_input[0].astype(f32)
    near = comm.near(w_keyval), comm.near(w_query)
    a_normed, a_factor = rms_forward(x)
    a_low = (a_normed * g_input).astype(bf16)
    a_columns = comm.columns(a_low)
    angles = rope_angles(positions, HEAD)
    cosine, sine = jnp.cos(angles), jnp.sin(angles)
    near, a_columns, order, starts, position_column, line.inner, comm.rank = fence(
        (near, a_columns, order, starts, position_column, line.inner, comm.rank)
    )
    far = [comm.far(v) for v in near]
    far, w_out = fence((far, w_out))
    out_near = comm.near(w_out)
    keyval_blocks = comm.joined(w_keyval, near[0], far[0])
    query_blocks = comm.joined(w_query, near[1], far[1])
    kv_pre = add(*[dot(a, w) for a, w in zip(a_columns, keyval_blocks)])
    k_hat, k_factor = rms_forward(kv_pre[:, :HEAD])
    k_low = rotate(k_hat * g_key, cosine, sine).astype(bf16)
    kv_low = jnp.concatenate([k_low, kv_pre[:, HEAD:].astype(bf16)], axis=1)
    kv_low, keyval_blocks, query_blocks = fence((kv_low, keyval_blocks, query_blocks))
    kv_near = comm.near(kv_low)
    q_pre = add(*[dot(a, w) for a, w in zip(a_columns, query_blocks)])
    kv_near, out_near, q_pre = fence((kv_near, out_near, q_pre))
    kv_far = comm.far(kv_near)
    kv_far, out_near = fence((kv_far, out_near))
    kv_blocks = comm.joined(kv_low, kv_near, kv_far)
    out_far = comm.far(out_near)
    kv_blocks, out_far, w_gate, w_up, w_down, query_blocks, keyval_blocks = fence(
        (kv_blocks, out_far, w_gate, w_up, w_down, query_blocks, keyval_blocks)
    )
    out_blocks = comm.joined(w_out, out_near, out_far)
    head_args = (
        comm.slots().shape[0],
        order,
        q_pre,
        cosine,
        sine,
        g_query[None],
        position_column,
        *kv_blocks,
    )
    att_low, inverse = attend(*head_args)
    out_blocks, att_low, w_gate, w_up, w_down = fence((out_blocks, att_low, w_gate, w_up, w_down))
    gate_w, up_w, down_w = [comm.pair(w) for w in (w_gate.T, w_up.T, w_down)]
    groups = len(gate_w)
    att_columns = jnp.split(att_low, len(out_blocks), axis=1)
    attn = add(*[dot(v, w) for v, w in zip(att_columns, out_blocks)])
    attn_normed, attn_factor = rms_forward(attn)
    middle = x + attn_normed * g_post_attn
    b_normed, b_factor = rms_forward(middle)
    b_low = (b_normed * g_pre_ffn).astype(bf16)
    b_low, query_blocks, keyval_blocks = fence((b_low, query_blocks, keyval_blocks))
    weights = [w[i] for i in range(groups) for w in (gate_w, up_w, down_w)]

    near = comm.spread(b_low)
    kept = [feed(comm.first(b_low, near), weights, f32)]
    query_whole = comm.ordered(query_blocks)
    kept, near, query_whole, keyval_blocks = fence((kept, near, query_whole, keyval_blocks))
    far = comm.far(near)
    b_list = comm.tokens(b_low, near, far)
    kept += [feed(part, weights, bf16) for part in b_list[1:-1]]
    kept, far, tail = fence((kept, far, b_list[-1]))
    b_list[-1] = tail
    early = comm.early(kept[1][:2], kept[2][:2])
    kept.append(feed(tail, weights, bf16))
    kept, early = fence((kept, early))
    parts = [v[:2] for v in kept]
    hidden, acts, slopes = [[v[i] for v in kept] for i in (2, 3, 4)]
    relay = comm.relay(parts[-1])
    late = comm.late(parts[1], parts[2], relay)
    ffn = all_of([add(*terms) for terms in comm.halves(parts, early, late)])
    ffn_normed, ffn_factor = rms_forward(ffn)
    layer_out = (middle + ffn_normed * g_post_ffn).astype(bf16)

    g = out_grad[0]
    d_ffn = rms_backward(g * g_post_ffn, ffn_normed, ffn_factor).astype(bf16)
    d_ffn, ffn_normed, keyval_blocks = fence((d_ffn, ffn_normed, keyval_blocks))

    def back(part, i):
        return feed_back(part, acts[i], slopes[i], weights, bf16 if i else f32)

    def other_half(lefts, rights):
        return weight_grad(1, [ff], lefts, rights) if groups > 1 else ()

    near = comm.spread(d_ffn)
    gain_post_ffn = jnp.sum(g * ffn_normed, axis=0)
    kept = [back(comm.first(d_ffn, near), 0)]
    keyval_whole = comm.ordered(keyval_blocks)
    kept, near, gain_post_ffn, keyval_whole = fence((kept, near, gain_post_ffn, keyval_whole))
    far = comm.far(near)
    d_list = comm.tokens(d_ffn, near, far)
    last = len(d_list) - 1
    kept += [back(d_list[i], i) for i in range(1, last)]
    kept, far, tail = fence((kept, far, d_list[-1]))
    d_list[-1] = tail

    other = [comm.hop(v, 1) for v in other_half(hidden, d_list)]
    kept.append(back(tail, last))
    kept, other = fence((kept, other))
    parts = [v[:2] for v in kept]
    d_gate, d_up = [[v[i] for v in kept] for i in (2, 3)]
    thirds = [ff // 3] * 3
    line.chunks += [(v,) for v in weight_grad(0, thirds, hidden, d_list, *other)]

    line.chunks, parts, d_gate, d_up, a_late = fence((line.chunks, parts, d_gate, d_up, a_low))

    def beside(_):
        early = comm.early(parts[1], parts[2])
        relay = comm.relay(parts[-1])
        others = other_half(d_gate, b_list), other_half(d_up, b_list)
        return early, relay, others, d_gate, d_up, parts

    early, relay, others, d_gate, d_up, parts = line.step(beside)

    def beside(_):
        late = comm.late(parts[1], parts[2], relay)
        (grads,) = weight_grad(0, [ff], d_gate, b_list, *[comm.hop(v, 1) for v in others[0]])
        late, grads = fence((late, grads))
        middles = middle_back(
            comm.halves(parts, early, late), g, middle, attn, g_pre_ffn, g_post_attn, out_blocks
        )
        return grads, d_up, others[1], middles

    grads, d_up, other_up, (d_middle, d_attn, d_att, gain_pair) = line.step(beside)
    line.add_rows(grads, 3)

    def beside(_):
        heads = attend_back(*head_args, saved=(att_low, inverse), d_att=d_att)
        grad_out = [dot_cols(v, d_attn) for v in att_columns]
        return heads, d_up, grad_out, [comm.hop(v, 1) for v in other_up]

    heads, d_up, grad_out, other_up = line.step(beside)
    d_q_pre, *d_kv_blocks, gain_query = heads

    def beside(_):
        group = comm.group(d_kv_blocks, comm.across(d_kv_blocks[-1]))
        near = comm.group_near(group)
        (grads,) = weight_grad(0, [ff], d_up, b_list, *other_up)
        return group, near, grads, grad_out, a_late, (gain_post_ffn, gain_pair, gain_query)

    group, near, grads, grad_out, a_late, early_gains = line.step(beside)
    line.add_rows(grads, 3)

    def beside(_):
        d_kv = comm.group_sum(group, near, comm.group_far(group))
        d_k_normed = rotate(d_kv[:, :HEAD], cosine, -sine)
        gain_key = jnp.sum(d_k_normed * k_hat, axis=0)
        d_k_pre = rms_backward(d_k_normed * g_key, k_hat, k_factor)
        d_kv_pre = jnp.concatenate([d_k_pre, d_kv[:, HEAD:]], axis=1).astype(bf16)
        d_a = dot_rows(d_q_pre, query_whole) + dot_rows(d_kv_pre, keyval_whole)
        gain_input = jnp.sum(d_a * a_normed, axis=0)
        out_group = comm.group(grad_out, comm.across(grad_out[-1].astype(bf16)))
        return d_kv_pre, d_a, (gain_input, gain_key), out_group, a_late, early_gains

    d_kv_pre, d_a, (gain_input, gain_key), out_group, a_late, early_gains = line.step(beside)
    gain_post_ffn, gain_pair, gain_query = early_gains

    def beside(_):
        out_near = comm.group_near(out_group)
        d_qkv = jnp.concatenate([d_q_pre, d_kv_pre], axis=1)
        gains = [gain_input, gain_pair[1], gain_pair[0], gain_post_ffn]
        gains.append(jnp.concatenate([gain_query[0], gain_key]))
        gains = [jnp.pad(v, (0, d_qkv.shape[1] - v.shape[0])) for v in gains]
        row = lax.broadcasted_iota(jnp.int32, (16, d_qkv.shape[1]), 0)
        gains = add(*[jnp.where(row == i, v[None], 0.0) for i, v in enumerate(gains)])
        grad_qkv = comm.projection(a_late, d_qkv, gains)
        return out_group, out_near, grad_qkv, d_a

    out_group, out_near, grad_qkv, d_a = line.step(beside)

    def beside(_):
        qkv_moved = comm.across(grad_qkv[-1].astype(bf16))
        out_far = comm.group_far(out_group)
        d_input = d_middle + rms_backward(d_a * g_input, a_normed, a_factor)
        total_out = comm.group_sum(out_group, out_near, out_far).astype(bf16)
        return comm.group(grad_qkv, qkv_moved), total_out, d_input

    group, total_out, d_input = line.step(beside)

    def beside(_):
        return group, comm.group_near(group), total_out

    group, near, total_out = line.step(beside)

    def beside(_):
        return comm.group_far(group), near, total_out

    far, near, total_out = line.step(beside)
    line.chunks += [(comm.group_sum(group, near, far).astype(bf16),), (total_out,)]
    def owned(tail):
        def mine(row, start, size):
            return lax.dynamic_slice(
                tail[shard + row], (start,), (size,), allow_negative_indices=False
            )

        grads = [tail[:shard, : HEADS * HEAD], tail[:shard, HEADS * HEAD :]]
        names = [mine(i, starts[0], shard) for i in range(4)]
        return grads, names + [mine(4, start, HEAD // n) for start in starts[1:]]

    (*done, _, total_out), ((grad_query, grad_keyval), names) = line.finish(owned)
    down, gate, up = all_of(done[:3]), all_of(done[3:6]), all_of(done[6:])
    return (
        layer_out[None],
        d_input[None],
        grad_query,
        grad_keyval,
        total_out,
        gate.T,
        up.T,
        down,
        *names,
    )


def solution(mesh):
    cube = mesh.shape["seq"] == 8 and mesh.shape["dp"] == 4
    in_specs = (
        P("dp", "seq", None),
        P("dp", None),
        P("dp", "seq"),
        P("seq", None),
        P("seq", None),
        P("seq", None),
        P(None, "seq"),
        P(None, "seq"),
        P("seq", None),
        P(),
        P(),
        P(),
        P(),
        P(),
        P(),
        P("dp", "seq", None),
    )
    out_specs = (
        P("dp", "seq", None),
        P("dp", "seq", None),
        P("seq", None),
        P("seq", None),
        P("seq", None),
        P(None, "seq"),
        P(None, "seq"),
        P("seq", None),
        P("seq"),
        P("seq"),
        P("seq"),
        P("seq"),
        P("seq"),
        P("seq"),
    )
    return jax.shard_map(
        functools.partial(on_device, Cube if cube else Plain),
        mesh=mesh,
        in_specs=in_specs,
        out_specs=out_specs,
        check_vma=False,
    )
```

```python
import functools

import jax
import jax.numpy as jnp
from jax import lax
from jax.experimental import pallas as pl
from jax.experimental.pallas import tpu as pltpu
from jax.sharding import PartitionSpec as P

HEADS = 4
HEAD = 256
BLOCK = 256
LANES = 128
FEED_VMEM = 12 << 20

norm_eps = 1e-06
rope_base = 1000000.0
score_scale = HEAD**-0.5
bf16 = jnp.bfloat16
f32 = jnp.float32
BRIEF = pl.CostEstimate(flops=1, bytes_accessed=1, transcendentals=0)


def rms_forward(values):
    factor = lax.rsqrt(jnp.mean(values * values, axis=-1, keepdims=True) + norm_eps)
    return (values * factor, factor)


def rms_backward(upstream, normed, factor):
    return factor * (upstream - normed * jnp.mean(upstream * normed, axis=-1, keepdims=True))


def rope_angles(positions, width):
    half_width = width // 2
    inverse_freq = rope_base ** (-(jnp.arange(half_width).astype(f32) * 2.0 / width))
    return positions.astype(f32)[:, None] * inverse_freq[None, :]


def rotate(values, cosine, sine):
    half_width = values.shape[-1] // 2
    first = values[..., :half_width]
    second = values[..., half_width:]
    return jnp.concatenate(
        [first * cosine - second * sine, second * cosine + first * sine], axis=-1
    )


def dot(left, right):
    return jnp.dot(left, right, preferred_element_type=f32)


def dot_rows(left, right):
    return lax.dot_general(left, right, (((1,), (1,)), ((), ())), preferred_element_type=f32)


def dot_cols(left, right):
    return lax.dot_general(left, right, (((0,), (0,)), ((), ())), preferred_element_type=f32)


def visible_mask(block_id, first_row, pos_ref):
    shape = (BLOCK, BLOCK)
    query = first_row + lax.broadcasted_iota(jnp.int32, shape, 0)
    key = block_id * BLOCK + lax.broadcasted_iota(jnp.int32, shape, 1)
    return (key <= query) & (key >= query - pos_ref[:, :1])


def head_rows(h):
    return pl.ds(h * BLOCK, BLOCK)


def put_queries(q_ref, q_pre_ref, gain_ref, cosine, sine):
    for h in range(HEADS):
        normed, _ = rms_forward(q_pre_ref[:, pl.ds(h * HEAD, HEAD)])
        q_ref[head_rows(h), :] = rotate(normed * gain_ref[...], cosine, sine).astype(bf16)


def column_blocks(columns, order_ref):
    if columns == 1:
        for h in range(HEADS):
            yield pl.ds(h * HEAD, HEAD), head_rows(h), pl.ds(0, HEAD)
        return
    slot, size = order_ref.shape[0] - columns, HEADS * HEAD // columns
    for k in range(columns):
        at = order_ref[slot + k] * size
        rows = pl.ds(pl.multiple_of(at // HEAD * BLOCK, BLOCK), BLOCK)
        yield pl.ds(k * size, size), rows, pl.ds(pl.multiple_of(at % HEAD, size), size)


def attend_kernel(
    n_blocks,
    columns,
    order_ref,
    q_pre_ref,
    cos_ref,
    sin_ref,
    gain_ref,
    pos_ref,
    *refs,
):
    kv_refs = refs[:-7]
    att_low_ref, inv_ref, q_ref, att_ref, total_ref, score_ref, weight_ref = refs[-7:]
    first_row = order_ref[n_blocks]
    first_key = order_ref[n_blocks + 1]
    put_queries(q_ref, q_pre_ref, gain_ref, cos_ref[...], sin_ref[...])
    att_ref[...] = jnp.zeros_like(att_ref)
    total_ref[...] = jnp.zeros_like(total_ref)

    def step(kv_ref, base, k, _):
        block_id = order_ref[base + k]
        live = (block_id * BLOCK <= first_row) & ((block_id + 1) * BLOCK > first_key)

        @pl.when(live)
        def _():
            rows = pl.ds(pl.multiple_of(k * BLOCK, BLOCK), BLOCK)
            visible = visible_mask(block_id, first_row, pos_ref)
            score_ref[...] = dot_rows(q_ref[...], kv_ref[rows, :HEAD])
            for h in range(HEADS):
                at = head_rows(h)
                weight = jnp.where(visible, jnp.exp(score_ref[at, :] * score_scale), 0.0)
                total_ref[at, :] += weight[:, :LANES] + weight[:, LANES:]
                weight_ref[at, :] = weight.astype(bf16)
            att_ref[...] += dot(weight_ref[...], kv_ref[rows, HEAD:])

        return 0

    each = n_blocks // len(kv_refs)
    for i, kv_ref in enumerate(kv_refs):
        lax.fori_loop(0, each, functools.partial(step, kv_ref, i * each), 0)
    for h in range(HEADS):
        at = head_rows(h)
        inverse = 1.0 / jnp.sum(total_ref[at, :], axis=-1, keepdims=True)
        inv_ref[:, pl.ds(h, 1)] = inverse
        att_ref[at, :] = att_ref[at, :] * inverse
    for stored, rows, lanes in column_blocks(columns, order_ref):
        att_low_ref[:, stored] = att_ref[rows, lanes].astype(bf16)


def attend(columns, order, q_pre, cosine, sine, gain, pos, *kv):
    rows = q_pre.shape[0]
    n_blocks = sum(v.shape[0] for v in kv) // BLOCK
    whole = pl.BlockSpec(memory_space=pltpu.VMEM)
    return pl.pallas_call(
        functools.partial(attend_kernel, n_blocks, columns),
        out_shape=(
            jax.ShapeDtypeStruct((rows, HEADS * HEAD), bf16),
            jax.ShapeDtypeStruct((rows, LANES), f32),
        ),
        in_specs=[pl.BlockSpec(memory_space=pltpu.SMEM)] + [whole] * (5 + len(kv)),
        out_specs=(whole,) * 2,
        scratch_shapes=[
            pltpu.VMEM((HEADS * rows, HEAD), bf16),
            pltpu.VMEM((HEADS * rows, HEAD), f32),
            pltpu.VMEM((HEADS * rows, LANES), f32),
            pltpu.VMEM((HEADS * rows, HEAD), f32),
            pltpu.VMEM((HEADS * rows, HEAD), bf16),
        ],
        cost_estimate=BRIEF,
        compiler_params=pltpu.CompilerParams(vmem_limit_bytes=10 << 20),
        name="attend",
    )(order, q_pre, cosine, sine, gain, pos, *kv)


def attend_back_kernel(
    n_blocks,
    columns,
    order_ref,
    q_pre_ref,
    cos_ref,
    sin_ref,
    gain_ref,
    pos_ref,
    att_ref,
    inv_ref,
    d_moved_ref,
    *refs,
):
    groups = (len(refs) - 10) // 2
    kv_refs, d_q_pre_ref, d_kv_refs = refs[:groups], refs[groups], refs[groups + 1 : -9]
    d_gain_ref, d_q_ref, row_dot_ref, d_att_ref, q_ref = refs[-9:-4]
    score_ref, d_prob_ref, prob_ref, d_score_ref = refs[-4:]
    cosine, sine = cos_ref[...], sin_ref[...]
    put_queries(q_ref, q_pre_ref, gain_ref, cosine, sine)
    row_dot_ref[...] = jnp.zeros_like(row_dot_ref)
    for stored, rows, lanes in column_blocks(columns, order_ref):
        moved = d_moved_ref[:, stored]
        d_att_ref[rows, lanes] = moved
        product = moved.astype(f32) * att_ref[:, stored].astype(f32)
        for i in range(product.shape[1] // LANES):
            row_dot_ref[rows, :] += product[:, i * LANES : (i + 1) * LANES]
    for h in range(HEADS):
        at = head_rows(h)
        total = jnp.sum(row_dot_ref[at, :], axis=-1, keepdims=True)
        row_dot_ref[at, pl.ds(0, 1)] = total
    first_row = order_ref[n_blocks]
    first_key = order_ref[n_blocks + 1]
    d_q_ref[...] = jnp.zeros_like(d_q_ref)

    def step(kv_ref, d_kv_ref, base, k, _):
        block_id = order_ref[base + k]
        live = (block_id * BLOCK <= first_row) & ((block_id + 1) * BLOCK > first_key)
        rows = pl.ds(pl.multiple_of(k * BLOCK, BLOCK), BLOCK)

        @pl.when(live)
        def _():
            keys = kv_ref[rows, :HEAD]
            visible = visible_mask(block_id, first_row, pos_ref)
            score_ref[...] = dot_rows(q_ref[...], keys)
            d_prob_ref[...] = dot_rows(d_att_ref[...], kv_ref[rows, HEAD:])
            for h in range(HEADS):
                at = head_rows(h)
                weight = jnp.where(visible, jnp.exp(score_ref[at, :] * score_scale), 0.0)
                prob = weight * inv_ref[:, pl.ds(h, 1)]
                prob_ref[at, :] = prob.astype(bf16)
                d_score = prob * (d_prob_ref[at, :] - row_dot_ref[at, pl.ds(0, 1)])
                d_score_ref[at, :] = d_score.astype(bf16)
            d_q_ref[...] += dot(d_score_ref[...], keys)
            d_keys = dot_cols(d_score_ref[...], q_ref[...])
            d_kv_ref[rows, :HEAD] = (d_keys * score_scale).astype(bf16)
            d_kv_ref[rows, HEAD:] = dot_cols(prob_ref[...], d_att_ref[...]).astype(bf16)

        @pl.when(jnp.logical_not(live))
        def _():
            d_kv_ref[rows, :] = jnp.zeros((BLOCK, 2 * HEAD), bf16)

        return 0

    each = n_blocks // groups
    for i in range(groups):
        walk = functools.partial(step, kv_refs[i], d_kv_refs[i], i * each)
        lax.fori_loop(0, each, walk, 0)
    d_gain = jnp.zeros((1, HEAD), f32)
    for h in range(HEADS):
        cols = pl.ds(h * HEAD, HEAD)
        normed, factor = rms_forward(q_pre_ref[:, cols])
        d_normed = rotate(d_q_ref[head_rows(h), :] * score_scale, cosine, -sine)
        d_gain += jnp.sum(d_normed * normed, axis=0, keepdims=True)
        d_q_pre_ref[:, cols] = rms_backward(d_normed * gain_ref[...], normed, factor).astype(bf16)
    d_gain_ref[...] = d_gain


def attend_back(columns, order, q_pre, cosine, sine, gain, pos, *kv, saved, d_att):
    rows = q_pre.shape[0]
    n_blocks = sum(v.shape[0] for v in kv) // BLOCK
    whole = pl.BlockSpec(memory_space=pltpu.VMEM)
    return pl.pallas_call(
        functools.partial(attend_back_kernel, n_blocks, columns),
        out_shape=(
            jax.ShapeDtypeStruct((rows, HEADS * HEAD), bf16),
            *[jax.ShapeDtypeStruct(v.shape, bf16) for v in kv],
            jax.ShapeDtypeStruct((1, HEAD), f32),
        ),
        in_specs=[pl.BlockSpec(memory_space=pltpu.SMEM)] + [whole] * (8 + len(kv)),
        out_specs=(whole,) * (2 + len(kv)),
        scratch_shapes=[
            pltpu.VMEM((HEADS * rows, HEAD), f32),
            pltpu.VMEM((HEADS * rows, LANES), f32),
            pltpu.VMEM((HEADS * rows, HEAD), bf16),
            pltpu.VMEM((HEADS * rows, HEAD), bf16),
            pltpu.VMEM((HEADS * rows, HEAD), f32),
            pltpu.VMEM((HEADS * rows, HEAD), f32),
            pltpu.VMEM((HEADS * rows, HEAD), bf16),
            pltpu.VMEM((HEADS * rows, HEAD), bf16),
        ],
        cost_estimate=BRIEF,
        compiler_params=pltpu.CompilerParams(vmem_limit_bytes=16 << 20),
        name="attend_back",
    )(order, q_pre, cosine, sine, gain, pos, *saved, d_att, *kv)


def gelu_parts(gate):
    c = (2.0 / jnp.pi) ** 0.5
    square = gate * gate
    t = jnp.tanh(gate * (c + (c * 0.044715) * square))
    half = 0.5 + 0.5 * t
    act = gate * half
    slope = half + act * (1.0 - t) * (c + (3 * c * 0.044715) * square)
    return act, slope


def put_halves(part, refs):
    half = part.shape[0] // 2
    refs[0][...] = part[:half].astype(refs[0].dtype)
    refs[1][...] = part[half:].astype(refs[1].dtype)


def feed_kernel(groups, pieces, *refs):
    weights, halves, (hidden_ref, act_ref, slope_ref) = refs[pieces:-5], refs[-5:-3], refs[-3:]
    b = jnp.concatenate([r[...] for r in refs[:pieces]], axis=0)
    part = 0.0
    for i in range(groups):
        gate_ref, up_ref, down_ref = weights[3 * i : 3 * i + 3]
        gate = dot_rows(b, gate_ref[...])
        up = dot_rows(b, up_ref[...])
        act, slope = gelu_parts(gate)
        hidden_ref[i] = (act * up).astype(bf16)
        act_ref[i] = act.astype(bf16)
        slope_ref[i] = (up * slope).astype(bf16)
        part = part + dot(hidden_ref[i], down_ref[...])
    put_halves(part, halves)


def feed(b, weights, dtype):
    rows, width = sum(v.shape[0] for v in b), b[0].shape[1]
    groups, ff = len(weights) // 3, weights[0].shape[0]
    whole = pl.BlockSpec(memory_space=pltpu.VMEM)
    return pl.pallas_call(
        functools.partial(feed_kernel, groups, len(b)),
        out_shape=(
            *[jax.ShapeDtypeStruct((rows // 2, width), dtype)] * 2,
            *[jax.ShapeDtypeStruct((groups, rows, ff), bf16)] * 3,
        ),
        in_specs=[whole] * (len(b) + len(weights)),
        out_specs=(whole,) * 5,
        cost_estimate=BRIEF,
        compiler_params=pltpu.CompilerParams(vmem_limit_bytes=FEED_VMEM),
        name="feed",
    )(*b, *weights)


def feed_back_kernel(groups, pieces, act_ref, slope_ref, *refs):
    weights, halves, (d_gate_ref, d_up_ref) = refs[pieces:-4], refs[-4:-2], refs[-2:]
    d = jnp.concatenate([r[...] for r in refs[:pieces]], axis=0)
    part = 0.0
    for i in range(groups):
        gate_ref, up_ref, down_ref = weights[3 * i : 3 * i + 3]
        d_hidden = dot_rows(d, down_ref[...])
        d_gate_ref[i] = (d_hidden * slope_ref[i].astype(f32)).astype(bf16)
        d_up_ref[i] = (d_hidden * act_ref[i].astype(f32)).astype(bf16)
        part = part + dot(d_gate_ref[i], gate_ref[...]) + dot(d_up_ref[i], up_ref[...])
    put_halves(part, halves)


def feed_back(d, act, slope, weights, dtype):
    rows, width = sum(v.shape[0] for v in d), d[0].shape[1]
    groups, ff = len(weights) // 3, weights[0].shape[0]
    whole = pl.BlockSpec(memory_space=pltpu.VMEM)
    return pl.pallas_call(
        functools.partial(feed_back_kernel, groups, len(d)),
        out_shape=(
            *[jax.ShapeDtypeStruct((rows // 2, width), dtype)] * 2,
            *[jax.ShapeDtypeStruct((groups, rows, ff), bf16)] * 2,
        ),
        in_specs=[whole] * (2 + len(d) + len(weights)),
        out_specs=(whole,) * 4,
        cost_estimate=BRIEF,
        compiler_params=pltpu.CompilerParams(vmem_limit_bytes=FEED_VMEM),
        name="feed_back",
    )(act, slope, *d, *weights)


def weight_grad_kernel(index, sizes, count, pieces, *refs):
    lefts, rights, rest = refs[:count], refs[count : count + pieces], refs[count + pieces :]
    extra, outs = rest[: -len(sizes)], rest[-len(sizes) :]
    left = jnp.concatenate([v[index] for v in lefts], axis=0)
    right = jnp.concatenate([v[...] for v in rights], axis=0)
    total = dot_cols(left, right)
    if extra:
        total = total + extra[0][...].astype(f32)
    begin = 0
    for size, out in zip(sizes, outs):
        out[...] = total[begin : begin + size].astype(bf16)
        begin += size


def weight_grad(index, sizes, lefts, rights, *extra):
    rights = [piece for part in rights for piece in part]
    width = rights[0].shape[1]
    whole = pl.BlockSpec(memory_space=pltpu.VMEM)
    return pl.pallas_call(
        functools.partial(weight_grad_kernel, index, sizes, len(lefts), len(rights)),
        out_shape=tuple(jax.ShapeDtypeStruct((size, width), bf16) for size in sizes),
        in_specs=[whole] * (len(lefts) + len(rights) + len(extra)),
        out_specs=(whole,) * len(sizes),
        cost_estimate=BRIEF,
        compiler_params=pltpu.CompilerParams(vmem_limit_bytes=FEED_VMEM),
        name="weight_grad",
    )(*lefts, *rights, *extra)


def middle_back_kernel(counts, out_count, *refs):
    terms, refs = refs[: sum(counts)], refs[sum(counts) :]
    g_ref, middle_ref, attn_ref, pre_ref, post_ref = refs[:5]
    outs, (d_middle_ref, d_attn_ref, d_att_ref, gain_ref) = refs[5 : 5 + out_count], refs[-4:]
    pre, post = 0.0, 0.0
    half = g_ref.shape[0] // 2
    for i in range(2):
        own = terms[: counts[0]] if i == 0 else terms[counts[0] :]
        rows = pl.ds(i * half, half)
        d_b = functools.reduce(jnp.add, [t[...].astype(f32) for t in own])
        normed, factor = rms_forward(middle_ref[rows, :])
        pre = pre + jnp.sum(d_b * normed, axis=0, keepdims=True)
        d_middle = g_ref[rows, :] + rms_backward(d_b * pre_ref[...], normed, factor)
        d_middle_ref[rows, :] = d_middle
        normed, factor = rms_forward(attn_ref[rows, :])
        post = post + jnp.sum(d_middle * normed, axis=0, keepdims=True)
        d_attn = rms_backward(d_middle * post_ref[...], normed, factor).astype(bf16)
        d_attn_ref[rows, :] = d_attn
    at = 0
    for out in outs:
        d_att_ref[:, at : at + out.shape[0]] = dot_rows(d_attn_ref[...], out[...]).astype(bf16)
        at += out.shape[0]
    gain_ref[0:1, :] = pre
    gain_ref[1:2, :] = post


def middle_back(halves, g, middle, attn, g_pre, g_post, outs):
    rows, width = g.shape
    whole = pl.BlockSpec(memory_space=pltpu.VMEM)
    return pl.pallas_call(
        functools.partial(middle_back_kernel, [len(h) for h in halves], len(outs)),
        out_shape=(
            jax.ShapeDtypeStruct((rows, width), f32),
            jax.ShapeDtypeStruct((rows, width), bf16),
            jax.ShapeDtypeStruct((rows, HEADS * HEAD), bf16),
            jax.ShapeDtypeStruct((2, width), f32),
        ),
        in_specs=[whole] * (sum(len(h) for h in halves) + 5 + len(outs)),
        out_specs=(whole,) * 4,
        cost_estimate=BRIEF,
        compiler_params=pltpu.CompilerParams(vmem_limit_bytes=FEED_VMEM),
        name="middle_back",
    )(*halves[0], *halves[1], g, middle, attn, g_pre[None], g_post[None], *outs)


def add(*terms):
    return functools.reduce(jnp.add, [t.astype(f32) for t in terms])


fence = lax.optimization_barrier


class Plain:
    def __init__(self, n, rank, place):
        self.n, self.rank, self.place = n, rank, place

    def order(self):
        return jnp.arange(self.n, dtype=jnp.int32)

    def slots(self):
        return jnp.zeros(1, jnp.int32)

    def send(self, shard):
        return [shard]

    def paired(self, shards):
        return [lax.all_gather(shards[0], "seq", axis=0, tiled=True)]

    def joined(self, shard, near, far):
        return self.paired([shard])

    def columns(self, value):
        return [value]

    def ordered(self, blocks):
        return blocks[0]

    def pair(self, shard):
        return [shard]

    def near(self, shard):
        return ()

    def far(self, near):
        return ()

    def spread(self, shard):
        return tuple(jnp.split(self.joined(shard, (), ())[0], self.n, axis=0))

    def first(self, shard, near):
        return (near[0],)

    def tokens(self, shard, near, far):
        return [(part,) for part in near]

    def early(self, x, y):
        return ()

    def relay(self, far):
        return ()

    def late(self, x, y, relay):
        return ()

    def halves(self, parts, early, late):
        whole = self.scatter(all_of([half.astype(bf16) for part in parts for half in part]))
        return [[half] for half in jnp.split(whole, 2, axis=0)]

    def across(self, value):
        return ()

    def group(self, partial, moved):
        return (partial[0],)

    def group_near(self, group):
        return ()

    def group_far(self, group):
        return ()

    def group_sum(self, group, near, far):
        return self.scatter(group[0])

    def scatter(self, partial):
        return lax.psum_scatter(
            partial.astype(bf16), "seq", scatter_dimension=0, tiled=True
        ).astype(f32)

    def projection(self, left, right, gains):
        grad = dot_cols(left, right).reshape(self.n, -1, right.shape[1])
        gains = jnp.broadcast_to(gains[None], (self.n, *gains.shape))
        return [jnp.concatenate([grad, gains], axis=1).reshape(-1, right.shape[1])]

    def line(self):
        return PlainLine(None)


class Cube(Plain):
    chips = (0, 2, 4, 6)
    ranks = (0, 2, 4, 6, 1, 3, 5, 7)

    def hop(self, value, bit):
        return lax.ppermute(value, "seq", [(i, i ^ bit) for i in range(8)])

    def order(self):
        return self.rank ^ jnp.array(self.ranks, dtype=jnp.int32)

    def slots(self):
        return self.order()

    def send(self, shard):
        return [shard] + [self.hop(shard, bit) for bit in self.chips[1:]]

    def joined(self, shard, near, far):
        return self.paired([shard, *near, *far])

    def paired(self, shards):
        group = all_of(shards)
        return [group, self.hop(group, 1)]

    def near(self, shard):
        return (self.hop(shard, 2), self.hop(shard, 4))

    def far(self, near):
        half = near[0].shape[0] // 2
        return (self.hop(near[1][:half], 2), self.hop(near[0][half:], 4))

    def spread(self, shard):
        return self.near(shard)

    def first(self, shard, near):
        return (shard,)

    def tokens(self, shard, near, far):
        return [(shard,), *[(v,) for v in near], tuple(far)]

    def early(self, x, y):
        return (self.hop(x[0], 2), self.hop(y[1], 4))

    def relay(self, far):
        return (self.hop(far[0], 2), self.hop(far[1], 4))

    def late(self, x, y, relay):
        return (
            self.hop(add(x[1], relay[1]).astype(bf16), 2),
            self.hop(add(y[0], relay[0]).astype(bf16), 4),
        )

    def halves(self, parts, early, late):
        own = parts[0]
        return [[own[0], early[0], late[1]], [own[1], early[1], late[0]]]

    def across(self, value):
        return (self.hop(value, 1),)

    def group(self, partial, moved):
        parts = jnp.split(add(partial[0], *moved), 4, axis=0)
        return (parts[0], *[p.astype(bf16) for p in parts[1:]])

    def group_near(self, group):
        return (self.hop(group[1], 2), self.hop(group[2], 4))

    def group_far(self, group):
        return (self.hop(group[3], 6),)

    def group_sum(self, group, near, far):
        return add(group[0], *near, *far)

    def select(self, size, stride):
        shape = (self.n * size, self.n * stride)
        col = lax.broadcasted_iota(jnp.int32, shape, 1)
        block, at = col // stride, col % stride
        source = self.rank ^ ((2 * block) % 8 + block // 4)
        row = lax.broadcasted_iota(jnp.int32, shape, 0)
        return ((row == source * size + at) & (at < size)).astype(bf16)

    def columns(self, value):
        moved = dot(value, self.select(value.shape[1] // self.n, value.shape[1] // self.n))
        return jnp.split(moved.astype(value.dtype), 2, axis=1)

    def ordered(self, blocks):
        whole = all_of(blocks)
        size = whole.shape[0] // self.n
        return dot(self.select(size, size), whole).astype(whole.dtype)

    def pair(self, shard):
        return [shard, self.hop(shard, 1)]

    def projection(self, left, right, gains):
        size, extra = left.shape[1] // self.n, gains.shape[0]
        stride = size + extra
        moved = dot(left, self.select(size, stride)).astype(bf16)
        shape = (extra, self.n * stride)
        at = lax.broadcasted_iota(jnp.int32, shape, 1) % stride
        pick = (at == size + lax.broadcasted_iota(jnp.int32, shape, 0)).astype(bf16)
        left = jnp.concatenate([moved, pick], axis=0)
        right = jnp.concatenate([right, gains.astype(bf16)], axis=0)
        half = self.n * stride // 2
        return [dot_cols(left[:, :half], right), dot_cols(left[:, half:], right)]

    def line(self):
        return CubeLine((self.place == 1) | (self.place == 2))


class PlainLine:
    def __init__(self, inner):
        self.inner = inner
        self.chunks, self.wholes = [], []

    def add_rows(self, whole, parts):
        size = whole.shape[0] // parts
        self.wholes.append(whole)
        self.chunks += [(len(self.wholes) - 1, i * size, size) for i in range(parts)]

    def chunk(self, at):
        if len(self.chunks[at]) == 1:
            return self.chunks[at][0]
        source, start, size = self.chunks[at]
        return self.wholes[source][start : start + size]

    def step(self, beside, sum_first=False):
        return fence(beside(()))

    def finish(self, early):
        chunks = [self.chunk(i) for i in range(len(self.chunks))]
        done = [lax.psum(c, "dp").astype(f32) for c in chunks]
        return done, early(done[-2])


class CubeLine(PlainLine):
    def __init__(self, inner):
        super().__init__(inner)
        self.halves, self.totals, self.out = {}, {}, {}
        self.at = 0

    def step(self, beside, sum_first=False):
        tick = self.at
        self.at += 1
        mine = self.chunk(tick) if tick < len(self.chunks) else None
        back, half = self.totals.get(tick - 2), self.halves.get(tick - 1)
        got = {}
        if mine is not None and back is not None and mine.shape == back.shape:
            both = jnp.where(self.inner, back, mine)
            got["in"] = lax.ppermute(both, "dp", [(0, 1), (1, 0), (2, 3), (3, 2)])
        else:
            if back is not None:
                got["out"] = self.outwards(back)
            if mine is not None:
                got["in"] = lax.ppermute(mine, "dp", [(0, 1), (3, 2)])
        if half is not None:
            across = lax.ppermute(half, "dp", [(1, 2), (2, 1)])
            got["middle"] = add(half, across).astype(bf16) if sum_first else across
        values = beside(())
        later = [c for c in self.chunks[tick + 1 :] if len(c) == 1]
        got, values, later, self.wholes = fence((got, values, later, self.wholes))
        for at in range(tick + 1, len(self.chunks)):
            if len(self.chunks[at]) == 1:
                self.chunks[at] = later.pop(0)
        if mine is not None:
            self.halves[tick] = add(mine, got["in"]).astype(bf16)
        if half is not None:
            middle = got["middle"]
            self.totals[tick - 1] = middle if sum_first else add(half, middle).astype(bf16)
        if back is not None:
            self.out[tick - 2] = jnp.where(self.inner, back, got["out"] if "out" in got else got["in"])
        return values

    def finish(self, early):
        count = len(self.chunks)
        while self.at < count:
            self.step(lambda values: values)
        back, half = self.totals[count - 2], self.halves[count - 1]
        back_moved = self.outwards(back)
        total = add(half, lax.ppermute(half, "dp", [(1, 2), (2, 1)])).astype(bf16)
        self.out[count - 2] = jnp.where(self.inner, back, back_moved)
        self.out[count - 1] = jnp.where(self.inner, total, self.outwards(total))
        made = early(self.out[count - 2].astype(f32))
        return [self.out[i].astype(f32) for i in range(count)], made

    def outwards(self, value):
        return lax.ppermute(value, "dp", [(1, 0), (2, 3)])


def all_of(values):
    return jnp.concatenate(values, axis=0)


def on_device(
    kind,
    layer_input,
    segment_ids,
    position_ids,
    w_query,
    w_keyval,
    w_out,
    w_gate,
    w_up,
    w_down,
    g_input,
    g_post_attn,
    g_pre_ffn,
    g_post_ffn,
    g_query,
    g_key,
    out_grad,
):
    n = lax.axis_size("seq")
    comm = kind(n, lax.axis_index("seq"), lax.axis_index("dp"))
    rows = layer_input.shape[1]
    width = layer_input.shape[2]
    ff = w_gate.shape[1]
    positions = position_ids[0]
    row_offset = comm.rank * rows
    order = jnp.concatenate(
        [comm.order(), row_offset[None], (row_offset - positions[0])[None], comm.slots()]
    ).astype(jnp.int32)
    shard = width // n
    starts = (comm.rank * shard, comm.rank * (HEAD // n), HEAD + comm.rank * (HEAD // n))
    line = comm.line()
    position_column = positions[:, None] + jnp.zeros((1, LANES), jnp.int32)

    x = layer_input[0].astype(f32)
    near = comm.near(w_keyval), comm.near(w_query)
    a_normed, a_factor = rms_forward(x)
    a_low = (a_normed * g_input).astype(bf16)
    a_columns = comm.columns(a_low)
    angles = rope_angles(positions, HEAD)
    cosine, sine = jnp.cos(angles), jnp.sin(angles)
    near, a_columns, order, starts, position_column, line.inner, comm.rank = fence(
        (near, a_columns, order, starts, position_column, line.inner, comm.rank)
    )
    far = [comm.far(v) for v in near]
    far, w_out = fence((far, w_out))
    out_near = comm.near(w_out)
    keyval_blocks = comm.joined(w_keyval, near[0], far[0])
    query_blocks = comm.joined(w_query, near[1], far[1])
    kv_pre = add(*[dot(a, w) for a, w in zip(a_columns, keyval_blocks)])
    k_hat, k_factor = rms_forward(kv_pre[:, :HEAD])
    k_low = rotate(k_hat * g_key, cosine, sine).astype(bf16)
    kv_low = jnp.concatenate([k_low, kv_pre[:, HEAD:].astype(bf16)], axis=1)
    kv_low, keyval_blocks, query_blocks = fence((kv_low, keyval_blocks, query_blocks))
    kv_near = comm.near(kv_low)
    q_pre = add(*[dot(a, w) for a, w in zip(a_columns, query_blocks)])
    kv_near, out_near, q_pre = fence((kv_near, out_near, q_pre))
    kv_far = comm.far(kv_near)
    kv_far, out_near = fence((kv_far, out_near))
    kv_blocks = comm.joined(kv_low, kv_near, kv_far)
    out_far = comm.far(out_near)
    kv_blocks, out_far, w_gate, w_up, w_down, query_blocks, keyval_blocks = fence(
        (kv_blocks, out_far, w_gate, w_up, w_down, query_blocks, keyval_blocks)
    )
    out_blocks = comm.joined(w_out, out_near, out_far)
    head_args = (
        comm.slots().shape[0],
        order,
        q_pre,
        cosine,
        sine,
        g_query[None],
        position_column,
        *kv_blocks,
    )
    att_low, inverse = attend(*head_args)
    out_blocks, att_low, w_gate, w_up, w_down = fence((out_blocks, att_low, w_gate, w_up, w_down))
    gate_w, up_w, down_w = [comm.pair(w) for w in (w_gate.T, w_up.T, w_down)]
    groups = len(gate_w)
    att_columns = jnp.split(att_low, len(out_blocks), axis=1)
    attn = add(*[dot(v, w) for v, w in zip(att_columns, out_blocks)])
    attn_normed, attn_factor = rms_forward(attn)
    middle = x + attn_normed * g_post_attn
    b_normed, b_factor = rms_forward(middle)
    b_low = (b_normed * g_pre_ffn).astype(bf16)
    b_low, query_blocks, keyval_blocks = fence((b_low, query_blocks, keyval_blocks))
    weights = [w[i] for i in range(groups) for w in (gate_w, up_w, down_w)]

    near = comm.spread(b_low)
    kept = [feed(comm.first(b_low, near), weights, f32)]
    query_whole = comm.ordered(query_blocks)
    kept, near, query_whole, keyval_blocks = fence((kept, near, query_whole, keyval_blocks))
    far = comm.far(near)
    b_list = comm.tokens(b_low, near, far)
    kept += [feed(part, weights, bf16) for part in b_list[1:-1]]
    kept, far, tail = fence((kept, far, b_list[-1]))
    b_list[-1] = tail
    early = comm.early(kept[1][:2], kept[2][:2])
    kept.append(feed(tail, weights, bf16))
    kept, early = fence((kept, early))
    parts = [v[:2] for v in kept]
    hidden, acts, slopes = [[v[i] for v in kept] for i in (2, 3, 4)]
    relay = comm.relay(parts[-1])
    late = comm.late(parts[1], parts[2], relay)
    ffn = all_of([add(*terms) for terms in comm.halves(parts, early, late)])
    ffn_normed, ffn_factor = rms_forward(ffn)
    layer_out = (middle + ffn_normed * g_post_ffn).astype(bf16)

    g = out_grad[0]
    d_ffn = rms_backward(g * g_post_ffn, ffn_normed, ffn_factor).astype(bf16)
    d_ffn, ffn_normed, keyval_blocks = fence((d_ffn, ffn_normed, keyval_blocks))

    def back(part, i):
        return feed_back(part, acts[i], slopes[i], weights, bf16 if i else f32)

    def other_half(lefts, rights):
        return weight_grad(1, [ff], lefts, rights) if groups > 1 else ()

    near = comm.spread(d_ffn)
    gain_post_ffn = jnp.sum(g * ffn_normed, axis=0)
    kept = [back(comm.first(d_ffn, near), 0)]
    keyval_whole = comm.ordered(keyval_blocks)
    kept, near, gain_post_ffn, keyval_whole = fence((kept, near, gain_post_ffn, keyval_whole))
    far = comm.far(near)
    d_list = comm.tokens(d_ffn, near, far)
    last = len(d_list) - 1
    kept += [back(d_list[i], i) for i in range(1, last)]
    kept, far, tail = fence((kept, far, d_list[-1]))
    d_list[-1] = tail

    other = [comm.hop(v, 1) for v in other_half(hidden, d_list)]
    kept.append(back(tail, last))
    kept, other = fence((kept, other))
    parts = [v[:2] for v in kept]
    d_gate, d_up = [[v[i] for v in kept] for i in (2, 3)]
    thirds = [ff // 3] * 3
    line.chunks += [(v,) for v in weight_grad(0, thirds, hidden, d_list, *other)]

    line.chunks, parts, d_gate, d_up, a_late = fence((line.chunks, parts, d_gate, d_up, a_low))

    def beside(_):
        early = comm.early(parts[1], parts[2])
        relay = comm.relay(parts[-1])
        others = other_half(d_gate, b_list), other_half(d_up, b_list)
        return early, relay, others, d_gate, d_up, parts

    early, relay, others, d_gate, d_up, parts = line.step(beside)

    def beside(_):
        late = comm.late(parts[1], parts[2], relay)
        (grads,) = weight_grad(0, [ff], d_gate, b_list, *[comm.hop(v, 1) for v in others[0]])
        late, grads = fence((late, grads))
        middles = middle_back(
            comm.halves(parts, early, late), g, middle, attn, g_pre_ffn, g_post_attn, out_blocks
        )
        return grads, d_up, others[1], middles

    grads, d_up, other_up, (d_middle, d_attn, d_att, gain_pair) = line.step(beside)
    line.add_rows(grads, 3)

    def beside(_):
        heads = attend_back(*head_args, saved=(att_low, inverse), d_att=d_att)
        grad_out = [dot_cols(v, d_attn) for v in att_columns]
        return heads, d_up, grad_out, [comm.hop(v, 1) for v in other_up]

    heads, d_up, grad_out, other_up = line.step(beside)
    d_q_pre, *d_kv_blocks, gain_query = heads

    def beside(_):
        group = comm.group(d_kv_blocks, comm.across(d_kv_blocks[-1]))
        near = comm.group_near(group)
        (grads,) = weight_grad(0, [ff], d_up, b_list, *other_up)
        return group, near, grads, grad_out, a_late, (gain_post_ffn, gain_pair, gain_query)

    group, near, grads, grad_out, a_late, early_gains = line.step(beside)
    line.add_rows(grads, 3)

    def beside(_):
        d_kv = comm.group_sum(group, near, comm.group_far(group))
        d_k_normed = rotate(d_kv[:, :HEAD], cosine, -sine)
        gain_key = jnp.sum(d_k_normed * k_hat, axis=0)
        d_k_pre = rms_backward(d_k_normed * g_key, k_hat, k_factor)
        d_kv_pre = jnp.concatenate([d_k_pre, d_kv[:, HEAD:]], axis=1).astype(bf16)
        d_a = dot_rows(d_q_pre, query_whole) + dot_rows(d_kv_pre, keyval_whole)
        gain_input = jnp.sum(d_a * a_normed, axis=0)
        out_group = comm.group(grad_out, comm.across(grad_out[-1].astype(bf16)))
        return d_kv_pre, d_a, (gain_input, gain_key), out_group, a_late, early_gains

    d_kv_pre, d_a, (gain_input, gain_key), out_group, a_late, early_gains = line.step(beside)
    gain_post_ffn, gain_pair, gain_query = early_gains

    def beside(_):
        out_near = comm.group_near(out_group)
        d_qkv = jnp.concatenate([d_q_pre, d_kv_pre], axis=1)
        gains = [gain_input, gain_pair[1], gain_pair[0], gain_post_ffn]
        gains.append(jnp.concatenate([gain_query[0], gain_key]))
        gains = [jnp.pad(v, (0, d_qkv.shape[1] - v.shape[0])) for v in gains]
        row = lax.broadcasted_iota(jnp.int32, (16, d_qkv.shape[1]), 0)
        gains = add(*[jnp.where(row == i, v[None], 0.0) for i, v in enumerate(gains)])
        grad_qkv = comm.projection(a_late, d_qkv, gains)
        return out_group, out_near, grad_qkv, d_a

    out_group, out_near, grad_qkv, d_a = line.step(beside, True)

    def beside(_):
        qkv_moved = comm.across(grad_qkv[-1].astype(bf16))
        out_far = comm.group_far(out_group)
        d_input = d_middle + rms_backward(d_a * g_input, a_normed, a_factor)
        total_out = comm.group_sum(out_group, out_near, out_far).astype(bf16)
        return comm.group(grad_qkv, qkv_moved), total_out, d_input

    group, total_out, d_input = line.step(beside, True)

    def beside(_):
        return group, comm.group_near(group), total_out

    group, near, total_out = line.step(beside, True)

    def beside(_):
        return comm.group_far(group), near, total_out

    far, near, total_out = line.step(beside, True)
    line.chunks += [(comm.group_sum(group, near, far).astype(bf16),), (total_out,)]
    def owned(tail):
        def mine(row, start, size):
            return lax.dynamic_slice(
                tail[shard + row], (start,), (size,), allow_negative_indices=False
            )

        grads = [tail[:shard, : HEADS * HEAD], tail[:shard, HEADS * HEAD :]]
        names = [mine(i, starts[0], shard) for i in range(4)]
        return grads, names + [mine(4, start, HEAD // n) for start in starts[1:]]

    (*done, _, total_out), ((grad_query, grad_keyval), names) = line.finish(owned)
    down, gate, up = all_of(done[:3]), all_of(done[3:6]), all_of(done[6:])
    return (
        layer_out[None],
        d_input[None],
        grad_query,
        grad_keyval,
        total_out,
        gate.T,
        up.T,
        down,
        *names,
    )


def solution(mesh):
    cube = mesh.shape["seq"] == 8 and mesh.shape["dp"] == 4
    in_specs = (
        P("dp", "seq", None),
        P("dp", None),
        P("dp", "seq"),
        P("seq", None),
        P("seq", None),
        P("seq", None),
        P(None, "seq"),
        P(None, "seq"),
        P("seq", None),
        P(),
        P(),
        P(),
        P(),
        P(),
        P(),
        P("dp", "seq", None),
    )
    out_specs = (
        P("dp", "seq", None),
        P("dp", "seq", None),
        P("seq", None),
        P("seq", None),
        P("seq", None),
        P(None, "seq"),
        P(None, "seq"),
        P("seq", None),
        P("seq"),
        P("seq"),
        P("seq"),
        P("seq"),
        P("seq"),
        P("seq"),
    )
    return jax.shard_map(
        functools.partial(on_device, Cube if cube else Plain),
        mesh=mesh,
        in_specs=in_specs,
        out_specs=out_specs,
        check_vma=False,
    )
```

```python
import functools

import jax
import jax.numpy as jnp
from jax import lax
from jax.experimental import pallas as pl
from jax.experimental.pallas import tpu as pltpu
from jax.sharding import PartitionSpec as P

HEADS = 4
HEAD = 256
BLOCK = 256
LANES = 128
FEED_VMEM = 12 << 20

norm_eps = 1e-06
rope_base = 1000000.0
score_scale = HEAD**-0.5
bf16 = jnp.bfloat16
f32 = jnp.float32
BRIEF = pl.CostEstimate(flops=1, bytes_accessed=1, transcendentals=0)


def rms_forward(values):
    factor = lax.rsqrt(jnp.mean(values * values, axis=-1, keepdims=True) + norm_eps)
    return (values * factor, factor)


def rms_backward(upstream, normed, factor):
    return factor * (upstream - normed * jnp.mean(upstream * normed, axis=-1, keepdims=True))


def rope_angles(positions, width):
    half_width = width // 2
    inverse_freq = rope_base ** (-(jnp.arange(half_width).astype(f32) * 2.0 / width))
    return positions.astype(f32)[:, None] * inverse_freq[None, :]


def rotate(values, cosine, sine):
    half_width = values.shape[-1] // 2
    first = values[..., :half_width]
    second = values[..., half_width:]
    return jnp.concatenate(
        [first * cosine - second * sine, second * cosine + first * sine], axis=-1
    )


def dot(left, right):
    return jnp.dot(left, right, preferred_element_type=f32)


def dot_rows(left, right):
    return lax.dot_general(left, right, (((1,), (1,)), ((), ())), preferred_element_type=f32)


def dot_cols(left, right):
    return lax.dot_general(left, right, (((0,), (0,)), ((), ())), preferred_element_type=f32)


def visible_mask(block_id, first_row, pos_ref):
    shape = (BLOCK, BLOCK)
    query = first_row + lax.broadcasted_iota(jnp.int32, shape, 0)
    key = block_id * BLOCK + lax.broadcasted_iota(jnp.int32, shape, 1)
    return (key <= query) & (key >= query - pos_ref[:, :1])


def head_rows(h):
    return pl.ds(h * BLOCK, BLOCK)


def put_queries(q_ref, q_pre_ref, gain_ref, cosine, sine):
    for h in range(HEADS):
        normed, _ = rms_forward(q_pre_ref[:, pl.ds(h * HEAD, HEAD)])
        q_ref[head_rows(h), :] = rotate(normed * gain_ref[...], cosine, sine).astype(bf16)


def column_blocks(columns, order_ref):
    if columns == 1:
        for h in range(HEADS):
            yield pl.ds(h * HEAD, HEAD), head_rows(h), pl.ds(0, HEAD)
        return
    slot, size = order_ref.shape[0] - columns, HEADS * HEAD // columns
    for k in range(columns):
        at = order_ref[slot + k] * size
        rows = pl.ds(pl.multiple_of(at // HEAD * BLOCK, BLOCK), BLOCK)
        yield pl.ds(k * size, size), rows, pl.ds(pl.multiple_of(at % HEAD, size), size)


def attend_kernel(
    n_blocks,
    columns,
    order_ref,
    q_pre_ref,
    cos_ref,
    sin_ref,
    gain_ref,
    pos_ref,
    *refs,
):
    kv_refs = refs[:-7]
    att_low_ref, inv_ref, q_ref, att_ref, total_ref, score_ref, weight_ref = refs[-7:]
    first_row = order_ref[n_blocks]
    first_key = order_ref[n_blocks + 1]
    put_queries(q_ref, q_pre_ref, gain_ref, cos_ref[...], sin_ref[...])
    att_ref[...] = jnp.zeros_like(att_ref)
    total_ref[...] = jnp.zeros_like(total_ref)

    def step(kv_ref, base, k, _):
        block_id = order_ref[base + k]
        live = (block_id * BLOCK <= first_row) & ((block_id + 1) * BLOCK > first_key)

        @pl.when(live)
        def _():
            rows = pl.ds(pl.multiple_of(k * BLOCK, BLOCK), BLOCK)
            visible = visible_mask(block_id, first_row, pos_ref)
            score_ref[...] = dot_rows(q_ref[...], kv_ref[rows, :HEAD])
            for h in range(HEADS):
                at = head_rows(h)
                weight = jnp.where(visible, jnp.exp(score_ref[at, :] * score_scale), 0.0)
                total_ref[at, :] += weight[:, :LANES] + weight[:, LANES:]
                weight_ref[at, :] = weight.astype(bf16)
            att_ref[...] += dot(weight_ref[...], kv_ref[rows, HEAD:])

        return 0

    each = n_blocks // len(kv_refs)
    for i, kv_ref in enumerate(kv_refs):
        lax.fori_loop(0, each, functools.partial(step, kv_ref, i * each), 0)
    for h in range(HEADS):
        at = head_rows(h)
        inverse = 1.0 / jnp.sum(total_ref[at, :], axis=-1, keepdims=True)
        inv_ref[:, pl.ds(h, 1)] = inverse
        att_ref[at, :] = att_ref[at, :] * inverse
    for stored, rows, lanes in column_blocks(columns, order_ref):
        att_low_ref[:, stored] = att_ref[rows, lanes].astype(bf16)


def attend(columns, order, q_pre, cosine, sine, gain, pos, *kv):
    rows = q_pre.shape[0]
    n_blocks = sum(v.shape[0] for v in kv) // BLOCK
    whole = pl.BlockSpec(memory_space=pltpu.VMEM)
    return pl.pallas_call(
        functools.partial(attend_kernel, n_blocks, columns),
        out_shape=(
            jax.ShapeDtypeStruct((rows, HEADS * HEAD), bf16),
            jax.ShapeDtypeStruct((rows, LANES), f32),
        ),
        in_specs=[pl.BlockSpec(memory_space=pltpu.SMEM)] + [whole] * (5 + len(kv)),
        out_specs=(whole,) * 2,
        scratch_shapes=[
            pltpu.VMEM((HEADS * rows, HEAD), bf16),
            pltpu.VMEM((HEADS * rows, HEAD), f32),
            pltpu.VMEM((HEADS * rows, LANES), f32),
            pltpu.VMEM((HEADS * rows, HEAD), f32),
            pltpu.VMEM((HEADS * rows, HEAD), bf16),
        ],
        cost_estimate=BRIEF,
        compiler_params=pltpu.CompilerParams(vmem_limit_bytes=10 << 20),
        name="attend",
    )(order, q_pre, cosine, sine, gain, pos, *kv)


def attend_back_kernel(
    n_blocks,
    columns,
    order_ref,
    q_pre_ref,
    cos_ref,
    sin_ref,
    gain_ref,
    pos_ref,
    att_ref,
    inv_ref,
    d_moved_ref,
    *refs,
):
    groups = (len(refs) - 10) // 2
    kv_refs, d_q_pre_ref, d_kv_refs = refs[:groups], refs[groups], refs[groups + 1 : -9]
    d_gain_ref, d_q_ref, row_dot_ref, d_att_ref, q_ref = refs[-9:-4]
    score_ref, d_prob_ref, prob_ref, d_score_ref = refs[-4:]
    cosine, sine = cos_ref[...], sin_ref[...]
    put_queries(q_ref, q_pre_ref, gain_ref, cosine, sine)
    row_dot_ref[...] = jnp.zeros_like(row_dot_ref)
    for stored, rows, lanes in column_blocks(columns, order_ref):
        moved = d_moved_ref[:, stored]
        d_att_ref[rows, lanes] = moved
        product = moved.astype(f32) * att_ref[:, stored].astype(f32)
        for i in range(product.shape[1] // LANES):
            row_dot_ref[rows, :] += product[:, i * LANES : (i + 1) * LANES]
    for h in range(HEADS):
        at = head_rows(h)
        total = jnp.sum(row_dot_ref[at, :], axis=-1, keepdims=True)
        row_dot_ref[at, pl.ds(0, 1)] = total
    first_row = order_ref[n_blocks]
    first_key = order_ref[n_blocks + 1]
    d_q_ref[...] = jnp.zeros_like(d_q_ref)

    def step(kv_ref, d_kv_ref, base, k, _):
        block_id = order_ref[base + k]
        live = (block_id * BLOCK <= first_row) & ((block_id + 1) * BLOCK > first_key)
        rows = pl.ds(pl.multiple_of(k * BLOCK, BLOCK), BLOCK)

        @pl.when(live)
        def _():
            keys = kv_ref[rows, :HEAD]
            visible = visible_mask(block_id, first_row, pos_ref)
            score_ref[...] = dot_rows(q_ref[...], keys)
            d_prob_ref[...] = dot_rows(d_att_ref[...], kv_ref[rows, HEAD:])
            for h in range(HEADS):
                at = head_rows(h)
                weight = jnp.where(visible, jnp.exp(score_ref[at, :] * score_scale), 0.0)
                prob = weight * inv_ref[:, pl.ds(h, 1)]
                prob_ref[at, :] = prob.astype(bf16)
                d_score = prob * (d_prob_ref[at, :] - row_dot_ref[at, pl.ds(0, 1)])
                d_score_ref[at, :] = d_score.astype(bf16)
            d_q_ref[...] += dot(d_score_ref[...], keys)
            d_keys = dot_cols(d_score_ref[...], q_ref[...])
            d_kv_ref[rows, :HEAD] = (d_keys * score_scale).astype(bf16)
            d_kv_ref[rows, HEAD:] = dot_cols(prob_ref[...], d_att_ref[...]).astype(bf16)

        @pl.when(jnp.logical_not(live))
        def _():
            d_kv_ref[rows, :] = jnp.zeros((BLOCK, 2 * HEAD), bf16)

        return 0

    each = n_blocks // groups
    for i in range(groups):
        walk = functools.partial(step, kv_refs[i], d_kv_refs[i], i * each)
        lax.fori_loop(0, each, walk, 0)
    d_gain = jnp.zeros((1, HEAD), f32)
    for h in range(HEADS):
        cols = pl.ds(h * HEAD, HEAD)
        normed, factor = rms_forward(q_pre_ref[:, cols])
        d_normed = rotate(d_q_ref[head_rows(h), :] * score_scale, cosine, -sine)
        d_gain += jnp.sum(d_normed * normed, axis=0, keepdims=True)
        d_q_pre_ref[:, cols] = rms_backward(d_normed * gain_ref[...], normed, factor).astype(bf16)
    d_gain_ref[...] = d_gain


def attend_back(columns, order, q_pre, cosine, sine, gain, pos, *kv, saved, d_att):
    rows = q_pre.shape[0]
    n_blocks = sum(v.shape[0] for v in kv) // BLOCK
    whole = pl.BlockSpec(memory_space=pltpu.VMEM)
    return pl.pallas_call(
        functools.partial(attend_back_kernel, n_blocks, columns),
        out_shape=(
            jax.ShapeDtypeStruct((rows, HEADS * HEAD), bf16),
            *[jax.ShapeDtypeStruct(v.shape, bf16) for v in kv],
            jax.ShapeDtypeStruct((1, HEAD), f32),
        ),
        in_specs=[pl.BlockSpec(memory_space=pltpu.SMEM)] + [whole] * (8 + len(kv)),
        out_specs=(whole,) * (2 + len(kv)),
        scratch_shapes=[
            pltpu.VMEM((HEADS * rows, HEAD), f32),
            pltpu.VMEM((HEADS * rows, LANES), f32),
            pltpu.VMEM((HEADS * rows, HEAD), bf16),
            pltpu.VMEM((HEADS * rows, HEAD), bf16),
            pltpu.VMEM((HEADS * rows, HEAD), f32),
            pltpu.VMEM((HEADS * rows, HEAD), f32),
            pltpu.VMEM((HEADS * rows, HEAD), bf16),
            pltpu.VMEM((HEADS * rows, HEAD), bf16),
        ],
        cost_estimate=BRIEF,
        compiler_params=pltpu.CompilerParams(vmem_limit_bytes=16 << 20),
        name="attend_back",
    )(order, q_pre, cosine, sine, gain, pos, *saved, d_att, *kv)


def gelu_parts(gate):
    c = (2.0 / jnp.pi) ** 0.5
    square = gate * gate
    t = jnp.tanh(gate * (c + (c * 0.044715) * square))
    half = 0.5 + 0.5 * t
    act = gate * half
    slope = half + act * (1.0 - t) * (c + (3 * c * 0.044715) * square)
    return act, slope


def put_halves(part, refs):
    half = part.shape[0] // 2
    refs[0][...] = part[:half].astype(refs[0].dtype)
    refs[1][...] = part[half:].astype(refs[1].dtype)


def feed_kernel(groups, pieces, *refs):
    weights, halves, (hidden_ref, act_ref, slope_ref) = refs[pieces:-5], refs[-5:-3], refs[-3:]
    b = jnp.concatenate([r[...] for r in refs[:pieces]], axis=0)
    part = 0.0
    for i in range(groups):
        gate_ref, up_ref, down_ref = weights[3 * i : 3 * i + 3]
        gate = dot_rows(b, gate_ref[...])
        up = dot_rows(b, up_ref[...])
        act, slope = gelu_parts(gate)
        hidden_ref[i] = (act * up).astype(bf16)
        act_ref[i] = act.astype(bf16)
        slope_ref[i] = (up * slope).astype(bf16)
        part = part + dot(hidden_ref[i], down_ref[...])
    put_halves(part, halves)


def feed(b, weights, dtype):
    rows, width = sum(v.shape[0] for v in b), b[0].shape[1]
    groups, ff = len(weights) // 3, weights[0].shape[0]
    whole = pl.BlockSpec(memory_space=pltpu.VMEM)
    return pl.pallas_call(
        functools.partial(feed_kernel, groups, len(b)),
        out_shape=(
            *[jax.ShapeDtypeStruct((rows // 2, width), dtype)] * 2,
            *[jax.ShapeDtypeStruct((groups, rows, ff), bf16)] * 3,
        ),
        in_specs=[whole] * (len(b) + len(weights)),
        out_specs=(whole,) * 5,
        cost_estimate=BRIEF,
        compiler_params=pltpu.CompilerParams(vmem_limit_bytes=FEED_VMEM),
        name="feed",
    )(*b, *weights)


def feed_back_kernel(groups, pieces, act_ref, slope_ref, *refs):
    weights, halves, (d_gate_ref, d_up_ref) = refs[pieces:-4], refs[-4:-2], refs[-2:]
    d = jnp.concatenate([r[...] for r in refs[:pieces]], axis=0)
    part = 0.0
    for i in range(groups):
        gate_ref, up_ref, down_ref = weights[3 * i : 3 * i + 3]
        d_hidden = dot_rows(d, down_ref[...])
        d_gate_ref[i] = (d_hidden * slope_ref[i].astype(f32)).astype(bf16)
        d_up_ref[i] = (d_hidden * act_ref[i].astype(f32)).astype(bf16)
        part = part + dot(d_gate_ref[i], gate_ref[...]) + dot(d_up_ref[i], up_ref[...])
    put_halves(part, halves)


def feed_back(d, act, slope, weights, dtype):
    rows, width = sum(v.shape[0] for v in d), d[0].shape[1]
    groups, ff = len(weights) // 3, weights[0].shape[0]
    whole = pl.BlockSpec(memory_space=pltpu.VMEM)
    return pl.pallas_call(
        functools.partial(feed_back_kernel, groups, len(d)),
        out_shape=(
            *[jax.ShapeDtypeStruct((rows // 2, width), dtype)] * 2,
            *[jax.ShapeDtypeStruct((groups, rows, ff), bf16)] * 2,
        ),
        in_specs=[whole] * (2 + len(d) + len(weights)),
        out_specs=(whole,) * 4,
        cost_estimate=BRIEF,
        compiler_params=pltpu.CompilerParams(vmem_limit_bytes=FEED_VMEM),
        name="feed_back",
    )(act, slope, *d, *weights)


def weight_grad_kernel(index, sizes, count, pieces, *refs):
    lefts, rights, rest = refs[:count], refs[count : count + pieces], refs[count + pieces :]
    extra, outs = rest[: -len(sizes)], rest[-len(sizes) :]
    left = jnp.concatenate([v[index] for v in lefts], axis=0)
    right = jnp.concatenate([v[...] for v in rights], axis=0)
    total = dot_cols(left, right)
    if extra:
        total = total + extra[0][...].astype(f32)
    begin = 0
    for size, out in zip(sizes, outs):
        out[...] = total[begin : begin + size].astype(bf16)
        begin += size


def weight_grad(index, sizes, lefts, rights, *extra):
    rights = [piece for part in rights for piece in part]
    width = rights[0].shape[1]
    whole = pl.BlockSpec(memory_space=pltpu.VMEM)
    return pl.pallas_call(
        functools.partial(weight_grad_kernel, index, sizes, len(lefts), len(rights)),
        out_shape=tuple(jax.ShapeDtypeStruct((size, width), bf16) for size in sizes),
        in_specs=[whole] * (len(lefts) + len(rights) + len(extra)),
        out_specs=(whole,) * len(sizes),
        cost_estimate=BRIEF,
        compiler_params=pltpu.CompilerParams(vmem_limit_bytes=FEED_VMEM),
        name="weight_grad",
    )(*lefts, *rights, *extra)


def middle_back_kernel(counts, out_count, *refs):
    terms, refs = refs[: sum(counts)], refs[sum(counts) :]
    g_ref, middle_ref, attn_ref, pre_ref, post_ref = refs[:5]
    outs, (d_middle_ref, d_attn_ref, d_att_ref, gain_ref) = refs[5 : 5 + out_count], refs[-4:]
    pre, post = 0.0, 0.0
    half = g_ref.shape[0] // 2
    for i in range(2):
        own = terms[: counts[0]] if i == 0 else terms[counts[0] :]
        rows = pl.ds(i * half, half)
        d_b = functools.reduce(jnp.add, [t[...].astype(f32) for t in own])
        normed, factor = rms_forward(middle_ref[rows, :])
        pre = pre + jnp.sum(d_b * normed, axis=0, keepdims=True)
        d_middle = g_ref[rows, :] + rms_backward(d_b * pre_ref[...], normed, factor)
        d_middle_ref[rows, :] = d_middle
        normed, factor = rms_forward(attn_ref[rows, :])
        post = post + jnp.sum(d_middle * normed, axis=0, keepdims=True)
        d_attn = rms_backward(d_middle * post_ref[...], normed, factor).astype(bf16)
        d_attn_ref[rows, :] = d_attn
    at = 0
    for out in outs:
        d_att_ref[:, at : at + out.shape[0]] = dot_rows(d_attn_ref[...], out[...]).astype(bf16)
        at += out.shape[0]
    gain_ref[0:1, :] = pre
    gain_ref[1:2, :] = post


def middle_back(halves, g, middle, attn, g_pre, g_post, outs):
    rows, width = g.shape
    whole = pl.BlockSpec(memory_space=pltpu.VMEM)
    return pl.pallas_call(
        functools.partial(middle_back_kernel, [len(h) for h in halves], len(outs)),
        out_shape=(
            jax.ShapeDtypeStruct((rows, width), f32),
            jax.ShapeDtypeStruct((rows, width), bf16),
            jax.ShapeDtypeStruct((rows, HEADS * HEAD), bf16),
            jax.ShapeDtypeStruct((2, width), f32),
        ),
        in_specs=[whole] * (sum(len(h) for h in halves) + 5 + len(outs)),
        out_specs=(whole,) * 4,
        cost_estimate=BRIEF,
        compiler_params=pltpu.CompilerParams(vmem_limit_bytes=FEED_VMEM),
        name="middle_back",
    )(*halves[0], *halves[1], g, middle, attn, g_pre[None], g_post[None], *outs)


def add(*terms):
    return functools.reduce(jnp.add, [t.astype(f32) for t in terms])


fence = lax.optimization_barrier


class Plain:
    def __init__(self, n, rank, place):
        self.n, self.rank, self.place = n, rank, place

    def order(self):
        return jnp.arange(self.n, dtype=jnp.int32)

    def slots(self):
        return jnp.zeros(1, jnp.int32)

    def send(self, shard):
        return [shard]

    def paired(self, shards):
        return [lax.all_gather(shards[0], "seq", axis=0, tiled=True)]

    def joined(self, shard, near, far):
        return self.paired([shard])

    def columns(self, value):
        return [value]

    def ordered(self, blocks):
        return blocks[0]

    def pair(self, shard):
        return [shard]

    def near(self, shard):
        return ()

    def far(self, near):
        return ()

    def spread(self, shard):
        return tuple(jnp.split(self.joined(shard, (), ())[0], self.n, axis=0))

    def first(self, shard, near):
        return (near[0],)

    def tokens(self, shard, near, far):
        return [(part,) for part in near]

    def early(self, x, y):
        return ()

    def relay(self, far):
        return ()

    def late(self, x, y, relay):
        return ()

    def halves(self, parts, early, late):
        whole = self.scatter(all_of([half.astype(bf16) for part in parts for half in part]))
        return [[half] for half in jnp.split(whole, 2, axis=0)]

    def across(self, value):
        return ()

    def group(self, partial, moved):
        return (partial[0],)

    def group_near(self, group):
        return ()

    def group_far(self, group):
        return ()

    def group_sum(self, group, near, far):
        return self.scatter(group[0])

    def scatter(self, partial):
        return lax.psum_scatter(
            partial.astype(bf16), "seq", scatter_dimension=0, tiled=True
        ).astype(f32)

    def projection(self, left, right, gains):
        grad = dot_cols(left, right).reshape(self.n, -1, right.shape[1])
        gains = jnp.broadcast_to(gains[None], (self.n, *gains.shape))
        return [jnp.concatenate([grad, gains], axis=1).reshape(-1, right.shape[1])]

    def line(self):
        return PlainLine(None)


class Cube(Plain):
    chips = (0, 2, 4, 6)
    ranks = (0, 2, 4, 6, 1, 3, 5, 7)

    def hop(self, value, bit):
        return lax.ppermute(value, "seq", [(i, i ^ bit) for i in range(8)])

    def order(self):
        return self.rank ^ jnp.array(self.ranks, dtype=jnp.int32)

    def slots(self):
        return self.order()

    def send(self, shard):
        return [shard] + [self.hop(shard, bit) for bit in self.chips[1:]]

    def joined(self, shard, near, far):
        return self.paired([shard, *near, *far])

    def paired(self, shards):
        group = all_of(shards)
        return [group, self.hop(group, 1)]

    def near(self, shard):
        return (self.hop(shard, 2), self.hop(shard, 4))

    def far(self, near):
        half = near[0].shape[0] // 2
        return (self.hop(near[1][:half], 2), self.hop(near[0][half:], 4))

    def spread(self, shard):
        return self.near(shard)

    def first(self, shard, near):
        return (shard,)

    def tokens(self, shard, near, far):
        return [(shard,), *[(v,) for v in near], tuple(far)]

    def early(self, x, y):
        return (self.hop(x[0], 2), self.hop(y[1], 4))

    def relay(self, far):
        return (self.hop(far[0], 2), self.hop(far[1], 4))

    def late(self, x, y, relay):
        return (
            self.hop(add(x[1], relay[1]).astype(bf16), 2),
            self.hop(add(y[0], relay[0]).astype(bf16), 4),
        )

    def halves(self, parts, early, late):
        own = parts[0]
        return [[own[0], early[0], late[1]], [own[1], early[1], late[0]]]

    def across(self, value):
        return (self.hop(value, 1),)

    def group(self, partial, moved):
        parts = jnp.split(add(partial[0], *moved), 4, axis=0)
        return (parts[0], *[p.astype(bf16) for p in parts[1:]])

    def group_near(self, group):
        return (self.hop(group[1], 2), self.hop(group[2], 4))

    def group_far(self, group):
        return (self.hop(group[3], 6),)

    def group_sum(self, group, near, far):
        return add(group[0], *near, *far)

    def select(self, size, stride):
        shape = (self.n * size, self.n * stride)
        col = lax.broadcasted_iota(jnp.int32, shape, 1)
        block, at = col // stride, col % stride
        source = self.rank ^ ((2 * block) % 8 + block // 4)
        row = lax.broadcasted_iota(jnp.int32, shape, 0)
        return ((row == source * size + at) & (at < size)).astype(bf16)

    def columns(self, value):
        moved = dot(value, self.select(value.shape[1] // self.n, value.shape[1] // self.n))
        return jnp.split(moved.astype(value.dtype), 2, axis=1)

    def ordered(self, blocks):
        whole = all_of(blocks)
        size = whole.shape[0] // self.n
        return dot(self.select(size, size), whole).astype(whole.dtype)

    def pair(self, shard):
        return [shard, self.hop(shard, 1)]

    def projection(self, left, right, gains):
        size, extra = left.shape[1] // self.n, gains.shape[0]
        stride = size + extra
        moved = dot(left, self.select(size, stride)).astype(bf16)
        shape = (extra, self.n * stride)
        at = lax.broadcasted_iota(jnp.int32, shape, 1) % stride
        pick = (at == size + lax.broadcasted_iota(jnp.int32, shape, 0)).astype(bf16)
        left = jnp.concatenate([moved, pick], axis=0)
        right = jnp.concatenate([right, gains.astype(bf16)], axis=0)
        half = self.n * stride // 2
        return [dot_cols(left[:, :half], right), dot_cols(left[:, half:], right)]

    def line(self):
        return CubeLine((self.place == 1) | (self.place == 2))


class PlainLine:
    def __init__(self, inner):
        self.inner = inner
        self.chunks, self.wholes = [], []

    def add_rows(self, whole, parts):
        size = whole.shape[0] // parts
        self.wholes.append(whole)
        self.chunks += [(len(self.wholes) - 1, i * size, size) for i in range(parts)]

    def chunk(self, at):
        if len(self.chunks[at]) == 1:
            return self.chunks[at][0]
        source, start, size = self.chunks[at]
        return self.wholes[source][start : start + size]

    def step(self, beside, sum_first=False):
        return fence(beside(()))

    def finish(self, early):
        chunks = [self.chunk(i) for i in range(len(self.chunks))]
        done = [lax.psum(c, "dp").astype(f32) for c in chunks]
        return done, early(done[-2])


class CubeLine(PlainLine):
    def __init__(self, inner):
        super().__init__(inner)
        self.halves, self.totals, self.out = {}, {}, {}
        self.at = 0

    def step(self, beside, sum_first=False):
        tick = self.at
        self.at += 1
        mine = self.chunk(tick) if tick < len(self.chunks) else None
        back, half = self.totals.get(tick - 2), self.halves.get(tick - 1)
        got = {}
        if mine is not None and back is not None and mine.shape == back.shape:
            both = jnp.where(self.inner, back, mine)
            got["in"] = lax.ppermute(both, "dp", [(0, 1), (1, 0), (2, 3), (3, 2)])
        else:
            if back is not None:
                got["out"] = self.outwards(back)
            if mine is not None:
                got["in"] = lax.ppermute(mine, "dp", [(0, 1), (3, 2)])
        if half is not None:
            across = lax.ppermute(half, "dp", [(1, 2), (2, 1)])
            got["middle"] = add(half, across).astype(bf16) if sum_first else across
        values = beside(())
        later = [c for c in self.chunks[tick + 1 :] if len(c) == 1]
        got, values, later, self.wholes = fence((got, values, later, self.wholes))
        for at in range(tick + 1, len(self.chunks)):
            if len(self.chunks[at]) == 1:
                self.chunks[at] = later.pop(0)
        if mine is not None:
            self.halves[tick] = add(mine, got["in"]).astype(bf16)
        if half is not None:
            middle = got["middle"]
            self.totals[tick - 1] = middle if sum_first else add(half, middle).astype(bf16)
        if back is not None:
            self.out[tick - 2] = jnp.where(self.inner, back, got["out"] if "out" in got else got["in"])
        return values

    def finish(self, early):
        count = len(self.chunks)
        while self.at < count:
            self.step(lambda values: values)
        back, half = self.totals[count - 2], self.halves[count - 1]
        back_moved = self.outwards(back)
        total = add(half, lax.ppermute(half, "dp", [(1, 2), (2, 1)])).astype(bf16)
        self.out[count - 2] = jnp.where(self.inner, back, back_moved)
        self.out[count - 1] = jnp.where(self.inner, total, self.outwards(total))
        made = early(self.out[count - 2].astype(f32))
        return [self.out[i].astype(f32) for i in range(count)], made

    def outwards(self, value):
        return lax.ppermute(value, "dp", [(1, 0), (2, 3)])


def all_of(values):
    return jnp.concatenate(values, axis=0)


def on_device(
    kind,
    layer_input,
    segment_ids,
    position_ids,
    w_query,
    w_keyval,
    w_out,
    w_gate,
    w_up,
    w_down,
    g_input,
    g_post_attn,
    g_pre_ffn,
    g_post_ffn,
    g_query,
    g_key,
    out_grad,
):
    n = lax.axis_size("seq")
    comm = kind(n, lax.axis_index("seq"), lax.axis_index("dp"))
    rows = layer_input.shape[1]
    width = layer_input.shape[2]
    ff = w_gate.shape[1]
    positions = position_ids[0]
    row_offset = comm.rank * rows
    order = jnp.concatenate(
        [comm.order(), row_offset[None], (row_offset - positions[0])[None], comm.slots()]
    ).astype(jnp.int32)
    shard = width // n
    starts = (comm.rank * shard, comm.rank * (HEAD // n), HEAD + comm.rank * (HEAD // n))
    line = comm.line()
    position_column = positions[:, None] + jnp.zeros((1, LANES), jnp.int32)

    x = layer_input[0].astype(f32)
    near = comm.near(w_keyval), comm.near(w_query)
    a_normed, a_factor = rms_forward(x)
    a_low = (a_normed * g_input).astype(bf16)
    a_columns = comm.columns(a_low)
    angles = rope_angles(positions, HEAD)
    cosine, sine = jnp.cos(angles), jnp.sin(angles)
    near, a_columns, order, starts, position_column, line.inner, comm.rank = fence(
        (near, a_columns, order, starts, position_column, line.inner, comm.rank)
    )
    far = [comm.far(v) for v in near]
    far, w_out = fence((far, w_out))
    out_near = comm.near(w_out)
    keyval_blocks = comm.joined(w_keyval, near[0], far[0])
    query_blocks = comm.joined(w_query, near[1], far[1])
    kv_pre = add(*[dot(a, w) for a, w in zip(a_columns, keyval_blocks)])
    k_hat, k_factor = rms_forward(kv_pre[:, :HEAD])
    k_low = rotate(k_hat * g_key, cosine, sine).astype(bf16)
    kv_low = jnp.concatenate([k_low, kv_pre[:, HEAD:].astype(bf16)], axis=1)
    kv_low, keyval_blocks, query_blocks = fence((kv_low, keyval_blocks, query_blocks))
    kv_near = comm.near(kv_low)
    q_pre = add(*[dot(a, w) for a, w in zip(a_columns, query_blocks)])
    kv_near, out_near, q_pre = fence((kv_near, out_near, q_pre))
    kv_far = comm.far(kv_near)
    kv_far, out_near = fence((kv_far, out_near))
    kv_blocks = comm.joined(kv_low, kv_near, kv_far)
    out_far = comm.far(out_near)
    kv_blocks, out_far, w_gate, w_up, w_down, query_blocks, keyval_blocks = fence(
        (kv_blocks, out_far, w_gate, w_up, w_down, query_blocks, keyval_blocks)
    )
    out_blocks = comm.joined(w_out, out_near, out_far)
    head_args = (
        comm.slots().shape[0],
        order,
        q_pre,
        cosine,
        sine,
        g_query[None],
        position_column,
        *kv_blocks,
    )
    att_low, inverse = attend(*head_args)
    out_blocks, att_low, w_gate, w_up, w_down = fence((out_blocks, att_low, w_gate, w_up, w_down))
    gate_w, up_w, down_w = [comm.pair(w) for w in (w_gate.T, w_up.T, w_down)]
    groups = len(gate_w)
    att_columns = jnp.split(att_low, len(out_blocks), axis=1)
    attn = add(*[dot(v, w) for v, w in zip(att_columns, out_blocks)])
    attn_normed, attn_factor = rms_forward(attn)
    middle = x + attn_normed * g_post_attn
    b_normed, b_factor = rms_forward(middle)
    b_low = (b_normed * g_pre_ffn).astype(bf16)
    b_low, query_blocks, keyval_blocks = fence((b_low, query_blocks, keyval_blocks))
    weights = [w[i] for i in range(groups) for w in (gate_w, up_w, down_w)]

    near = comm.spread(b_low)
    kept = [feed(comm.first(b_low, near), weights, f32)]
    query_whole = comm.ordered(query_blocks)
    kept, near, query_whole, keyval_blocks = fence((kept, near, query_whole, keyval_blocks))
    far = comm.far(near)
    b_list = comm.tokens(b_low, near, far)
    kept += [feed(part, weights, bf16) for part in b_list[1:-1]]
    kept, far, tail = fence((kept, far, b_list[-1]))
    b_list[-1] = tail
    early = comm.early(kept[1][:2], kept[2][:2])
    kept.append(feed(tail, weights, bf16))
    kept, early = fence((kept, early))
    parts = [v[:2] for v in kept]
    hidden, acts, slopes = [[v[i] for v in kept] for i in (2, 3, 4)]
    relay = comm.relay(parts[-1])
    late = comm.late(parts[1], parts[2], relay)
    ffn = all_of([add(*terms) for terms in comm.halves(parts, early, late)])
    ffn_normed, ffn_factor = rms_forward(ffn)
    layer_out = (middle + ffn_normed * g_post_ffn).astype(bf16)

    g = out_grad[0]
    d_ffn = rms_backward(g * g_post_ffn, ffn_normed, ffn_factor).astype(bf16)
    d_ffn, ffn_normed, keyval_blocks = fence((d_ffn, ffn_normed, keyval_blocks))

    def back(part, i):
        return feed_back(part, acts[i], slopes[i], weights, bf16 if i else f32)

    def other_half(lefts, rights):
        return weight_grad(1, [ff], lefts, rights) if groups > 1 else ()

    near = comm.spread(d_ffn)
    gain_post_ffn = jnp.sum(g * ffn_normed, axis=0)
    kept = [back(comm.first(d_ffn, near), 0)]
    keyval_whole = comm.ordered(keyval_blocks)
    kept, near, gain_post_ffn, keyval_whole = fence((kept, near, gain_post_ffn, keyval_whole))
    far = comm.far(near)
    d_list = comm.tokens(d_ffn, near, far)
    last = len(d_list) - 1
    kept += [back(d_list[i], i) for i in range(1, last)]
    kept, far, tail = fence((kept, far, d_list[-1]))
    d_list[-1] = tail

    other = [comm.hop(v, 1) for v in other_half(hidden, d_list)]
    kept.append(back(tail, last))
    kept, other = fence((kept, other))
    parts = [v[:2] for v in kept]
    d_gate, d_up = [[v[i] for v in kept] for i in (2, 3)]
    thirds = [ff // 3] * 3
    line.chunks += [(v,) for v in weight_grad(0, thirds, hidden, d_list, *other)]

    line.chunks, parts, d_gate, d_up, a_late = fence((line.chunks, parts, d_gate, d_up, a_low))

    def beside(_):
        early = comm.early(parts[1], parts[2])
        relay = comm.relay(parts[-1])
        others = other_half(d_gate, b_list), other_half(d_up, b_list)
        return early, relay, others, d_gate, d_up, parts

    early, relay, others, d_gate, d_up, parts = line.step(beside)

    def beside(_):
        late = comm.late(parts[1], parts[2], relay)
        (grads,) = weight_grad(0, [ff], d_gate, b_list, *[comm.hop(v, 1) for v in others[0]])
        late, grads = fence((late, grads))
        middles = middle_back(
            comm.halves(parts, early, late), g, middle, attn, g_pre_ffn, g_post_attn, out_blocks
        )
        return grads, d_up, others[1], middles

    grads, d_up, other_up, (d_middle, d_attn, d_att, gain_pair) = line.step(beside)
    line.add_rows(grads, 3)

    def beside(_):
        heads = attend_back(*head_args, saved=(att_low, inverse), d_att=d_att)
        grad_out = [dot_cols(v, d_attn) for v in att_columns]
        return heads, d_up, grad_out, [comm.hop(v, 1) for v in other_up]

    heads, d_up, grad_out, other_up = line.step(beside, True)
    d_q_pre, *d_kv_blocks, gain_query = heads

    def beside(_):
        group = comm.group(d_kv_blocks, comm.across(d_kv_blocks[-1]))
        near = comm.group_near(group)
        (grads,) = weight_grad(0, [ff], d_up, b_list, *other_up)
        return group, near, grads, grad_out, a_late, (gain_post_ffn, gain_pair, gain_query)

    group, near, grads, grad_out, a_late, early_gains = line.step(beside)
    line.add_rows(grads, 3)

    def beside(_):
        d_kv = comm.group_sum(group, near, comm.group_far(group))
        d_k_normed = rotate(d_kv[:, :HEAD], cosine, -sine)
        gain_key = jnp.sum(d_k_normed * k_hat, axis=0)
        d_k_pre = rms_backward(d_k_normed * g_key, k_hat, k_factor)
        d_kv_pre = jnp.concatenate([d_k_pre, d_kv[:, HEAD:]], axis=1).astype(bf16)
        d_a = dot_rows(d_q_pre, query_whole) + dot_rows(d_kv_pre, keyval_whole)
        gain_input = jnp.sum(d_a * a_normed, axis=0)
        out_group = comm.group(grad_out, comm.across(grad_out[-1].astype(bf16)))
        return d_kv_pre, d_a, (gain_input, gain_key), out_group, a_late, early_gains

    d_kv_pre, d_a, (gain_input, gain_key), out_group, a_late, early_gains = line.step(beside)
    gain_post_ffn, gain_pair, gain_query = early_gains

    def beside(_):
        out_near = comm.group_near(out_group)
        d_qkv = jnp.concatenate([d_q_pre, d_kv_pre], axis=1)
        gains = [gain_input, gain_pair[1], gain_pair[0], gain_post_ffn]
        gains.append(jnp.concatenate([gain_query[0], gain_key]))
        gains = [jnp.pad(v, (0, d_qkv.shape[1] - v.shape[0])) for v in gains]
        row = lax.broadcasted_iota(jnp.int32, (16, d_qkv.shape[1]), 0)
        gains = add(*[jnp.where(row == i, v[None], 0.0) for i, v in enumerate(gains)])
        grad_qkv = comm.projection(a_late, d_qkv, gains)
        return out_group, out_near, grad_qkv, d_a

    out_group, out_near, grad_qkv, d_a = line.step(beside, True)

    def beside(_):
        qkv_moved = comm.across(grad_qkv[-1].astype(bf16))
        out_far = comm.group_far(out_group)
        d_input = d_middle + rms_backward(d_a * g_input, a_normed, a_factor)
        total_out = comm.group_sum(out_group, out_near, out_far).astype(bf16)
        return comm.group(grad_qkv, qkv_moved), total_out, d_input

    group, total_out, d_input = line.step(beside, True)

    def beside(_):
        return group, comm.group_near(group), total_out

    group, near, total_out = line.step(beside, True)

    def beside(_):
        return comm.group_far(group), near, total_out

    far, near, total_out = line.step(beside, True)
    line.chunks += [(comm.group_sum(group, near, far).astype(bf16),), (total_out,)]
    def owned(tail):
        def mine(row, start, size):
            return lax.dynamic_slice(
                tail[shard + row], (start,), (size,), allow_negative_indices=False
            )

        grads = [tail[:shard, : HEADS * HEAD], tail[:shard, HEADS * HEAD :]]
        names = [mine(i, starts[0], shard) for i in range(4)]
        return grads, names + [mine(4, start, HEAD // n) for start in starts[1:]]

    (*done, _, total_out), ((grad_query, grad_keyval), names) = line.finish(owned)
    down, gate, up = all_of(done[:3]), all_of(done[3:6]), all_of(done[6:])
    return (
        layer_out[None],
        d_input[None],
        grad_query,
        grad_keyval,
        total_out,
        gate.T,
        up.T,
        down,
        *names,
    )


def solution(mesh):
    cube = mesh.shape["seq"] == 8 and mesh.shape["dp"] == 4
    in_specs = (
        P("dp", "seq", None),
        P("dp", None),
        P("dp", "seq"),
        P("seq", None),
        P("seq", None),
        P("seq", None),
        P(None, "seq"),
        P(None, "seq"),
        P("seq", None),
        P(),
        P(),
        P(),
        P(),
        P(),
        P(),
        P("dp", "seq", None),
    )
    out_specs = (
        P("dp", "seq", None),
        P("dp", "seq", None),
        P("seq", None),
        P("seq", None),
        P("seq", None),
        P(None, "seq"),
        P(None, "seq"),
        P("seq", None),
        P("seq"),
        P("seq"),
        P("seq"),
        P("seq"),
        P("seq"),
        P("seq"),
    )
    return jax.shard_map(
        functools.partial(on_device, Cube if cube else Plain),
        mesh=mesh,
        in_specs=in_specs,
        out_specs=out_specs,
        check_vma=False,
    )
```
